32 devices in a mesh: lat: 4 (over z), lon: 8 (over y, x, core).
Axes of the slice: x: 2, y: 2, z: 4, core: 2. Of those that a mesh axis runs over, the one named last changes fastest.
Arguments:
- latents: bfloat16 [64, 128, 256], P('lat', 'lon'), may hold values from -6 to 6
- conv_weight: bfloat16 [9, 256, 256], replicated, may hold values from -0.125 to 0.125
- map_weight: bfloat16 [256, 1024], replicated, may hold values from -0.375 to 0.375
- map_bias: float32 [1024], replicated, may hold values from -6 to 6
- input_weight: float32 [3, 512], replicated, may hold values from -3.5 to 3.5
- hidden_weight: bfloat16 [1, 512, 512], replicated, may hold values from -0.25 to 0.25
- output_weight: float32 [512], replicated, may hold values from -0.25 to 0.25
- hit_owner: int32 [768], P(('lat', 'lon')), may hold values from 0 to 31, as said below
- serve_block: int32 [32, 32], P(('lat', 'lon')), may hold values from -1 to 1, as said below
- query_grid: int32 [3, 49152], P(None, ('lat', 'lon')), may hold values from 0 to 127, as said below
- cotangent: float32 [49152], P(('lat', 'lon')), may hold values from -6 to 6
Outputs:
- latent_grad: float32 [64, 128, 256], P('lat', 'lon')
- conv_grad: float32 [9, 256, 256], replicated
- map_grad: float32 [256, 1024], replicated
- map_bias_grad: float32 [1024], replicated
- input_grad: float32 [3, 512], replicated
- hidden_grad: float32 [1, 512, 512], replicated
- output_grad: float32 [512], replicated
The draws below stay inside these ranges and needn't reach their ends.
Inputs may be any that keep to these rules, and one draw needn't show every extreme that they name: `hit_owner`: each device's 24 entries name distinct devices, numbered lat index times the size of lon plus lon index. `serve_block`: entry [o, r] is a block of device o, 0 to 1, when the list of device r names o, and -1 otherwise. `query_grid`: row 0 is the cell within the block (row-major over 8 rows of 16 cells), row 1 the sub-cell (0 to 35, row-major), row 2 the level (0 to 36).
All inputs are finite; a program needn't handle non-finite values.
Results may differ from the reference program's by a relative error of at most 0.0095.
Values may be sent and summed in bfloat16 or wider, within the bound.
No kernel may reach another device: no remote copies, remote signals or barrier semaphores. Data moves between devices by JAX's collectives and lax.ppermute only.
A program may use at most 128 MiB of HBM per device.

```python
import math
import jax
import jax.numpy as jnp
from jax import lax

C = 256
WIDTH = 512
MODLAYERS = 2
BLOCK = 128
LEVELS = 37
SUB = 6
LAT_DEV = 16
LON_DEV = 16
GROUP = 64
BLK_DEV = 2
HITS = 24
NLAT = 64
NLON = 128
QUERIES = 49152
N_LAT = 4
N_LON = 8


def owner_table(key):
    device_total = N_LAT * N_LON
    base_score = jax.random.randint(jax.random.fold_in(key, 11), (device_total, device_total), 0, 2 ** 20)
    heat = jax.random.randint(jax.random.fold_in(key, 12), (device_total,), 0, 4) * 2 ** 19
    score = (base_score + heat[None, :]) * device_total + jnp.arange(device_total, dtype=jnp.int32)[None, :]
    _, owners = lax.top_k(score, HITS)
    return owners.astype(jnp.int32)


def draw_hit_owner(key, part):
    return owner_table(key).reshape(-1)


def draw_serve_block(key, part):
    device_total = N_LAT * N_LON
    owners = owner_table(key)
    member = jnp.zeros((device_total, device_total), jnp.int32).at[jnp.arange(device_total)[:, None], owners].set(1)
    picked = jax.random.randint(jax.random.fold_in(key, 13), (device_total, device_total), 0, BLK_DEV)
    return jnp.where(member.T == 1, picked, -1).astype(jnp.int32)


def draw_query_grid(key, part):
    total = N_LAT * N_LON * HITS * GROUP
    cell_index = jax.random.randint(jax.random.fold_in(key, 21), (total,), 0, BLOCK)
    sub_index = jax.random.randint(jax.random.fold_in(key, 22), (total,), 0, SUB * SUB)
    level_index = jax.random.randint(jax.random.fold_in(key, 23), (total,), 0, LEVELS)
    return jnp.stack([cell_index, sub_index, level_index]).astype(jnp.int32)


def block_levels(key, extent, cuts, smallest, top_value):
    def one(axis_at, blocks):
        steps = jax.random.uniform(jax.random.fold_in(jax.random.fold_in(key, 6), axis_at), (blocks,), jnp.float32, smallest / len(cuts), top_value / len(cuts))
        return jnp.repeat(jnp.exp(steps), extent[axis_at] // blocks).reshape((-1,) + (1,) * (len(extent) - axis_at - 1))

    loudness = one(*cuts[0])
    for cut in cuts[1:]:
        loudness = loudness * one(*cut)
    return loudness


def normal_values(stream_key, dims, spread, limit, shards=(), held_as=jnp.bfloat16):
    gain = block_levels(stream_key, dims, shards, -0.22, 0.18) if shards else 1.0
    drawn = jax.random.normal(stream_key, dims, jnp.float32) * spread * gain
    return jnp.minimum(jnp.maximum(drawn, -limit), limit).astype(held_as)


def setup_inputs(seed: int = 0) -> dict:
    keys = jax.random.split(jax.random.key(seed), 12)
    latents = normal_values(keys[0], (NLAT, NLON, C), 1.0, 6.0, ((0, 4), (1, 8)))
    conv_weight = normal_values(keys[1], (9, C, C), (9 * C) ** -0.5, 0.125)
    map_weight = normal_values(keys[2], (C, MODLAYERS * WIDTH), C ** -0.5, 0.375)
    map_bias = normal_values(keys[3], (MODLAYERS * WIDTH,), 1.0, 6.0, (), jnp.float32)
    input_weight = normal_values(keys[4], (3, WIDTH), 3 ** -0.5, 3.5, (), jnp.float32)
    hidden_weight = normal_values(keys[5], (MODLAYERS - 1, WIDTH, WIDTH), WIDTH ** -0.5, 0.25)
    output_weight = normal_values(keys[6], (WIDTH,), WIDTH ** -0.5, 0.25, (), jnp.float32)
    hit_owner = draw_hit_owner(jax.random.fold_in(keys[11], 71), 0)
    serve_block = draw_serve_block(jax.random.fold_in(keys[11], 71), 0)
    query_grid = draw_query_grid(jax.random.fold_in(keys[11], 71), 0)
    cotangent = normal_values(keys[10], (QUERIES,), 1.0, 6.0, ((0, 32),), jnp.float32)
    return dict(latents=latents, conv_weight=conv_weight, map_weight=map_weight, map_bias=map_bias, input_weight=input_weight, hidden_weight=hidden_weight, output_weight=output_weight, hit_owner=hit_owner, serve_block=serve_block, query_grid=query_grid, cotangent=cotangent)


OMEGA = 30.0

def conv_apply(padded, kernel, row_count, col_count, flipped):
    channels = padded.shape[-1]
    result = jnp.zeros((row_count * col_count, kernel.shape[-1]), jnp.float32)
    for shift_a in (-1, 0, 1):
        for shift_b in (-1, 0, 1):
            tap_index = (shift_a + 1) * 3 + shift_b + 1
            if flipped:
                window = padded[1 - shift_a:1 - shift_a + row_count, 1 - shift_b:1 - shift_b + col_count]
                matrix = kernel[tap_index].T
            else:
                window = padded[1 + shift_a:1 + shift_a + row_count, 1 + shift_b:1 + shift_b + col_count]
                matrix = kernel[tap_index]
            result = result + jnp.dot(window.reshape(row_count * col_count, channels), matrix, preferred_element_type=jnp.float32)
    return result

def conv_weight_grad(padded, grads, row_count, col_count):
    flat_grads = grads.reshape(row_count * col_count, -1)
    pieces = []
    for shift_a in (-1, 0, 1):
        for shift_b in (-1, 0, 1):
            window = padded[1 + shift_a:1 + shift_a + row_count, 1 + shift_b:1 + shift_b + col_count]
            window = window.reshape(row_count * col_count, -1)
            pieces.append(jnp.dot(window.T, flat_grads, preferred_element_type=jnp.float32))
    return jnp.stack(pieces)

def wrap_pad(source):
    extended = jnp.concatenate([source[:, -1:], source, source[:, :1]], axis=1)
    return jnp.pad(extended, ((1, 1), (0, 0), (0, 0)))

def query_coords(cell_index, sub_index, level_index, lat_base, lon_base, lon_tile, lat_cells, lon_cells):
    row_index = lat_base[:, None] + cell_index // lon_tile
    col_index = lon_base[:, None] + cell_index % lon_tile
    lat_coord = ((row_index * SUB + sub_index // SUB).astype(jnp.float32) + 0.5) / (lat_cells * SUB) * 2.0 - 1.0
    lon_coord = ((col_index * SUB + sub_index % SUB).astype(jnp.float32) + 0.5) / (lon_cells * SUB) * 2.0 - 1.0
    level_coord = (level_index.astype(jnp.float32) + 0.5) / LEVELS * 2.0 - 1.0
    return jnp.stack([lat_coord.reshape(-1), lon_coord.reshape(-1), level_coord.reshape(-1)])

def sine_grads(features, coords, cotan_rows, map_weight, map_bias, input_weight, hidden_weight, output_weight):
    hidden_size = input_weight.shape[1]
    depth_count = map_weight.shape[1] // hidden_size
    shifts = jnp.dot(features, map_weight, preferred_element_type=jnp.float32) + map_bias
    linear = coords[0][:, None] * input_weight[0] + coords[1][:, None] * input_weight[1] + coords[2][:, None] * input_weight[2]
    preacts = [OMEGA * linear + shifts[:, :hidden_size]]
    inputs_rounded = []
    for layer_index in range(1, depth_count):
        previous = jnp.sin(preacts[-1]).astype(jnp.bfloat16)
        inputs_rounded.append(previous)
        preacts.append(jnp.dot(previous, hidden_weight[layer_index - 1], preferred_element_type=jnp.float32) + shifts[:, layer_index * hidden_size:(layer_index + 1) * hidden_size])
    last_act = jnp.sin(preacts[-1])
    output_grad = jnp.dot(cotan_rows, last_act, precision=lax.Precision.HIGHEST)
    act_grad = cotan_rows[:, None] * output_weight[None, :]
    pre_grads = [None] * depth_count
    rounded_grads = [None] * depth_count
    hidden_grads = [None] * (depth_count - 1)
    for layer_index in range(depth_count - 1, -1, -1):
        pre_grads[layer_index] = act_grad * jnp.cos(preacts[layer_index])
        rounded_grads[layer_index] = pre_grads[layer_index].astype(jnp.bfloat16)
        if layer_index > 0:
            hidden_grads[layer_index - 1] = jnp.dot(inputs_rounded[layer_index - 1].T, rounded_grads[layer_index], preferred_element_type=jnp.float32)
            act_grad = jnp.dot(rounded_grads[layer_index], hidden_weight[layer_index - 1].T, preferred_element_type=jnp.float32)
    input_grad = OMEGA * jnp.dot(coords, pre_grads[0], precision=lax.Precision.HIGHEST)
    mod_grads = jnp.concatenate(rounded_grads, axis=1)
    bias_grad = lax.optimization_barrier(jnp.sum(jnp.concatenate(pre_grads, axis=1), axis=0))
    map_grad = jnp.dot(features.T, mod_grads, preferred_element_type=jnp.float32)
    feature_grads = jnp.dot(mod_grads, map_weight.T, preferred_element_type=jnp.float32)
    return (feature_grads, (map_grad, bias_grad, input_grad, jnp.stack(hidden_grads), output_grad))

def reference(latents, conv_weight, map_weight, map_bias, input_weight, hidden_weight, output_weight, hit_owner, serve_block, query_grid, cotangent):
    dev_count = N_LAT * N_LON
    padded = wrap_pad(latents)
    features = conv_apply(padded, conv_weight, NLAT, NLON, False).astype(jnp.bfloat16).reshape(NLAT, NLON, C)
    blocks = features.reshape(N_LAT, LAT_DEV, N_LON, LON_DEV, C).transpose(0, 2, 1, 3, 4).reshape(dev_count, BLK_DEV, BLOCK, C)
    owners = hit_owner.reshape(dev_count, HITS)
    query_rows = query_grid.reshape(3, dev_count, HITS, GROUP)
    cotan_all = cotangent.reshape(dev_count, HITS, GROUP)
    weights = (map_weight, map_bias, input_weight, hidden_weight, output_weight)
    zero_grads = (jnp.zeros((C, MODLAYERS * WIDTH), jnp.float32), jnp.zeros((MODLAYERS * WIDTH,), jnp.float32), jnp.zeros((3, WIDTH), jnp.float32), jnp.zeros((MODLAYERS - 1, WIDTH, WIDTH), jnp.float32), jnp.zeros((WIDTH,), jnp.float32))
    initial = (jnp.zeros((dev_count, BLK_DEV, BLOCK, C), jnp.float32), zero_grads)

    def visit(state_pair, device):
        block_sums, grad_totals = state_pair
        owner_row = owners[device]
        block_pick = serve_block[owner_row, device]
        hit_blocks = blocks[owner_row, block_pick]
        cell_index = query_rows[0, device]
        sub_index = query_rows[1, device]
        level_index = query_rows[2, device]
        features_q = jnp.take_along_axis(hit_blocks, cell_index[:, :, None], axis=1).reshape(HITS * GROUP, C)
        lat_base = owner_row // N_LON * LAT_DEV + block_pick * (BLOCK // LON_DEV)
        lon_base = owner_row % N_LON * LON_DEV
        coords = query_coords(cell_index, sub_index, level_index, lat_base, lon_base, LON_DEV, NLAT, NLON)
        feature_grads, grads = sine_grads(features_q, coords, cotan_all[device].reshape(-1), weights[0], weights[1], weights[2], weights[3], weights[4])
        hit_grads = jnp.zeros((HITS, BLOCK, C), jnp.float32).at[jnp.arange(HITS)[:, None], cell_index].add(feature_grads.reshape(HITS, GROUP, C))
        block_sums = block_sums.at[owner_row, block_pick].add(hit_grads)
        grad_totals = jax.tree.map(jnp.add, grad_totals, grads)
        return ((block_sums, grad_totals), None)
    (block_sums, grad_totals), _ = lax.scan(visit, initial, jnp.arange(dev_count, dtype=jnp.int32))
    feature_grad = block_sums.reshape(N_LAT, N_LON, LAT_DEV, LON_DEV, C).transpose(0, 2, 1, 3, 4).reshape(NLAT, NLON, C).astype(jnp.bfloat16)
    padded_grad = wrap_pad(feature_grad)
    latent_grad = conv_apply(padded_grad, conv_weight, NLAT, NLON, True).reshape(NLAT, NLON, C)
    conv_grad = conv_weight_grad(padded, feature_grad, NLAT, NLON)
    grad_scale = 1.0 / math.sqrt(QUERIES)
    return (latent_grad, conv_grad * grad_scale, grad_totals[0] * grad_scale, grad_totals[1] * grad_scale, grad_totals[2] * grad_scale, grad_totals[3] * grad_scale, grad_totals[4] * grad_scale)
```

```python
import functools

import jax
import jax.numpy as jnp
from jax import lax
from jax.experimental import pallas as pl
from jax.experimental.pallas import tpu as pltpu
from jax.sharding import PartitionSpec as P

BLOCK = 128
LEVELS = 37
SUB = 6


OMEGA = 30.0
TILE = 512


def padded_2(block, sides, width):
    for axis, dim in sides:
        count = lax.axis_size(axis)
        forward = [(i, i + 1) for i in range(count - 1)]
        forward.append((count - 1, 0))
        backward = [(target, source) for source, target in forward]
        low = lax.ppermute(
            lax.slice_in_dim(block, block.shape[dim] - width, None, axis=dim), axis, forward
        )
        high = lax.ppermute(lax.slice_in_dim(block, 0, width, axis=dim), axis, backward)
        block = jnp.concatenate([low, block, high], axis=dim)
    return block


def conv_apply(padded, kernel, row_count, col_count, flipped):
    channels = padded.shape[-1]
    result = jnp.zeros((row_count * col_count, kernel.shape[-1]), jnp.float32)
    for shift_a in (-1, 0, 1):
        for shift_b in (-1, 0, 1):
            tap_index = (shift_a + 1) * 3 + shift_b + 1
            if flipped:
                window = padded[
                    1 - shift_a : 1 - shift_a + row_count, 1 - shift_b : 1 - shift_b + col_count
                ]
                matrix = kernel[tap_index].T
            else:
                window = padded[
                    1 + shift_a : 1 + shift_a + row_count, 1 + shift_b : 1 + shift_b + col_count
                ]
                matrix = kernel[tap_index]
            result = result + jnp.dot(
                window.reshape(row_count * col_count, channels),
                matrix,
                preferred_element_type=jnp.float32,
            )
    return result


def conv_weight_grad(padded, grads, row_count, col_count):
    flat_grads = grads.reshape(row_count * col_count, -1)
    pieces = []
    for shift_a in (-1, 0, 1):
        for shift_b in (-1, 0, 1):
            window = padded[
                1 + shift_a : 1 + shift_a + row_count, 1 + shift_b : 1 + shift_b + col_count
            ]
            window = window.reshape(row_count * col_count, -1)
            pieces.append(jnp.dot(window.T, flat_grads, preferred_element_type=jnp.float32))
    return jnp.stack(pieces)


def close_poles(padded, lat_pos, lat_parts):
    top_rim = jnp.where(lat_pos == 0, jnp.zeros_like(padded[:1]), padded[:1])
    bottom_rim = jnp.where(lat_pos == lat_parts - 1, jnp.zeros_like(padded[-1:]), padded[-1:])
    return jnp.concatenate([top_rim, padded[1:-1], bottom_rim], axis=0)


SIN_TERMS = (
    0.7071067781421408,
    -0.029462767114633488,
    0.0003682722504284759,
    -2.1886040931894034e-06,
    7.195418014521965e-09,
)
COS_TERMS = (
    1.4142134959273227,
    -0.17677635831469551,
    0.0036825740917005817,
    -3.061241565438332e-05,
    1.2789559619534725e-07,
)
TURN = 6.283185307179586
TURN_HIGH = 6.28125
TURN_LOW = TURN - TURN_HIGH
EXTRA = 16
COORD_ROWS = 32
CHUNK = 64
LANES = 128


def sin_cos(angle):
    turns = jnp.round(angle * (1.0 / TURN))
    rest = (angle - turns * TURN_HIGH) - turns * TURN_LOW
    square = rest * rest

    def series(terms):
        value = jnp.full_like(square, terms[-1])
        for term in terms[-2::-1]:
            value = value * square + term
        return value

    half_sin = rest * series(SIN_TERMS)
    half_cos = series(COS_TERMS)
    return half_sin * half_cos, 1.0 - half_sin * half_sin


def query_kernel(
    cuts,
    scale,
    offsets_ref,
    rows_ref,
    coords_ref,
    features_ref,
    map_ref,
    coord_weight_ref,
    columns_ref,
    hidden_ref,
    map_grad_ref,
    hidden_grad_ref,
    small_ref,
    feature_grad_ref,
    feat_t,
    weight0,
    weight1,
    column_tiles,
    stack0,
    stack1,
    picks,
    pre,
    cos0,
    rounded0,
    rounded1,
    sums,
    hidden_sums,
    out_sums,
):
    step = pl.program_id(0)
    cells, channels = features_ref.shape
    hidden = hidden_ref.shape[0]
    block = rows_ref.shape[1]
    f32, bf16 = jnp.float32, jnp.bfloat16

    @pl.when(step == 0)
    def _():
        feat_t[...] = features_ref[...].T
        weight0[:, :channels] = map_ref[:, :hidden].T
        coef = coord_weight_ref[...]
        high = coef.astype(bf16).astype(f32)
        mid = (coef - high).astype(bf16).astype(f32)
        low = coef - high - mid
        parts = jnp.concatenate([high, mid, low, jnp.zeros((LANES - 24, hidden), f32)], axis=0)
        weight0[:, channels:] = parts.T.astype(bf16)
        weight1[:, :hidden] = hidden_ref[...].T
        weight1[:, hidden:] = map_ref[:, hidden:].T
        column_tiles[...] = columns_ref[...].T
        stack0[...] = jnp.zeros_like(stack0)
        sums[...] = jnp.zeros_like(sums)
        hidden_sums[...] = jnp.zeros_like(hidden_sums)
        out_sums[...] = jnp.zeros_like(out_sums)

    cell = rows_ref[0:1, :].astype(jnp.int32)
    ids = lax.broadcasted_iota(jnp.int32, (cells, block), 0)
    picks[:cells, :] = jnp.where(ids == cell, 1.0, 0.0).astype(bf16)
    picks[cells:, :] = coords_ref[:EXTRA, :]
    queried = jnp.dot(feat_t[...], picks[:cells, :], preferred_element_type=f32).astype(bf16)
    stack0[:channels, :] = queried
    stack0[channels : channels + COORD_ROWS, :] = coords_ref[...]
    stack1[hidden:, :] = queried
    pre[...] = jnp.dot(weight0[...], stack0[...], preferred_element_type=f32)
    for top in range(0, hidden, CHUNK):
        for left in range(0, block, LANES):
            at = (slice(top, top + CHUNK), slice(left, left + LANES))
            sine, cosine = sin_cos(pre[at])
            stack1[at] = sine.astype(bf16)
            cos0[at] = cosine
    pre[...] = jnp.dot(weight1[...], stack1[...], preferred_element_type=f32)
    for top in range(0, hidden, CHUNK):
        rows = slice(top, top + CHUNK)
        bias = column_tiles[rows, :LANES]
        out_weight = column_tiles[rows, LANES:]
        total = out_sums[rows, :]
        for left in range(0, block, LANES):
            at = (rows, slice(left, left + LANES))
            cotan = rows_ref[1:2, left : left + LANES]
            sine, cosine = sin_cos(pre[at] + bias)
            total = total + sine * cotan
            rounded1[at] = (out_weight * cotan * cosine).astype(bf16)
        out_sums[rows, :] = total
    act_grad = jnp.dot(hidden_ref[...], rounded1[...], preferred_element_type=f32)
    rounded0[...] = (act_grad * cos0[...]).astype(bf16)
    across = (((1,), (1,)), ((), ()))
    sums[:, hidden:] += lax.dot_general(
        picks[...], rounded1[...], across, preferred_element_type=f32
    )
    hidden_sums[...] += lax.dot_general(
        stack1[:hidden, :], rounded1[...], across, preferred_element_type=f32
    )
    sums[:, :hidden] += lax.dot_general(
        picks[...], rounded0[...], across, preferred_element_type=f32
    )

    @pl.when(step == pl.num_programs(0) - 1)
    def _():
        cell_sums = sums[:cells, :]
        upper = cell_sums.astype(bf16)
        lower = (cell_sums - upper.astype(f32)).astype(bf16)
        map_grad_ref[...] = (
            jnp.dot(feat_t[...], upper, preferred_element_type=f32)
            + jnp.dot(feat_t[...], lower, preferred_element_type=f32)
        ) * scale
        feature_grad_ref[...] = (
            lax.dot_general(upper, map_ref[...], across, preferred_element_type=f32)
            + lax.dot_general(lower, map_ref[...], across, preferred_element_type=f32)
        ).astype(bf16)
        hidden_grad_ref[...] = hidden_sums[...] * scale
        extra = sums[cells : cells + 8, :]
        lat_cell, lat_sub, lon_cell, lon_sub, level, level_offset = cuts
        total = extra[5:6, :hidden]
        lat_grad = (
            lat_cell * extra[0:1, :hidden]
            + lat_sub * extra[1:2, :hidden]
            + offsets_ref[0] * total
        )
        lon_grad = (
            lon_cell * extra[2:3, :hidden]
            + lon_sub * extra[3:4, :hidden]
            + offsets_ref[1] * total
        )
        level_grad = level * extra[4:5, :hidden] + level_offset * total
        out_grad = jnp.sum(out_sums[...].T, axis=0, keepdims=True)
        gain = OMEGA * scale
        small_ref[...] = jnp.zeros_like(small_ref)
        small_ref[0:1, :] = extra[5:6, :] * scale
        small_ref[1:2, :] = jnp.concatenate([lat_grad, lon_grad], axis=1) * gain
        small_ref[2:3, :] = jnp.concatenate([level_grad * gain, out_grad * scale], axis=1)


def query_pass(
    features, rows, coords, offsets, coord_weight, columns, map_weight, hidden_weight, cuts, scale
):
    cells, channels = features.shape
    queries = rows.shape[1]
    hidden = hidden_weight.shape[0]
    width = map_weight.shape[1]
    block = min(TILE, queries)
    f32, bf16 = jnp.float32, jnp.bfloat16

    def whole(shape):
        return pl.BlockSpec(shape, lambda i: (0,) * len(shape))

    return pl.pallas_call(
        functools.partial(query_kernel, cuts, scale),
        grid=(queries // block,),
        in_specs=[
            pl.BlockSpec(memory_space=pltpu.SMEM),
            pl.BlockSpec((rows.shape[0], block), lambda i: (0, i)),
            pl.BlockSpec((COORD_ROWS, block), lambda i: (0, i)),
            whole(features.shape),
            whole(map_weight.shape),
            whole(coord_weight.shape),
            whole(columns.shape),
            whole(hidden_weight.shape),
        ],
        out_specs=[
            whole((channels, width)),
            whole((hidden, hidden)),
            whole((8, width)),
            whole((cells, channels)),
        ],
        out_shape=[
            jax.ShapeDtypeStruct((channels, width), f32),
            jax.ShapeDtypeStruct((hidden, hidden), f32),
            jax.ShapeDtypeStruct((8, width), f32),
            jax.ShapeDtypeStruct((cells, channels), bf16),
        ],
        scratch_shapes=[
            pltpu.VMEM((channels, cells), bf16),
            pltpu.VMEM((hidden, channels + LANES), bf16),
            pltpu.VMEM((hidden, hidden + channels), bf16),
            pltpu.VMEM((hidden, 2 * LANES), f32),
            pltpu.VMEM((channels + LANES, block), bf16),
            pltpu.VMEM((hidden + channels, block), bf16),
            pltpu.VMEM((cells + EXTRA, block), bf16),
            pltpu.VMEM((hidden, block), f32),
            pltpu.VMEM((hidden, block), f32),
            pltpu.VMEM((hidden, block), bf16),
            pltpu.VMEM((hidden, block), bf16),
            pltpu.VMEM((cells + EXTRA, width), f32),
            pltpu.VMEM((hidden, hidden), f32),
            pltpu.VMEM((hidden, LANES), f32),
        ],
        compiler_params=pltpu.CompilerParams(vmem_limit_bytes=48 * 1024 * 1024),
        name="queries",
    )(offsets, rows, coords, features, map_weight, coord_weight, columns, hidden_weight)


def on_device(
    latents,
    conv_weight,
    map_weight,
    map_bias,
    input_weight,
    hidden_weight,
    output_weight,
    hit_owner,
    serve_block,
    query_grid,
    cotangent,
):
    lat_tile, lon_tile, channels = latents.shape
    lat_parts = lax.axis_size("lat")
    lon_parts = lax.axis_size("lon")
    dev_count = lat_parts * lon_parts
    lat_cells = lat_tile * lat_parts
    lon_cells = lon_tile * lon_parts
    block_rows = BLOCK
    lat_pos = lax.axis_index("lat")
    lon_pos = lax.axis_index("lon")
    padded = close_poles(padded_2(latents, (("lat", 0), ("lon", 1)), 1), lat_pos, lat_parts)
    features = conv_apply(padded, conv_weight, lat_tile, lon_tile, False).astype(jnp.bfloat16)
    serve_row = serve_block[0]
    hit_count = hit_owner.shape[0]
    group_size = cotangent.shape[0] // hit_count
    grid_groups = query_grid.reshape(3, hit_count, group_size).transpose(1, 0, 2)
    query_rows = jnp.concatenate(
        [
            grid_groups.astype(jnp.float32),
            cotangent.reshape(hit_count, 1, group_size),
        ],
        axis=1,
    ).reshape(hit_count, 4 * group_size)
    sent = jnp.zeros((dev_count, 4 * group_size), jnp.float32).at[hit_owner].set(query_rows)
    got = lax.all_to_all(sent, ("lat", "lon"), split_axis=0, concat_axis=0, tiled=True)
    got = got.reshape(dev_count, 4, group_size).transpose(1, 0, 2)
    block_cell = got[0].astype(jnp.int32)
    sub = got[1].astype(jnp.int32)
    tile_cell = jnp.where(
        serve_row[:, None] < 0, -1, serve_row[:, None] * block_rows + block_cell
    )
    queries = dev_count * group_size
    zero_row = jnp.zeros((dev_count, group_size), jnp.int32)
    coord_group = jnp.stack(
        [
            tile_cell // lon_tile,
            sub // SUB,
            tile_cell % lon_tile,
            sub % SUB,
            got[2].astype(jnp.int32),
            zero_row + 1,
            zero_row,
            zero_row,
        ]
    ).reshape(8, queries)
    coords = jnp.concatenate([coord_group] * 3 + [jnp.zeros_like(coord_group)], axis=0).astype(
        jnp.bfloat16
    )
    rows = jnp.concatenate(
        [tile_cell.astype(jnp.float32)[None], got[3][None]], axis=0
    ).reshape(2, queries)
    rows = jnp.pad(rows, ((0, 6), (0, 0)))
    lat_offset = (2 * SUB * lat_tile * lat_pos + 1).astype(jnp.float32) / (lat_cells * SUB) - 1.0
    lon_offset = (2 * SUB * lon_tile * lon_pos + 1).astype(jnp.float32) / (lon_cells * SUB) - 1.0
    level_offset = 1.0 / LEVELS - 1.0
    cuts = (
        2.0 / lat_cells,
        2.0 / (lat_cells * SUB),
        2.0 / lon_cells,
        2.0 / (lon_cells * SUB),
        2.0 / LEVELS,
        level_offset,
    )
    width = input_weight.shape[1]
    coord_weight = jnp.stack(
        [
            OMEGA * cuts[0] * input_weight[0],
            OMEGA * cuts[1] * input_weight[0],
            OMEGA * cuts[2] * input_weight[1],
            OMEGA * cuts[3] * input_weight[1],
            OMEGA * cuts[4] * input_weight[2],
            OMEGA
            * (
                lat_offset * input_weight[0]
                + lon_offset * input_weight[1]
                + level_offset * input_weight[2]
            )
            + map_bias[:width],
            jnp.zeros_like(input_weight[0]),
            jnp.zeros_like(input_weight[0]),
        ]
    )
    columns = jnp.concatenate(
        [
            jnp.broadcast_to(map_bias[None, width:], (LANES, width)),
            jnp.broadcast_to(output_weight[None, :], (LANES, width)),
        ],
        axis=0,
    )
    grad_scale = float(hit_count * group_size * dev_count) ** (-0.5)
    map_grad, hidden_grad, small, tile_grads = query_pass(
        features,
        rows,
        coords,
        jnp.stack([lat_offset, lon_offset]),
        coord_weight,
        columns,
        map_weight,
        hidden_weight[0],
        cuts,
        grad_scale,
    )
    feature_grad = tile_grads.reshape(lat_tile, lon_tile, channels).astype(jnp.bfloat16)
    padded_grad = close_poles(
        padded_2(feature_grad, (("lat", 0), ("lon", 1)), 1), lat_pos, lat_parts
    )
    latent_grad = conv_apply(padded_grad, conv_weight, lat_tile, lon_tile, True).reshape(
        lat_tile, lon_tile, channels
    )
    conv_local = conv_weight_grad(padded, feature_grad, lat_tile, lon_tile)
    conv_total, map_total, hidden_total, small_total = lax.psum(
        (conv_local * grad_scale, map_grad, hidden_grad, small), ("lat", "lon")
    )
    input_total = jnp.stack(
        [small_total[1, :width], small_total[1, width:], small_total[2, :width]]
    )
    return (
        latent_grad,
        conv_total,
        map_total,
        small_total[0],
        input_total,
        hidden_total[None],
        small_total[2, width:],
    )


def solution(mesh):
    placed = (
        P("lat", "lon", None),
        P(),
        P(),
        P(),
        P(),
        P(),
        P(),
        P(("lat", "lon")),
        P(("lat", "lon"), None),
        P(None, ("lat", "lon")),
        P(("lat", "lon")),
    )
    return jax.shard_map(
        on_device,
        mesh=mesh,
        in_specs=placed,
        out_specs=(P("lat", "lon", None), P(), P(), P(), P(), P(), P()),
        check_vma=False,
    )
```

```python
import functools

import jax
import jax.numpy as jnp
from jax import lax
from jax.experimental import pallas as pl
from jax.experimental.pallas import tpu as pltpu
from jax.sharding import PartitionSpec as P

BLOCK = 128
LEVELS = 37
SUB = 6


OMEGA = 30.0
TILE = 512
PARTS = 8


def padded_2(block, sides, width):
    for axis, dim in sides:
        count = lax.axis_size(axis)
        forward = [(i, i + 1) for i in range(count - 1)]
        forward.append((count - 1, 0))
        backward = [(target, source) for source, target in forward]
        low = lax.ppermute(
            lax.slice_in_dim(block, block.shape[dim] - width, None, axis=dim), axis, forward
        )
        high = lax.ppermute(lax.slice_in_dim(block, 0, width, axis=dim), axis, backward)
        block = jnp.concatenate([low, block, high], axis=dim)
    return block


def conv_apply(padded, kernel, row_count, col_count, flipped):
    channels = padded.shape[-1]
    result = jnp.zeros((row_count * col_count, kernel.shape[-1]), jnp.float32)
    for shift_a in (-1, 0, 1):
        for shift_b in (-1, 0, 1):
            tap_index = (shift_a + 1) * 3 + shift_b + 1
            if flipped:
                window = padded[
                    1 - shift_a : 1 - shift_a + row_count, 1 - shift_b : 1 - shift_b + col_count
                ]
                matrix = kernel[tap_index].T
            else:
                window = padded[
                    1 + shift_a : 1 + shift_a + row_count, 1 + shift_b : 1 + shift_b + col_count
                ]
                matrix = kernel[tap_index]
            result = result + jnp.dot(
                window.reshape(row_count * col_count, channels),
                matrix,
                preferred_element_type=jnp.float32,
            )
    return result


def conv_weight_grad(padded, grads, row_count, col_count):
    flat_grads = grads.reshape(row_count * col_count, -1)
    pieces = []
    for shift_a in (-1, 0, 1):
        for shift_b in (-1, 0, 1):
            window = padded[
                1 + shift_a : 1 + shift_a + row_count, 1 + shift_b : 1 + shift_b + col_count
            ]
            window = window.reshape(row_count * col_count, -1)
            pieces.append(jnp.dot(window.T, flat_grads, preferred_element_type=jnp.float32))
    return jnp.stack(pieces)


def close_poles(padded, lat_pos, lat_parts):
    top_rim = jnp.where(lat_pos == 0, jnp.zeros_like(padded[:1]), padded[:1])
    bottom_rim = jnp.where(lat_pos == lat_parts - 1, jnp.zeros_like(padded[-1:]), padded[-1:])
    return jnp.concatenate([top_rim, padded[1:-1], bottom_rim], axis=0)


SIN_TERMS = (
    0.7071067781421408,
    -0.029462767114633488,
    0.0003682722504284759,
    -2.1886040931894034e-06,
    7.195418014521965e-09,
)
COS_TERMS = (
    1.4142134959273227,
    -0.17677635831469551,
    0.0036825740917005817,
    -3.061241565438332e-05,
    1.2789559619534725e-07,
)
TURN = 6.283185307179586
TURN_HIGH = 6.28125
TURN_LOW = TURN - TURN_HIGH
EXTRA = 16
COORD_ROWS = 32
CHUNK = 64
LANES = 128


def sin_cos(angle):
    turns = jnp.round(angle * (1.0 / TURN))
    rest = (angle - turns * TURN_HIGH) - turns * TURN_LOW
    square = rest * rest

    def series(terms):
        value = jnp.full_like(square, terms[-1])
        for term in terms[-2::-1]:
            value = value * square + term
        return value

    half_sin = rest * series(SIN_TERMS)
    half_cos = series(COS_TERMS)
    return half_sin * half_cos, 1.0 - half_sin * half_sin


def query_kernel(
    cuts,
    scale,
    offsets_ref,
    rows_ref,
    coords_ref,
    features_ref,
    map_ref,
    coord_weight_ref,
    columns_ref,
    hidden_ref,
    shares_ref,
    feature_grad_ref,
    feat_t,
    weight0,
    weight1,
    column_tiles,
    stack0,
    stack1,
    picks,
    pre,
    cos0,
    rounded0,
    rounded1,
    sums,
    hidden_sums,
    out_sums,
):
    step = pl.program_id(0)
    cells, channels = features_ref.shape
    hidden = hidden_ref.shape[0]
    block = rows_ref.shape[1]
    f32, bf16 = jnp.float32, jnp.bfloat16

    @pl.when(step == 0)
    def _():
        feat_t[...] = features_ref[...].T
        weight0[:, :channels] = map_ref[:, :hidden].T
        coef = coord_weight_ref[...]
        high = coef.astype(bf16).astype(f32)
        mid = (coef - high).astype(bf16).astype(f32)
        low = coef - high - mid
        parts = jnp.concatenate([high, mid, low, jnp.zeros((LANES - 24, hidden), f32)], axis=0)
        weight0[:, channels:] = parts.T.astype(bf16)
        weight1[:, :hidden] = hidden_ref[...].T
        weight1[:, hidden:] = map_ref[:, hidden:].T
        column_tiles[...] = columns_ref[...].T
        stack0[...] = jnp.zeros_like(stack0)
        sums[...] = jnp.zeros_like(sums)
        hidden_sums[...] = jnp.zeros_like(hidden_sums)
        out_sums[...] = jnp.zeros_like(out_sums)

    cell = rows_ref[0:1, :].astype(jnp.int32)
    ids = lax.broadcasted_iota(jnp.int32, (cells, block), 0)
    picks[:cells, :] = jnp.where(ids == cell, 1.0, 0.0).astype(bf16)
    picks[cells:, :] = coords_ref[:EXTRA, :]
    queried = jnp.dot(feat_t[...], picks[:cells, :], preferred_element_type=f32).astype(bf16)
    stack0[:channels, :] = queried
    stack0[channels : channels + COORD_ROWS, :] = coords_ref[...]
    stack1[hidden:, :] = queried
    pre[...] = jnp.dot(weight0[...], stack0[...], preferred_element_type=f32)
    for top in range(0, hidden, CHUNK):
        for left in range(0, block, LANES):
            at = (slice(top, top + CHUNK), slice(left, left + LANES))
            sine, cosine = sin_cos(pre[at])
            stack1[at] = sine.astype(bf16)
            cos0[at] = cosine
    pre[...] = jnp.dot(weight1[...], stack1[...], preferred_element_type=f32)
    for top in range(0, hidden, CHUNK):
        rows = slice(top, top + CHUNK)
        bias = column_tiles[rows, :LANES]
        out_weight = column_tiles[rows, LANES:]
        total = out_sums[rows, :]
        for left in range(0, block, LANES):
            at = (rows, slice(left, left + LANES))
            cotan = rows_ref[1:2, left : left + LANES]
            sine, cosine = sin_cos(pre[at] + bias)
            total = total + sine * cotan
            rounded1[at] = (out_weight * cotan * cosine).astype(bf16)
        out_sums[rows, :] = total
    act_grad = jnp.dot(hidden_ref[...], rounded1[...], preferred_element_type=f32)
    rounded0[...] = (act_grad * cos0[...]).astype(bf16)
    across = (((1,), (1,)), ((), ()))
    sums[:, hidden:] += lax.dot_general(
        picks[...], rounded1[...], across, preferred_element_type=f32
    )
    hidden_sums[...] += lax.dot_general(
        stack1[:hidden, :], rounded1[...], across, preferred_element_type=f32
    )
    sums[:, :hidden] += lax.dot_general(
        picks[...], rounded0[...], across, preferred_element_type=f32
    )

    @pl.when(step == pl.num_programs(0) - 1)
    def _():
        cell_sums = sums[:cells, :]
        upper = cell_sums.astype(bf16)
        lower = (cell_sums - upper.astype(f32)).astype(bf16)
        map_grad = (
            jnp.dot(feat_t[...], upper, preferred_element_type=f32)
            + jnp.dot(feat_t[...], lower, preferred_element_type=f32)
        ) * scale
        feature_grad_ref[...] = (
            lax.dot_general(upper, map_ref[...], across, preferred_element_type=f32)
            + lax.dot_general(lower, map_ref[...], across, preferred_element_type=f32)
        ).astype(bf16)
        hidden_grad = hidden_sums[...] * scale
        extra = sums[cells : cells + 8, :]
        lat_cell, lat_sub, lon_cell, lon_sub, level, level_offset = cuts
        total = extra[5:6, :hidden]
        lat_grad = (
            lat_cell * extra[0:1, :hidden]
            + lat_sub * extra[1:2, :hidden]
            + offsets_ref[0] * total
        )
        lon_grad = (
            lon_cell * extra[2:3, :hidden]
            + lon_sub * extra[3:4, :hidden]
            + offsets_ref[1] * total
        )
        level_grad = level * extra[4:5, :hidden] + level_offset * total
        out_grad = jnp.sum(out_sums[...].T, axis=0, keepdims=True)
        gain = OMEGA * scale
        small = jnp.concatenate(
            [
                extra[5:6, :] * scale,
                jnp.concatenate([lat_grad, lon_grad], axis=1) * gain,
                jnp.concatenate([level_grad * gain, out_grad * scale], axis=1),
                jnp.zeros((EXTRA - 3, 2 * hidden), f32),
            ],
            axis=0,
        )
        folds = hidden_grad.shape[1] // LANES
        for part in range(shares_ref.shape[0]):
            lanes = slice(part * LANES, (part + 1) * LANES)
            top = part // folds * channels
            left = part % folds * LANES
            shares_ref[part, :channels, :] = map_grad[:, lanes].astype(bf16)
            shares_ref[part, channels : 2 * channels, :] = hidden_grad[
                top : top + channels, left : left + LANES
            ].astype(bf16)
            shares_ref[part, 2 * channels :, :] = small[:, lanes].astype(bf16)


def query_pass(
    features, rows, coords, offsets, coord_weight, columns, map_weight, hidden_weight, cuts, scale
):
    cells, channels = features.shape
    queries = rows.shape[1]
    hidden = hidden_weight.shape[0]
    width = map_weight.shape[1]
    block = min(TILE, queries)
    f32, bf16 = jnp.float32, jnp.bfloat16

    def whole(shape):
        return pl.BlockSpec(shape, lambda i: (0,) * len(shape))

    return pl.pallas_call(
        functools.partial(query_kernel, cuts, scale),
        grid=(queries // block,),
        in_specs=[
            pl.BlockSpec(memory_space=pltpu.SMEM),
            pl.BlockSpec((rows.shape[0], block), lambda i: (0, i)),
            pl.BlockSpec((COORD_ROWS, block), lambda i: (0, i)),
            whole(features.shape),
            whole(map_weight.shape),
            whole(coord_weight.shape),
            whole(columns.shape),
            whole(hidden_weight.shape),
        ],
        out_specs=[
            whole((PARTS, 2 * channels + EXTRA, LANES)),
            whole((cells, channels)),
        ],
        out_shape=[
            jax.ShapeDtypeStruct((PARTS, 2 * channels + EXTRA, LANES), bf16),
            jax.ShapeDtypeStruct((cells, channels), bf16),
        ],
        scratch_shapes=[
            pltpu.VMEM((channels, cells), bf16),
            pltpu.VMEM((hidden, channels + LANES), bf16),
            pltpu.VMEM((hidden, hidden + channels), bf16),
            pltpu.VMEM((hidden, 2 * LANES), f32),
            pltpu.VMEM((channels + LANES, block), bf16),
            pltpu.VMEM((hidden + channels, block), bf16),
            pltpu.VMEM((cells + EXTRA, block), bf16),
            pltpu.VMEM((hidden, block), f32),
            pltpu.VMEM((hidden, block), f32),
            pltpu.VMEM((hidden, block), bf16),
            pltpu.VMEM((hidden, block), bf16),
            pltpu.VMEM((cells + EXTRA, width), f32),
            pltpu.VMEM((hidden, hidden), f32),
            pltpu.VMEM((hidden, LANES), f32),
        ],
        compiler_params=pltpu.CompilerParams(vmem_limit_bytes=48 * 1024 * 1024),
        name="queries",
    )(offsets, rows, coords, features, map_weight, coord_weight, columns, hidden_weight)


def bits_of(axis):
    return lax.axis_size(axis).bit_length() - 1


def flip(values, step):
    axis, bit = step
    count = lax.axis_size(axis)
    return lax.ppermute(values, axis, [(i, i ^ (1 << bit)) for i in range(count)])


def own_bit(step):
    axis, bit = step
    return (lax.axis_index(axis) >> bit) & 1


def added(left, right):
    return (left.astype(jnp.float32) + right.astype(jnp.float32)).astype(left.dtype)


def reduced(values, split_steps, plain_steps):
    for step in split_steps:
        halves = values.reshape((2, values.shape[0] // 2) + values.shape[1:])
        mine = own_bit(step)
        away = lax.dynamic_index_in_dim(halves, 1 - mine, 0, keepdims=False)
        kept = lax.dynamic_index_in_dim(halves, mine, 0, keepdims=False)
        values = added(kept, flip(away, step))
    for step in plain_steps:
        values = added(values, flip(values, step))
    return values


def joined(mine, theirs, step):
    first = own_bit(step) == 0
    return jnp.concatenate(
        [jnp.where(first, mine, theirs), jnp.where(first, theirs, mine)], axis=0
    )


def gathered(values, split_steps):
    for step in split_steps[:0:-1]:
        values = joined(values, flip(values, step), step)
    return values, flip(values, split_steps[0])


def unpack_kernel(
    bit_ref, mine_a, theirs_a, mine_b, theirs_b, map_ref, hidden_ref, small_ref, conv_ref
):
    f32 = jnp.float32
    channels = map_ref.shape[0]
    folds = hidden_ref.shape[1] // LANES
    half = PARTS // 2

    def fill(low_a, high_a, low_b, high_b):
        for part in range(PARTS):
            source = (low_a if part < half else high_a).at[part % half]
            lanes = slice(part * LANES, (part + 1) * LANES)
            top = part // folds * channels
            left = part % folds * LANES
            map_ref[:, lanes] = source[:channels, :].astype(f32)
            hidden_ref[top : top + channels, left : left + LANES] = source[
                channels : 2 * channels, :
            ].astype(f32)
            small_ref[:, lanes] = source[2 * channels : 2 * channels + 8, :].astype(f32)
            source = (low_b if part < half else high_b).at[part % half]
            rows = source.shape[0]
            conv_ref[part * rows : (part + 1) * rows, :] = source[...].astype(f32)

    @pl.when(bit_ref[0] == 0)
    def _():
        fill(mine_a, theirs_a, mine_b, theirs_b)

    @pl.when(bit_ref[0] == 1)
    def _():
        fill(theirs_a, mine_a, theirs_b, mine_b)


def unpacked(bit, pair_a, pair_b, channels, hidden, width, conv_rows):
    f32 = jnp.float32
    vmem = pl.BlockSpec(memory_space=pltpu.VMEM)
    return pl.pallas_call(
        unpack_kernel,
        in_specs=[pl.BlockSpec(memory_space=pltpu.SMEM)] + [vmem] * 4,
        out_specs=[vmem] * 4,
        out_shape=[
            jax.ShapeDtypeStruct((channels, width), f32),
            jax.ShapeDtypeStruct((hidden, hidden), f32),
            jax.ShapeDtypeStruct((8, width), f32),
            jax.ShapeDtypeStruct((conv_rows, channels), f32),
        ],
        compiler_params=pltpu.CompilerParams(vmem_limit_bytes=32 * 1024 * 1024),
        name="unpack",
    )(bit.reshape(1), *pair_a, *pair_b)


def on_device(
    latents,
    conv_weight,
    map_weight,
    map_bias,
    input_weight,
    hidden_weight,
    output_weight,
    hit_owner,
    serve_block,
    query_grid,
    cotangent,
):
    lat_tile, lon_tile, channels = latents.shape
    lat_parts = lax.axis_size("lat")
    lon_parts = lax.axis_size("lon")
    dev_count = lat_parts * lon_parts
    lat_cells = lat_tile * lat_parts
    lon_cells = lon_tile * lon_parts
    block_rows = BLOCK
    lat_pos = lax.axis_index("lat")
    lon_pos = lax.axis_index("lon")
    padded = close_poles(padded_2(latents, (("lat", 0), ("lon", 1)), 1), lat_pos, lat_parts)
    features = conv_apply(padded, conv_weight, lat_tile, lon_tile, False).astype(jnp.bfloat16)
    serve_row = serve_block[0]
    hit_count = hit_owner.shape[0]
    group_size = cotangent.shape[0] // hit_count
    grid_groups = query_grid.reshape(3, hit_count, group_size).transpose(1, 0, 2)
    query_rows = jnp.concatenate(
        [
            grid_groups.astype(jnp.float32),
            cotangent.reshape(hit_count, 1, group_size),
        ],
        axis=1,
    ).reshape(hit_count, 4 * group_size)
    sent = jnp.zeros((dev_count, 4 * group_size), jnp.float32).at[hit_owner].set(query_rows)
    got = lax.all_to_all(sent, ("lat", "lon"), split_axis=0, concat_axis=0, tiled=True)
    got = got.reshape(dev_count, 4, group_size).transpose(1, 0, 2)
    block_cell = got[0].astype(jnp.int32)
    sub = got[1].astype(jnp.int32)
    tile_cell = jnp.where(
        serve_row[:, None] < 0, -1, serve_row[:, None] * block_rows + block_cell
    )
    queries = dev_count * group_size
    zero_row = jnp.zeros((dev_count, group_size), jnp.int32)
    coord_group = jnp.stack(
        [
            tile_cell // lon_tile,
            sub // SUB,
            tile_cell % lon_tile,
            sub % SUB,
            got[2].astype(jnp.int32),
            zero_row + 1,
            zero_row,
            zero_row,
        ]
    ).reshape(8, queries)
    coords = jnp.concatenate([coord_group] * 3 + [jnp.zeros_like(coord_group)], axis=0).astype(
        jnp.bfloat16
    )
    rows = jnp.concatenate(
        [tile_cell.astype(jnp.float32)[None], got[3][None]], axis=0
    ).reshape(2, queries)
    rows = jnp.pad(rows, ((0, 6), (0, 0)))
    lat_offset = (2 * SUB * lat_tile * lat_pos + 1).astype(jnp.float32) / (lat_cells * SUB) - 1.0
    lon_offset = (2 * SUB * lon_tile * lon_pos + 1).astype(jnp.float32) / (lon_cells * SUB) - 1.0
    level_offset = 1.0 / LEVELS - 1.0
    cuts = (
        2.0 / lat_cells,
        2.0 / (lat_cells * SUB),
        2.0 / lon_cells,
        2.0 / (lon_cells * SUB),
        2.0 / LEVELS,
        level_offset,
    )
    width = input_weight.shape[1]
    coord_weight = jnp.stack(
        [
            OMEGA * cuts[0] * input_weight[0],
            OMEGA * cuts[1] * input_weight[0],
            OMEGA * cuts[2] * input_weight[1],
            OMEGA * cuts[3] * input_weight[1],
            OMEGA * cuts[4] * input_weight[2],
            OMEGA
            * (
                lat_offset * input_weight[0]
                + lon_offset * input_weight[1]
                + level_offset * input_weight[2]
            )
            + map_bias[:width],
            jnp.zeros_like(input_weight[0]),
            jnp.zeros_like(input_weight[0]),
        ]
    )
    columns = jnp.concatenate(
        [
            jnp.broadcast_to(map_bias[None, width:], (LANES, width)),
            jnp.broadcast_to(output_weight[None, :], (LANES, width)),
        ],
        axis=0,
    )
    grad_scale = float(hit_count * group_size * dev_count) ** (-0.5)
    shares, tile_grads = query_pass(
        features,
        rows,
        coords,
        jnp.stack([lat_offset, lon_offset]),
        coord_weight,
        columns,
        map_weight,
        hidden_weight[0],
        cuts,
        grad_scale,
    )
    feature_grad = tile_grads.reshape(lat_tile, lon_tile, channels).astype(jnp.bfloat16)
    padded_grad = close_poles(
        padded_2(feature_grad, (("lat", 0), ("lon", 1)), 1), lat_pos, lat_parts
    )
    latent_grad = conv_apply(padded_grad, conv_weight, lat_tile, lon_tile, True).reshape(
        lat_tile, lon_tile, channels
    )
    conv_local = conv_weight_grad(padded, feature_grad, lat_tile, lon_tile)
    steps = [(axis, bit) for axis in ("lon", "lat") for bit in range(bits_of(axis))]
    split_a = steps[:3]
    split_b = [steps[0], steps[2], steps[1]]
    taps = conv_local.shape[0]
    conv_shares = (conv_local * grad_scale).astype(jnp.bfloat16)
    conv_shares = conv_shares.reshape(PARTS, taps * channels // PARTS, channels)
    pair_a = gathered(reduced(shares, split_a, steps[3:]), split_a)
    pair_b = gathered(reduced(conv_shares, split_b, steps[3:]), split_b)
    map_total, hidden_total, small_total, conv_total = unpacked(
        own_bit(steps[0]), pair_a, pair_b, channels, width, 2 * width, taps * channels
    )
    input_total = jnp.stack(
        [small_total[1, :width], small_total[1, width:], small_total[2, :width]]
    )
    return (
        latent_grad,
        conv_total.reshape(taps, channels, channels),
        map_total,
        small_total[0],
        input_total,
        hidden_total[None],
        small_total[2, width:],
    )


def solution(mesh):
    placed = (
        P("lat", "lon", None),
        P(),
        P(),
        P(),
        P(),
        P(),
        P(),
        P(("lat", "lon")),
        P(("lat", "lon"), None),
        P(None, ("lat", "lon")),
        P(("lat", "lon")),
    )
    return jax.shard_map(
        on_device,
        mesh=mesh,
        in_specs=placed,
        out_specs=(P("lat", "lon", None), P(), P(), P(), P(), P(), P()),
        check_vma=False,
    )
```

```python
import functools

import jax
import jax.numpy as jnp
from jax import lax
from jax.experimental import pallas as pl
from jax.experimental.pallas import tpu as pltpu
from jax.sharding import PartitionSpec as P

BLOCK = 128
LEVELS = 37
SUB = 6


OMEGA = 30.0
TILE = 512
PARTS = 8


def padded_2(block, sides, width):
    for axis, dim in sides:
        count = lax.axis_size(axis)
        forward = [(i, i + 1) for i in range(count - 1)]
        forward.append((count - 1, 0))
        backward = [(target, source) for source, target in forward]
        low = lax.ppermute(
            lax.slice_in_dim(block, block.shape[dim] - width, None, axis=dim), axis, forward
        )
        high = lax.ppermute(lax.slice_in_dim(block, 0, width, axis=dim), axis, backward)
        block = jnp.concatenate([low, block, high], axis=dim)
    return block


def conv_apply(padded, kernel, row_count, col_count, flipped):
    channels = padded.shape[-1]
    result = jnp.zeros((row_count * col_count, kernel.shape[-1]), jnp.float32)
    for shift_a in (-1, 0, 1):
        for shift_b in (-1, 0, 1):
            tap_index = (shift_a + 1) * 3 + shift_b + 1
            if flipped:
                window = padded[
                    1 - shift_a : 1 - shift_a + row_count, 1 - shift_b : 1 - shift_b + col_count
                ]
                matrix = kernel[tap_index].T
            else:
                window = padded[
                    1 + shift_a : 1 + shift_a + row_count, 1 + shift_b : 1 + shift_b + col_count
                ]
                matrix = kernel[tap_index]
            result = result + jnp.dot(
                window.reshape(row_count * col_count, channels),
                matrix,
                preferred_element_type=jnp.float32,
            )
    return result


def conv_weight_grad(padded, grads, row_count, col_count):
    flat_grads = grads.reshape(row_count * col_count, -1)
    pieces = []
    for shift_a in (-1, 0, 1):
        for shift_b in (-1, 0, 1):
            window = padded[
                1 + shift_a : 1 + shift_a + row_count, 1 + shift_b : 1 + shift_b + col_count
            ]
            window = window.reshape(row_count * col_count, -1)
            pieces.append(jnp.dot(window.T, flat_grads, preferred_element_type=jnp.float32))
    return jnp.stack(pieces)


def close_poles(padded, lat_pos, lat_parts):
    top_rim = jnp.where(lat_pos == 0, jnp.zeros_like(padded[:1]), padded[:1])
    bottom_rim = jnp.where(lat_pos == lat_parts - 1, jnp.zeros_like(padded[-1:]), padded[-1:])
    return jnp.concatenate([top_rim, padded[1:-1], bottom_rim], axis=0)


SIN_TERMS = (
    0.7071067781421408,
    -0.029462767114633488,
    0.0003682722504284759,
    -2.1886040931894034e-06,
    7.195418014521965e-09,
)
COS_TERMS = (
    1.4142134959273227,
    -0.17677635831469551,
    0.0036825740917005817,
    -3.061241565438332e-05,
    1.2789559619534725e-07,
)
TURN = 6.283185307179586
TURN_HIGH = 6.28125
TURN_LOW = TURN - TURN_HIGH
EXTRA = 16
COORD_ROWS = 32
CHUNK = 64
LANES = 128


def sin_cos(angle):
    turns = jnp.round(angle * (1.0 / TURN))
    rest = (angle - turns * TURN_HIGH) - turns * TURN_LOW
    square = rest * rest

    def series(terms):
        value = jnp.full_like(square, terms[-1])
        for term in terms[-2::-1]:
            value = value * square + term
        return value

    half_sin = rest * series(SIN_TERMS)
    half_cos = series(COS_TERMS)
    return half_sin * half_cos, 1.0 - half_sin * half_sin


def query_kernel(
    cuts,
    scale,
    offsets_ref,
    rows_ref,
    coords_ref,
    features_ref,
    map_ref,
    coord_weight_ref,
    columns_ref,
    hidden_ref,
    shares_ref,
    feature_grad_ref,
    feat_t,
    weight0,
    weight1,
    column_tiles,
    stack0,
    stack1,
    picks,
    pre,
    cos0,
    rounded0,
    rounded1,
    sums,
    hidden_sums,
    out_sums,
):
    step = pl.program_id(0)
    cells, channels = features_ref.shape
    hidden = hidden_ref.shape[0]
    block = rows_ref.shape[1]
    f32, bf16 = jnp.float32, jnp.bfloat16

    @pl.when(step == 0)
    def _():
        feat_t[...] = features_ref[...].T
        weight0[:, :channels] = map_ref[:, :hidden].T
        coef = coord_weight_ref[...]
        high = coef.astype(bf16).astype(f32)
        mid = (coef - high).astype(bf16).astype(f32)
        low = coef - high - mid
        parts = jnp.concatenate([high, mid, low, jnp.zeros((LANES - 24, hidden), f32)], axis=0)
        weight0[:, channels:] = parts.T.astype(bf16)
        weight1[:, :hidden] = hidden_ref[...].T
        weight1[:, hidden:] = map_ref[:, hidden:].T
        column_tiles[...] = columns_ref[...].T
        stack0[...] = jnp.zeros_like(stack0)
        sums[...] = jnp.zeros_like(sums)
        hidden_sums[...] = jnp.zeros_like(hidden_sums)
        out_sums[...] = jnp.zeros_like(out_sums)

    cell = rows_ref[0:1, :].astype(jnp.int32)
    ids = lax.broadcasted_iota(jnp.int32, (cells, block), 0)
    picks[:cells, :] = jnp.where(ids == cell, 1.0, 0.0).astype(bf16)
    picks[cells:, :] = coords_ref[:EXTRA, :]
    queried = jnp.dot(feat_t[...], picks[:cells, :], preferred_element_type=f32).astype(bf16)
    stack0[:channels, :] = queried
    stack0[channels : channels + COORD_ROWS, :] = coords_ref[...]
    stack1[hidden:, :] = queried
    pre[...] = jnp.dot(weight0[...], stack0[...], preferred_element_type=f32)
    for top in range(0, hidden, CHUNK):
        for left in range(0, block, LANES):
            at = (slice(top, top + CHUNK), slice(left, left + LANES))
            sine, cosine = sin_cos(pre[at])
            stack1[at] = sine.astype(bf16)
            cos0[at] = cosine
    pre[...] = jnp.dot(weight1[...], stack1[...], preferred_element_type=f32)
    for top in range(0, hidden, CHUNK):
        rows = slice(top, top + CHUNK)
        bias = column_tiles[rows, :LANES]
        out_weight = column_tiles[rows, LANES:]
        total = out_sums[rows, :]
        for left in range(0, block, LANES):
            at = (rows, slice(left, left + LANES))
            cotan = rows_ref[1:2, left : left + LANES]
            sine, cosine = sin_cos(pre[at] + bias)
            total = total + sine * cotan
            rounded1[at] = (out_weight * cotan * cosine).astype(bf16)
        out_sums[rows, :] = total
    act_grad = jnp.dot(hidden_ref[...], rounded1[...], preferred_element_type=f32)
    rounded0[...] = (act_grad * cos0[...]).astype(bf16)
    across = (((1,), (1,)), ((), ()))
    sums[:, hidden:] += lax.dot_general(
        picks[...], rounded1[...], across, preferred_element_type=f32
    )
    hidden_sums[...] += lax.dot_general(
        stack1[:hidden, :], rounded1[...], across, preferred_element_type=f32
    )
    sums[:, :hidden] += lax.dot_general(
        picks[...], rounded0[...], across, preferred_element_type=f32
    )

    @pl.when(step == pl.num_programs(0) - 1)
    def _():
        cell_sums = sums[:cells, :]
        upper = cell_sums.astype(bf16)
        lower = (cell_sums - upper.astype(f32)).astype(bf16)
        map_grad = (
            jnp.dot(feat_t[...], upper, preferred_element_type=f32)
            + jnp.dot(feat_t[...], lower, preferred_element_type=f32)
        ) * scale
        feature_grad_ref[...] = (
            lax.dot_general(upper, map_ref[...], across, preferred_element_type=f32)
            + lax.dot_general(lower, map_ref[...], across, preferred_element_type=f32)
        ).astype(bf16)
        hidden_grad = hidden_sums[...] * scale
        extra = sums[cells : cells + 8, :]
        lat_cell, lat_sub, lon_cell, lon_sub, level, level_offset = cuts
        total = extra[5:6, :hidden]
        lat_grad = (
            lat_cell * extra[0:1, :hidden]
            + lat_sub * extra[1:2, :hidden]
            + offsets_ref[0] * total
        )
        lon_grad = (
            lon_cell * extra[2:3, :hidden]
            + lon_sub * extra[3:4, :hidden]
            + offsets_ref[1] * total
        )
        level_grad = level * extra[4:5, :hidden] + level_offset * total
        out_grad = jnp.sum(out_sums[...].T, axis=0, keepdims=True)
        gain = OMEGA * scale
        small = jnp.concatenate(
            [
                extra[5:6, :] * scale,
                jnp.concatenate([lat_grad, lon_grad], axis=1) * gain,
                jnp.concatenate([level_grad * gain, out_grad * scale], axis=1),
                jnp.zeros((EXTRA - 3, 2 * hidden), f32),
            ],
            axis=0,
        )
        folds = hidden_grad.shape[1] // LANES
        for part in range(shares_ref.shape[0]):
            lanes = slice(part * LANES, (part + 1) * LANES)
            top = part // folds * channels
            left = part % folds * LANES
            shares_ref[part, :channels, :] = map_grad[:, lanes].astype(bf16)
            shares_ref[part, channels : 2 * channels, :] = hidden_grad[
                top : top + channels, left : left + LANES
            ].astype(bf16)
            shares_ref[part, 2 * channels :, :] = small[:, lanes].astype(bf16)


def query_pass(
    features, rows, coords, offsets, coord_weight, columns, map_weight, hidden_weight, cuts, scale
):
    cells, channels = features.shape
    queries = rows.shape[1]
    hidden = hidden_weight.shape[0]
    width = map_weight.shape[1]
    block = min(TILE, queries)
    f32, bf16 = jnp.float32, jnp.bfloat16

    def whole(shape):
        return pl.BlockSpec(shape, lambda i: (0,) * len(shape))

    return pl.pallas_call(
        functools.partial(query_kernel, cuts, scale),
        grid=(queries // block,),
        in_specs=[
            pl.BlockSpec(memory_space=pltpu.SMEM),
            pl.BlockSpec((rows.shape[0], block), lambda i: (0, i)),
            pl.BlockSpec((COORD_ROWS, block), lambda i: (0, i)),
            whole(features.shape),
            whole(map_weight.shape),
            whole(coord_weight.shape),
            whole(columns.shape),
            whole(hidden_weight.shape),
        ],
        out_specs=[
            whole((PARTS, 2 * channels + EXTRA, LANES)),
            whole((cells, channels)),
        ],
        out_shape=[
            jax.ShapeDtypeStruct((PARTS, 2 * channels + EXTRA, LANES), bf16),
            jax.ShapeDtypeStruct((cells, channels), bf16),
        ],
        scratch_shapes=[
            pltpu.VMEM((channels, cells), bf16),
            pltpu.VMEM((hidden, channels + LANES), bf16),
            pltpu.VMEM((hidden, hidden + channels), bf16),
            pltpu.VMEM((hidden, 2 * LANES), f32),
            pltpu.VMEM((channels + LANES, block), bf16),
            pltpu.VMEM((hidden + channels, block), bf16),
            pltpu.VMEM((cells + EXTRA, block), bf16),
            pltpu.VMEM((hidden, block), f32),
            pltpu.VMEM((hidden, block), f32),
            pltpu.VMEM((hidden, block), bf16),
            pltpu.VMEM((hidden, block), bf16),
            pltpu.VMEM((cells + EXTRA, width), f32),
            pltpu.VMEM((hidden, hidden), f32),
            pltpu.VMEM((hidden, LANES), f32),
        ],
        compiler_params=pltpu.CompilerParams(vmem_limit_bytes=48 * 1024 * 1024),
        name="queries",
    )(offsets, rows, coords, features, map_weight, coord_weight, columns, hidden_weight)


def bits_of(axis):
    return lax.axis_size(axis).bit_length() - 1


def flip(values, step):
    axis, bit = step
    count = lax.axis_size(axis)
    return lax.ppermute(values, axis, [(i, i ^ (1 << bit)) for i in range(count)])


def own_bit(step):
    axis, bit = step
    return (lax.axis_index(axis) >> bit) & 1


def added(left, right):
    return (left.astype(jnp.float32) + right.astype(jnp.float32)).astype(left.dtype)


def halved(values, step):
    halves = values.reshape((2, values.shape[0] // 2) + values.shape[1:])
    mine = own_bit(step)
    away = lax.dynamic_index_in_dim(halves, 1 - mine, 0, keepdims=False)
    kept = lax.dynamic_index_in_dim(halves, mine, 0, keepdims=False)
    return added(kept, flip(away, step))


def reduced(values, split_steps, plain_steps):
    for step in split_steps:
        values = halved(values, step)
    for step in plain_steps:
        values = added(values, flip(values, step))
    return values


def joined(mine, theirs, step):
    first = own_bit(step) == 0
    return jnp.concatenate(
        [jnp.where(first, mine, theirs), jnp.where(first, theirs, mine)], axis=0
    )


def gathered(values, split_steps):
    for step in split_steps[:0:-1]:
        values = joined(values, flip(values, step), step)
    return values, flip(values, split_steps[0])


def unpack_kernel(
    bit_ref,
    mine_a,
    theirs_a,
    mine_b,
    theirs_b,
    conv_ref,
    map_ref,
    bias_ref,
    input_ref,
    hidden_ref,
    out_ref,
):
    f32 = jnp.float32
    channels = map_ref.shape[0]
    folds = hidden_ref.shape[1] // LANES
    half = PARTS // 2

    def fill(low_a, high_a, low_b, high_b):
        for part in range(PARTS):
            source = (low_a if part < half else high_a).at[part % half]
            lanes = slice(part * LANES, (part + 1) * LANES)
            top = part // folds * channels
            left = part % folds * LANES
            map_ref[:, lanes] = source[:channels, :].astype(f32)
            hidden_ref[top : top + channels, left : left + LANES] = source[
                channels : 2 * channels, :
            ].astype(f32)
            small = source[2 * channels :, :].astype(f32)
            bias_ref[lanes] = small[0, :]
            side = slice(left, left + LANES)
            input_ref[part // folds, side] = small[1, :]
            if part < folds:
                input_ref[2, side] = small[2, :]
            else:
                out_ref[side] = small[2, :]
            source = (low_b if part < half else high_b).at[part % half]
            rows = source.shape[0]
            conv_ref[part * rows : (part + 1) * rows, :] = source[...].astype(f32)

    @pl.when(bit_ref[0] == 0)
    def _():
        fill(mine_a, theirs_a, mine_b, theirs_b)

    @pl.when(bit_ref[0] == 1)
    def _():
        fill(theirs_a, mine_a, theirs_b, mine_b)


def unpacked(bit, pair_a, pair_b, channels, hidden, width, conv_rows):
    f32 = jnp.float32
    vmem = pl.BlockSpec(memory_space=pltpu.VMEM)
    return pl.pallas_call(
        unpack_kernel,
        in_specs=[pl.BlockSpec(memory_space=pltpu.SMEM)] + [vmem] * 4,
        out_specs=[vmem] * 6,
        out_shape=[
            jax.ShapeDtypeStruct((conv_rows, channels), f32),
            jax.ShapeDtypeStruct((channels, width), f32),
            jax.ShapeDtypeStruct((width,), f32),
            jax.ShapeDtypeStruct((3, hidden), f32),
            jax.ShapeDtypeStruct((hidden, hidden), f32),
            jax.ShapeDtypeStruct((hidden,), f32),
        ],
        compiler_params=pltpu.CompilerParams(vmem_limit_bytes=32 * 1024 * 1024),
        name="unpack",
    )(bit.reshape(1), *pair_a, *pair_b)


def on_device(
    latents,
    conv_weight,
    map_weight,
    map_bias,
    input_weight,
    hidden_weight,
    output_weight,
    hit_owner,
    serve_block,
    query_grid,
    cotangent,
):
    lat_tile, lon_tile, channels = latents.shape
    lat_parts = lax.axis_size("lat")
    lon_parts = lax.axis_size("lon")
    dev_count = lat_parts * lon_parts
    lat_cells = lat_tile * lat_parts
    lon_cells = lon_tile * lon_parts
    block_rows = BLOCK
    lat_pos = lax.axis_index("lat")
    lon_pos = lax.axis_index("lon")
    padded = close_poles(padded_2(latents, (("lat", 0), ("lon", 1)), 1), lat_pos, lat_parts)
    features = conv_apply(padded, conv_weight, lat_tile, lon_tile, False).astype(jnp.bfloat16)
    serve_row = serve_block[0]
    hit_count = hit_owner.shape[0]
    group_size = cotangent.shape[0] // hit_count
    grid_groups = query_grid.reshape(3, hit_count, group_size).transpose(1, 0, 2)
    query_rows = jnp.concatenate(
        [
            grid_groups.astype(jnp.float32),
            cotangent.reshape(hit_count, 1, group_size),
        ],
        axis=1,
    ).reshape(hit_count, 4 * group_size)
    sent = jnp.zeros((dev_count, 4 * group_size), jnp.float32).at[hit_owner].set(query_rows)
    got = lax.all_to_all(sent, ("lat", "lon"), split_axis=0, concat_axis=0, tiled=True)
    got = got.reshape(dev_count, 4, group_size).transpose(1, 0, 2)
    block_cell = got[0].astype(jnp.int32)
    sub = got[1].astype(jnp.int32)
    tile_cell = jnp.where(
        serve_row[:, None] < 0, -1, serve_row[:, None] * block_rows + block_cell
    )
    queries = dev_count * group_size
    zero_row = jnp.zeros((dev_count, group_size), jnp.int32)
    coord_group = jnp.stack(
        [
            tile_cell // lon_tile,
            sub // SUB,
            tile_cell % lon_tile,
            sub % SUB,
            got[2].astype(jnp.int32),
            zero_row + 1,
            zero_row,
            zero_row,
        ]
    ).reshape(8, queries)
    coords = jnp.concatenate([coord_group] * 3 + [jnp.zeros_like(coord_group)], axis=0).astype(
        jnp.bfloat16
    )
    rows = jnp.concatenate(
        [tile_cell.astype(jnp.float32)[None], got[3][None]], axis=0
    ).reshape(2, queries)
    rows = jnp.pad(rows, ((0, 6), (0, 0)))
    lat_offset = (2 * SUB * lat_tile * lat_pos + 1).astype(jnp.float32) / (lat_cells * SUB) - 1.0
    lon_offset = (2 * SUB * lon_tile * lon_pos + 1).astype(jnp.float32) / (lon_cells * SUB) - 1.0
    level_offset = 1.0 / LEVELS - 1.0
    cuts = (
        2.0 / lat_cells,
        2.0 / (lat_cells * SUB),
        2.0 / lon_cells,
        2.0 / (lon_cells * SUB),
        2.0 / LEVELS,
        level_offset,
    )
    width = input_weight.shape[1]
    coord_weight = jnp.stack(
        [
            OMEGA * cuts[0] * input_weight[0],
            OMEGA * cuts[1] * input_weight[0],
            OMEGA * cuts[2] * input_weight[1],
            OMEGA * cuts[3] * input_weight[1],
            OMEGA * cuts[4] * input_weight[2],
            OMEGA
            * (
                lat_offset * input_weight[0]
                + lon_offset * input_weight[1]
                + level_offset * input_weight[2]
            )
            + map_bias[:width],
            jnp.zeros_like(input_weight[0]),
            jnp.zeros_like(input_weight[0]),
        ]
    )
    columns = jnp.concatenate(
        [
            jnp.broadcast_to(map_bias[None, width:], (LANES, width)),
            jnp.broadcast_to(output_weight[None, :], (LANES, width)),
        ],
        axis=0,
    )
    grad_scale = float(hit_count * group_size * dev_count) ** (-0.5)
    shares, tile_grads = query_pass(
        features,
        rows,
        coords,
        jnp.stack([lat_offset, lon_offset]),
        coord_weight,
        columns,
        map_weight,
        hidden_weight[0],
        cuts,
        grad_scale,
    )
    steps = [(axis, bit) for axis in ("lon", "lat") for bit in range(bits_of(axis))]
    split_a = steps[:3]
    split_b = [steps[0], steps[2], steps[1]]
    rest = steps[3:]
    shares = halved(shares, split_a[0])
    feature_grad = tile_grads.reshape(lat_tile, lon_tile, channels)
    conv_local = conv_weight_grad(padded, feature_grad, lat_tile, lon_tile)
    taps = conv_local.shape[0]
    conv_shares = (conv_local * grad_scale).astype(jnp.bfloat16)
    conv_shares = conv_shares.reshape(PARTS, taps * channels // PARTS, channels)
    conv_shares = halved(conv_shares, split_b[0])
    late_grad, shares, conv_shares = lax.optimization_barrier(
        (feature_grad, shares, conv_shares)
    )
    pair_a = gathered(reduced(shares, split_a[1:], rest), split_a)
    pair_b = gathered(reduced(conv_shares, split_b[1:], rest[::-1]), split_b)
    padded_grad = close_poles(
        padded_2(late_grad, (("lat", 0), ("lon", 1)), 1), lat_pos, lat_parts
    )
    latent_grad = conv_apply(padded_grad, conv_weight, lat_tile, lon_tile, True).reshape(
        lat_tile, lon_tile, channels
    )
    totals = unpacked(
        own_bit(steps[0]), pair_a, pair_b, channels, width, 2 * width, taps * channels
    )
    return (
        latent_grad,
        totals[0].reshape(taps, channels, channels),
        *totals[1:4],
        totals[4][None],
        totals[5],
    )


def solution(mesh):
    placed = (
        P("lat", "lon", None),
        P(),
        P(),
        P(),
        P(),
        P(),
        P(),
        P(("lat", "lon")),
        P(("lat", "lon"), None),
        P(None, ("lat", "lon")),
        P(("lat", "lon")),
    )
    return jax.shard_map(
        on_device,
        mesh=mesh,
        in_specs=placed,
        out_specs=(P("lat", "lon", None), P(), P(), P(), P(), P(), P()),
        check_vma=False,
    )
```

```python
import functools

import jax
import jax.numpy as jnp
from jax import lax
from jax.experimental import pallas as pl
from jax.experimental.pallas import tpu as pltpu
from jax.sharding import PartitionSpec as P

BLOCK = 128
LEVELS = 37
SUB = 6


OMEGA = 30.0
TILE = 512
PARTS = 8


def padded_2(block, sides, width):
    for axis, dim in sides:
        count = lax.axis_size(axis)
        forward = [(i, i + 1) for i in range(count - 1)]
        forward.append((count - 1, 0))
        backward = [(target, source) for source, target in forward]
        low = lax.ppermute(
            lax.slice_in_dim(block, block.shape[dim] - width, None, axis=dim), axis, forward
        )
        high = lax.ppermute(lax.slice_in_dim(block, 0, width, axis=dim), axis, backward)
        block = jnp.concatenate([low, block, high], axis=dim)
    return block


def conv_apply(padded, kernel, row_count, col_count, flipped):
    channels = padded.shape[-1]
    result = jnp.zeros((row_count * col_count, kernel.shape[-1]), jnp.float32)
    for shift_a in (-1, 0, 1):
        for shift_b in (-1, 0, 1):
            tap_index = (shift_a + 1) * 3 + shift_b + 1
            if flipped:
                window = padded[
                    1 - shift_a : 1 - shift_a + row_count, 1 - shift_b : 1 - shift_b + col_count
                ]
                matrix = kernel[tap_index].T
            else:
                window = padded[
                    1 + shift_a : 1 + shift_a + row_count, 1 + shift_b : 1 + shift_b + col_count
                ]
                matrix = kernel[tap_index]
            result = result + jnp.dot(
                window.reshape(row_count * col_count, channels),
                matrix,
                preferred_element_type=jnp.float32,
            )
    return result


def close_poles(padded, lat_pos, lat_parts):
    top_rim = jnp.where(lat_pos == 0, jnp.zeros_like(padded[:1]), padded[:1])
    bottom_rim = jnp.where(lat_pos == lat_parts - 1, jnp.zeros_like(padded[-1:]), padded[-1:])
    return jnp.concatenate([top_rim, padded[1:-1], bottom_rim], axis=0)


SIN_TERMS = (
    0.7071067781421408,
    -0.029462767114633488,
    0.0003682722504284759,
    -2.1886040931894034e-06,
    7.195418014521965e-09,
)
COS_TERMS = (
    1.4142134959273227,
    -0.17677635831469551,
    0.0036825740917005817,
    -3.061241565438332e-05,
    1.2789559619534725e-07,
)
TURN = 6.283185307179586
TURN_HIGH = 6.28125
TURN_LOW = TURN - TURN_HIGH
EXTRA = 16
COORD_ROWS = 32
CHUNK = 64
LANES = 128


def sin_cos(angle):
    turns = jnp.round(angle * (1.0 / TURN))
    rest = (angle - turns * TURN_HIGH) - turns * TURN_LOW
    square = rest * rest

    def series(terms):
        value = jnp.full_like(square, terms[-1])
        for term in terms[-2::-1]:
            value = value * square + term
        return value

    half_sin = rest * series(SIN_TERMS)
    half_cos = series(COS_TERMS)
    return half_sin * half_cos, 1.0 - half_sin * half_sin


def pack_kernel(owner_ref, grid_ref, cotan_ref, sent_ref):
    half = LANES // 2
    lower = lax.broadcasted_iota(jnp.int32, (1, LANES), 1) < half
    sent_ref[...] = jnp.zeros_like(sent_ref)
    for pair in range(owner_ref.shape[0] // 2):
        lanes = slice(pair * LANES, (pair + 1) * LANES)
        grid = grid_ref[:, lanes].astype(jnp.float32)
        values = [grid[0:1], grid[1:2], grid[2:3], cotan_ref[lanes].reshape(1, LANES)]
        turned = [pltpu.roll(value, half, 1) for value in values]
        sent_ref[owner_ref[2 * pair]] = jnp.concatenate(
            [
                jnp.where(lower, values[0], turned[1]),
                jnp.where(lower, values[2], turned[3]),
            ],
            axis=1,
        )
        sent_ref[owner_ref[2 * pair + 1]] = jnp.concatenate(
            [
                jnp.where(lower, turned[0], values[1]),
                jnp.where(lower, turned[2], values[3]),
            ],
            axis=1,
        )


def packed(hit_owner, query_grid, cotangent, slots, group_size):
    vmem = pl.BlockSpec(memory_space=pltpu.VMEM)
    return pl.pallas_call(
        pack_kernel,
        in_specs=[pl.BlockSpec(memory_space=pltpu.SMEM), vmem, vmem],
        out_specs=vmem,
        out_shape=jax.ShapeDtypeStruct((slots, 1, 4 * group_size), jnp.float32),
        name="pack",
    )(hit_owner, query_grid, cotangent)


def query_kernel(
    cuts,
    scale,
    taps,
    scalars_ref,
    serve_ref,
    got_ref,
    tile_ref,
    top_ref,
    bottom_ref,
    left_ref,
    right_ref,
    conv_ref,
    map_ref,
    bias_ref,
    input_ref,
    hidden_ref,
    output_ref,
    kept_ref,
    away_ref,
    conv_kept_ref,
    conv_away_ref,
    feature_grad_ref,
    windows,
    shifted,
    fields,
    feat_t,
    weight0,
    weight1,
    column_tiles,
    stack0,
    stack1,
    picks,
    pre,
    cos0,
    rounded0,
    rounded1,
    sums,
    hidden_sums,
    out_sums,
):
    step = pl.program_id(0)
    lat_tile, lon_tile, channels = tile_ref.shape
    cells = lat_tile * lon_tile
    hidden = hidden_ref.shape[0]
    block = rounded0.shape[1]
    f32, bf16 = jnp.float32, jnp.bfloat16
    lat_cell, lat_sub, lon_cell, lon_sub, level_cut, level_offset = cuts
    lat_pos, lat_last, lon_pos, bit = (scalars_ref[i] for i in range(4))
    lat_base = (2 * SUB * lat_tile * lat_pos + 1).astype(f32)
    lon_base = (2 * SUB * lon_tile * lon_pos + 1).astype(f32)
    lat_offset = lat_base * (0.5 * lat_sub) - 1.0
    lon_offset = lon_base * (0.5 * lon_sub) - 1.0

    @pl.when(step == 0)
    def _():
        flat = jnp.concatenate(
            [top_ref[0], tile_ref[...].reshape(cells, channels), bottom_ref[0]], axis=0
        )
        first = jnp.where(lat_pos == 0, 0.0, 1.0)
        last = jnp.where(lat_last == 0, 1.0, 0.0)
        ends = cells + lon_tile

        def keep(slot, values):
            windows[slot, :lon_tile, :] = (values[:lon_tile] * first).astype(bf16)
            windows[slot, lon_tile:ends, :] = values[lon_tile:ends].astype(bf16)
            windows[slot, ends:, :] = (values[ends:] * last).astype(bf16)

        flat = flat.astype(f32)
        total_rows = flat.shape[0]
        keep(1, flat)
        left = left_ref[...].astype(f32)
        right = right_ref[...].astype(f32)
        shifted[...] = pltpu.roll(flat, 1, 0)
        for row in range(lat_tile + 2):
            shifted[row * lon_tile : row * lon_tile + 1, :] = left[row : row + 1]
        keep(0, shifted[...])
        shifted[...] = pltpu.roll(flat, total_rows - 1, 0)
        for row in range(1, lat_tile + 3):
            shifted[row * lon_tile - 1 : row * lon_tile, :] = right[row - 1 : row]
        keep(2, shifted[...])
        features = jnp.zeros((cells, channels), f32)
        for tap in range(taps):
            top = tap // 3 * lon_tile
            features = features + jnp.dot(
                windows[tap % 3, top : top + cells, :], conv_ref[tap], preferred_element_type=f32
            )
        feat_t[...] = features.T.astype(bf16)

        half = LANES // 2
        lower = lax.broadcasted_iota(jnp.int32, (1, LANES), 1) < half
        for pair in range(got_ref.shape[0] // 2):
            even, odd = got_ref[2 * pair], got_ref[2 * pair + 1]
            row = slice(pair, pair + 1)
            for place in range(2):
                lanes = slice(place * LANES, (place + 1) * LANES)
                near, far = even[:, lanes], odd[:, lanes]
                fields[2 * place, row, :] = jnp.where(lower, near, pltpu.roll(far, half, 1))
                fields[2 * place + 1, row, :] = jnp.where(lower, pltpu.roll(near, half, 1), far)
            serve = jnp.where(lower, serve_ref[0, 2 * pair], serve_ref[0, 2 * pair + 1])
            fields[4, row, :] = serve.astype(f32)
        serve = fields[4]
        tile_cell = jnp.where(serve < 0.0, -1.0, serve * float(BLOCK) + fields[0])
        cell_row = jnp.floor((tile_cell + 0.5) * (1.0 / lon_tile))
        sub = fields[1]
        sub_row = jnp.floor((sub + 0.5) * (1.0 / SUB))
        fields[0] = tile_cell
        fields[1] = cell_row
        fields[4] = sub_row
        fields[5] = tile_cell - cell_row * float(lon_tile)
        fields[6] = sub - sub_row * float(SUB)

        weight0[:, :channels] = map_ref[:, :hidden].T
        bias = bias_ref[...].reshape(1, 2 * hidden)
        lat_weight = OMEGA * input_ref[0:1, :]
        lon_weight = OMEGA * input_ref[1:2, :]
        level_weight = OMEGA * input_ref[2:3, :]
        constant = (
            lat_offset * lat_weight
            + lon_offset * lon_weight
            + level_offset * level_weight
            + bias[:, :hidden]
        )
        zero = jnp.zeros_like(constant)
        coef = jnp.concatenate(
            [
                lat_cell * lat_weight,
                lat_sub * lat_weight,
                lon_cell * lon_weight,
                lon_sub * lon_weight,
                level_cut * level_weight,
                constant,
                zero,
                zero,
            ],
            axis=0,
        )
        high = coef.astype(bf16).astype(f32)
        mid = (coef - high).astype(bf16).astype(f32)
        low = coef - high - mid
        parts = jnp.concatenate([high, mid, low, jnp.zeros((LANES - 24, hidden), f32)], axis=0)
        weight0[:, channels:] = parts.T.astype(bf16)
        weight1[:, :hidden] = hidden_ref[...].T
        weight1[:, hidden:] = map_ref[:, hidden:].T
        column_tiles[:, :LANES] = jnp.broadcast_to(bias[:, hidden:], (LANES, hidden)).T
        column_tiles[:, LANES:] = jnp.broadcast_to(
            output_ref[...].reshape(1, hidden), (LANES, hidden)
        ).T
        stack0[...] = jnp.zeros_like(stack0)
        sums[...] = jnp.zeros_like(sums)
        hidden_sums[...] = jnp.zeros_like(hidden_sums)
        out_sums[...] = jnp.zeros_like(out_sums)

    ids = lax.broadcasted_iota(jnp.int32, (cells, LANES), 0)
    strips = block // LANES
    for strip in range(strips):
        row = pl.ds(step * strips + strip, 1)
        lanes = slice(strip * LANES, (strip + 1) * LANES)
        cell = fields[0, row, :].astype(jnp.int32)
        picks[:cells, lanes] = jnp.where(ids == cell, 1.0, 0.0).astype(bf16)
        one = jnp.ones((1, LANES), f32)
        group = jnp.concatenate(
            [
                fields[1, row, :],
                fields[4, row, :],
                fields[5, row, :],
                fields[6, row, :],
                fields[2, row, :],
                one,
                jnp.zeros((2, LANES), f32),
            ],
            axis=0,
        )
        coords = jnp.concatenate([group, group, group, jnp.zeros_like(group)], axis=0).astype(
            bf16
        )
        stack0[channels : channels + COORD_ROWS, lanes] = coords
        picks[cells:, lanes] = coords[:EXTRA]
    queried = jnp.dot(feat_t[...], picks[:cells, :], preferred_element_type=f32).astype(bf16)
    stack0[:channels, :] = queried
    stack1[hidden:, :] = queried
    pre[...] = jnp.dot(weight0[...], stack0[...], preferred_element_type=f32)
    for top in range(0, hidden, CHUNK):
        for left in range(0, block, LANES):
            at = (slice(top, top + CHUNK), slice(left, left + LANES))
            sine, cosine = sin_cos(pre[at])
            stack1[at] = sine.astype(bf16)
            cos0[at] = cosine
    pre[...] = jnp.dot(weight1[...], stack1[...], preferred_element_type=f32)
    for top in range(0, hidden, CHUNK):
        rows = slice(top, top + CHUNK)
        bias = column_tiles[rows, :LANES]
        out_weight = column_tiles[rows, LANES:]
        total = out_sums[rows, :]
        for strip in range(strips):
            at = (rows, slice(strip * LANES, (strip + 1) * LANES))
            cotan = fields[3, pl.ds(step * strips + strip, 1), :]
            sine, cosine = sin_cos(pre[at] + bias)
            total = total + sine * cotan
            rounded1[at] = (out_weight * cotan * cosine).astype(bf16)
        out_sums[rows, :] = total
    act_grad = jnp.dot(hidden_ref[...], rounded1[...], preferred_element_type=f32)
    rounded0[...] = (act_grad * cos0[...]).astype(bf16)
    across = (((1,), (1,)), ((), ()))
    sums[:, hidden:] += lax.dot_general(
        picks[...], rounded1[...], across, preferred_element_type=f32
    )
    hidden_sums[...] += lax.dot_general(
        stack1[:hidden, :], rounded1[...], across, preferred_element_type=f32
    )
    sums[:, :hidden] += lax.dot_general(
        picks[...], rounded0[...], across, preferred_element_type=f32
    )

    @pl.when(step == pl.num_programs(0) - 1)
    def _():
        cell_sums = sums[:cells, :]
        upper = cell_sums.astype(bf16)
        lower = (cell_sums - upper.astype(f32)).astype(bf16)
        map_grad = (
            jnp.dot(feat_t[...], upper, preferred_element_type=f32)
            + jnp.dot(feat_t[...], lower, preferred_element_type=f32)
        ) * scale
        feature_grad = (
            lax.dot_general(upper, map_ref[...], across, preferred_element_type=f32)
            + lax.dot_general(lower, map_ref[...], across, preferred_element_type=f32)
        ).astype(bf16)
        feature_grad_ref[...] = feature_grad
        hidden_grad = hidden_sums[...] * scale
        extra = sums[cells : cells + 8, :]
        total = extra[5:6, :hidden]
        lat_grad = (
            lat_cell * extra[0:1, :hidden] + lat_sub * extra[1:2, :hidden] + lat_offset * total
        )
        lon_grad = (
            lon_cell * extra[2:3, :hidden] + lon_sub * extra[3:4, :hidden] + lon_offset * total
        )
        level_grad = level_cut * extra[4:5, :hidden] + level_offset * total
        out_grad = jnp.sum(out_sums[...].T, axis=0, keepdims=True)
        gain = OMEGA * scale
        small = jnp.concatenate(
            [
                extra[5:6, :] * scale,
                jnp.concatenate([lat_grad, lon_grad], axis=1) * gain,
                jnp.concatenate([level_grad * gain, out_grad * scale], axis=1),
                jnp.zeros((EXTRA - 3, 2 * hidden), f32),
            ],
            axis=0,
        )
        folds = hidden // LANES

        def share(part):
            lanes = slice(part * LANES, (part + 1) * LANES)
            top = part // folds * channels
            left = part % folds * LANES
            return (
                map_grad[:, lanes],
                hidden_grad[top : top + channels, left : left + LANES],
                small[:, lanes],
            )

        half = PARTS // 2
        places = (
            slice(0, channels),
            slice(channels, 2 * channels),
            slice(2 * channels, 2 * channels + EXTRA),
        )
        for part in range(half):
            for place, low, high in zip(places, share(part), share(part + half)):
                kept_ref[part, place, :] = jnp.where(bit == 0, low, high).astype(bf16)
                away_ref[part, place, :] = jnp.where(bit == 0, high, low).astype(bf16)

        rows = taps * channels // PARTS
        pieces = {}
        for tap in range(taps):
            top = tap // 3 * lon_tile
            grad = lax.dot_general(
                windows[tap % 3, top : top + cells, :],
                feature_grad,
                (((0,), (0,)), ((), ())),
                preferred_element_type=f32,
            )
            grad = (grad * scale).astype(bf16)
            start = tap * channels
            while start < (tap + 1) * channels:
                end = min((start // rows + 1) * rows, (tap + 1) * channels)
                inside = slice(start % rows, start % rows + end - start)
                value = grad[start - tap * channels : end - tap * channels]
                part = start // rows

                @pl.when(bit == part // half)
                def _():
                    conv_kept_ref[part % half, inside, :] = value

                @pl.when(bit != part // half)
                def _():
                    conv_away_ref[part % half, inside, :] = value

                start = end


def query_pass(
    scalars,
    serve_block,
    got,
    latents,
    rims,
    conv_weight,
    map_weight,
    map_bias,
    input_weight,
    hidden_weight,
    output_weight,
    cuts,
    scale,
):
    lat_tile, lon_tile, channels = latents.shape
    cells = lat_tile * lon_tile
    taps = conv_weight.shape[0]
    slots = got.shape[0]
    queries = slots * got.shape[2] // 4
    hidden = hidden_weight.shape[0]
    width = map_weight.shape[1]
    block = min(TILE, queries)
    f32, bf16 = jnp.float32, jnp.bfloat16
    smem = pl.BlockSpec(memory_space=pltpu.SMEM)
    vmem = pl.BlockSpec(memory_space=pltpu.VMEM)
    share = (PARTS // 2, 2 * channels + EXTRA, LANES)
    conv_share = (PARTS // 2, taps * channels // PARTS, channels)

    return pl.pallas_call(
        functools.partial(query_kernel, cuts, scale, taps),
        grid=(queries // block,),
        in_specs=[smem, smem] + [vmem] * 12,
        out_specs=[vmem] * 5,
        out_shape=[
            jax.ShapeDtypeStruct(share, bf16),
            jax.ShapeDtypeStruct(share, bf16),
            jax.ShapeDtypeStruct(conv_share, bf16),
            jax.ShapeDtypeStruct(conv_share, bf16),
            jax.ShapeDtypeStruct((cells, channels), bf16),
        ],
        scratch_shapes=[
            pltpu.VMEM((3, cells + 2 * lon_tile, channels), bf16),
            pltpu.VMEM((cells + 2 * lon_tile, channels), f32),
            pltpu.VMEM((7, slots // 2, LANES), f32),
            pltpu.VMEM((channels, cells), bf16),
            pltpu.VMEM((hidden, channels + LANES), bf16),
            pltpu.VMEM((hidden, hidden + channels), bf16),
            pltpu.VMEM((hidden, 2 * LANES), f32),
            pltpu.VMEM((channels + LANES, block), bf16),
            pltpu.VMEM((hidden + channels, block), bf16),
            pltpu.VMEM((cells + EXTRA, block), bf16),
            pltpu.VMEM((hidden, block), f32),
            pltpu.VMEM((hidden, block), f32),
            pltpu.VMEM((hidden, block), bf16),
            pltpu.VMEM((hidden, block), bf16),
            pltpu.VMEM((cells + EXTRA, width), f32),
            pltpu.VMEM((hidden, hidden), f32),
            pltpu.VMEM((hidden, LANES), f32),
        ],
        compiler_params=pltpu.CompilerParams(vmem_limit_bytes=48 * 1024 * 1024),
        name="queries",
    )(
        scalars,
        serve_block,
        got,
        latents,
        *rims,
        conv_weight,
        map_weight,
        map_bias,
        input_weight,
        hidden_weight,
        output_weight,
    )


def bits_of(axis):
    return lax.axis_size(axis).bit_length() - 1


def flip(values, step):
    axis, bit = step
    count = lax.axis_size(axis)
    return lax.ppermute(values, axis, [(i, i ^ (1 << bit)) for i in range(count)])


def own_bit(step):
    axis, bit = step
    return (lax.axis_index(axis) >> bit) & 1


def added(left, right):
    return (left.astype(jnp.float32) + right.astype(jnp.float32)).astype(left.dtype)


def halved(values, step):
    halves = values.reshape((2, values.shape[0] // 2) + values.shape[1:])
    mine = own_bit(step)
    away = lax.dynamic_index_in_dim(halves, 1 - mine, 0, keepdims=False)
    kept = lax.dynamic_index_in_dim(halves, mine, 0, keepdims=False)
    return added(kept, flip(away, step))


def ring(axis, turn):
    count = lax.axis_size(axis)
    return [(i, (i + turn) % count) for i in range(count)]


def rims_of(tile):
    top = lax.ppermute(tile[-1:], "lat", ring("lat", 1))
    bottom = lax.ppermute(tile[:1], "lat", ring("lat", -1))
    last = jnp.concatenate([top[:, -1], tile[:, -1], bottom[:, -1]], axis=0)
    first = jnp.concatenate([top[:, 0], tile[:, 0], bottom[:, 0]], axis=0)
    left = lax.ppermute(last, "lon", ring("lon", 1))
    right = lax.ppermute(first, "lon", ring("lon", -1))
    return (top, bottom, left, right)


def reduced(values, split_steps, plain_steps):
    for step in split_steps:
        values = halved(values, step)
    for step in plain_steps:
        values = added(values, flip(values, step))
    return values


def joined(mine, theirs, step):
    first = own_bit(step) == 0
    return jnp.concatenate(
        [jnp.where(first, mine, theirs), jnp.where(first, theirs, mine)], axis=0
    )


def gathered(values, split_steps):
    for step in split_steps[:0:-1]:
        values = joined(values, flip(values, step), step)
    return values, flip(values, split_steps[0])


def unpack_kernel(
    bit_ref,
    mine_a,
    theirs_a,
    mine_b,
    theirs_b,
    conv_ref,
    map_ref,
    bias_ref,
    input_ref,
    hidden_ref,
    out_ref,
):
    f32 = jnp.float32
    channels = map_ref.shape[0]
    folds = hidden_ref.shape[1] // LANES
    half = PARTS // 2

    def fill(low_a, high_a, low_b, high_b):
        for part in range(PARTS):
            source = (low_a if part < half else high_a).at[part % half]
            lanes = slice(part * LANES, (part + 1) * LANES)
            top = part // folds * channels
            left = part % folds * LANES
            map_ref[:, lanes] = source[:channels, :].astype(f32)
            hidden_ref[top : top + channels, left : left + LANES] = source[
                channels : 2 * channels, :
            ].astype(f32)
            small = source[2 * channels :, :].astype(f32)
            bias_ref[lanes] = small[0, :]
            side = slice(left, left + LANES)
            input_ref[part // folds, side] = small[1, :]
            if part < folds:
                input_ref[2, side] = small[2, :]
            else:
                out_ref[side] = small[2, :]
            source = (low_b if part < half else high_b).at[part % half]
            rows = source.shape[0]
            conv_ref[part * rows : (part + 1) * rows, :] = source[...].astype(f32)

    @pl.when(bit_ref[0] == 0)
    def _():
        fill(mine_a, theirs_a, mine_b, theirs_b)

    @pl.when(bit_ref[0] == 1)
    def _():
        fill(theirs_a, mine_a, theirs_b, mine_b)


def unpacked(bit, pair_a, pair_b, channels, hidden, width, conv_rows):
    f32 = jnp.float32
    vmem = pl.BlockSpec(memory_space=pltpu.VMEM)
    return pl.pallas_call(
        unpack_kernel,
        in_specs=[pl.BlockSpec(memory_space=pltpu.SMEM)] + [vmem] * 4,
        out_specs=[vmem] * 6,
        out_shape=[
            jax.ShapeDtypeStruct((conv_rows, channels), f32),
            jax.ShapeDtypeStruct((channels, width), f32),
            jax.ShapeDtypeStruct((width,), f32),
            jax.ShapeDtypeStruct((3, hidden), f32),
            jax.ShapeDtypeStruct((hidden, hidden), f32),
            jax.ShapeDtypeStruct((hidden,), f32),
        ],
        compiler_params=pltpu.CompilerParams(vmem_limit_bytes=32 * 1024 * 1024),
        name="unpack",
    )(bit.reshape(1), *pair_a, *pair_b)


def on_device(
    latents,
    conv_weight,
    map_weight,
    map_bias,
    input_weight,
    hidden_weight,
    output_weight,
    hit_owner,
    serve_block,
    query_grid,
    cotangent,
):
    lat_tile, lon_tile, channels = latents.shape
    lat_parts = lax.axis_size("lat")
    lon_parts = lax.axis_size("lon")
    dev_count = lat_parts * lon_parts
    lat_cells = lat_tile * lat_parts
    lon_cells = lon_tile * lon_parts
    lat_pos = lax.axis_index("lat")
    lon_pos = lax.axis_index("lon")
    hit_count = hit_owner.shape[0]
    group_size = cotangent.shape[0] // hit_count
    width = input_weight.shape[1]
    sent = packed(hit_owner, query_grid, cotangent, dev_count, group_size)
    got = lax.all_to_all(sent, ("lat", "lon"), split_axis=0, concat_axis=0, tiled=True)
    rims = rims_of(latents)
    cuts = (
        2.0 / lat_cells,
        2.0 / (lat_cells * SUB),
        2.0 / lon_cells,
        2.0 / (lon_cells * SUB),
        2.0 / LEVELS,
        1.0 / LEVELS - 1.0,
    )
    grad_scale = float(hit_count * group_size * dev_count) ** (-0.5)
    steps = [(axis, bit) for axis in ("lon", "lat") for bit in range(bits_of(axis))]
    split_a = steps[:3]
    split_b = [steps[0], steps[2], steps[1]]
    rest = steps[3:]
    scalars = jnp.stack(
        [lat_pos, (lat_pos == lat_parts - 1).astype(jnp.int32), lon_pos, own_bit(steps[0])]
    )
    kept, away, conv_kept, conv_away, tile_grads = query_pass(
        scalars,
        serve_block,
        got,
        latents,
        rims,
        conv_weight,
        map_weight,
        map_bias,
        input_weight,
        hidden_weight[0],
        output_weight,
        cuts,
        grad_scale,
    )
    shares = added(kept, flip(away, steps[0]))
    conv_shares = added(conv_kept, flip(conv_away, steps[0]))
    taps = conv_weight.shape[0]
    feature_grad = tile_grads.reshape(lat_tile, lon_tile, channels)
    shares = halved(shares, split_a[1])
    conv_shares = halved(conv_shares, split_b[1])
    shares = halved(shares, split_a[2])
    conv_shares = halved(conv_shares, split_b[2])
    shares = added(shares, flip(shares, rest[0]))
    late_grad, shares = lax.optimization_barrier((feature_grad, shares))
    pair_a = gathered(reduced(shares, [], rest[1:]), split_a)
    pair_b = gathered(reduced(conv_shares, [], rest[::-1]), split_b)
    padded_grad = close_poles(
        padded_2(late_grad, (("lat", 0), ("lon", 1)), 1), lat_pos, lat_parts
    )
    latent_grad = conv_apply(padded_grad, conv_weight, lat_tile, lon_tile, True).reshape(
        lat_tile, lon_tile, channels
    )
    totals = unpacked(
        own_bit(steps[0]), pair_a, pair_b, channels, width, 2 * width, taps * channels
    )
    return (
        latent_grad,
        totals[0].reshape(taps, channels, channels),
        *totals[1:4],
        totals[4][None],
        totals[5],
    )


def solution(mesh):
    placed = (
        P("lat", "lon", None),
        P(),
        P(),
        P(),
        P(),
        P(),
        P(),
        P(("lat", "lon")),
        P(("lat", "lon"), None),
        P(None, ("lat", "lon")),
        P(("lat", "lon")),
    )
    return jax.shard_map(
        on_device,
        mesh=mesh,
        in_specs=placed,
        out_specs=(P("lat", "lon", None), P(), P(), P(), P(), P(), P()),
        check_vma=False,
    )
```

```python
import functools

import jax
import jax.numpy as jnp
from jax import lax
from jax.experimental import pallas as pl
from jax.experimental.pallas import tpu as pltpu
from jax.sharding import PartitionSpec as P

BLOCK = 128
LEVELS = 37
SUB = 6


OMEGA = 30.0
TILE = 512
PARTS = 8


def conv_apply(padded, kernel, row_count, col_count, flipped):
    channels = padded.shape[-1]
    result = jnp.zeros((row_count * col_count, kernel.shape[-1]), jnp.float32)
    for shift_a in (-1, 0, 1):
        for shift_b in (-1, 0, 1):
            tap_index = (shift_a + 1) * 3 + shift_b + 1
            if flipped:
                window = padded[
                    1 - shift_a : 1 - shift_a + row_count, 1 - shift_b : 1 - shift_b + col_count
                ]
                matrix = kernel[tap_index].T
            else:
                window = padded[
                    1 + shift_a : 1 + shift_a + row_count, 1 + shift_b : 1 + shift_b + col_count
                ]
                matrix = kernel[tap_index]
            result = result + jnp.dot(
                window.reshape(row_count * col_count, channels),
                matrix,
                preferred_element_type=jnp.float32,
            )
    return result


def close_poles(padded, lat_pos, lat_parts):
    top_rim = jnp.where(lat_pos == 0, jnp.zeros_like(padded[:1]), padded[:1])
    bottom_rim = jnp.where(lat_pos == lat_parts - 1, jnp.zeros_like(padded[-1:]), padded[-1:])
    return jnp.concatenate([top_rim, padded[1:-1], bottom_rim], axis=0)


SIN_TERMS = (
    0.7071067781421408,
    -0.029462767114633488,
    0.0003682722504284759,
    -2.1886040931894034e-06,
    7.195418014521965e-09,
)
COS_TERMS = (
    1.4142134959273227,
    -0.17677635831469551,
    0.0036825740917005817,
    -3.061241565438332e-05,
    1.2789559619534725e-07,
)
TURN = 6.283185307179586
TURN_HIGH = 6.28125
TURN_LOW = TURN - TURN_HIGH
EXTRA = 16
COORD_ROWS = 32
CHUNK = 64
LANES = 128


def sin_cos(angle):
    turns = jnp.round(angle * (1.0 / TURN))
    rest = (angle - turns * TURN_HIGH) - turns * TURN_LOW
    square = rest * rest

    def series(terms):
        value = jnp.full_like(square, terms[-1])
        for term in terms[-2::-1]:
            value = value * square + term
        return value

    half_sin = rest * series(SIN_TERMS)
    half_cos = series(COS_TERMS)
    return half_sin * half_cos, 1.0 - half_sin * half_sin


def pack_kernel(owner_ref, grid_ref, cotan_ref, sent_ref):
    half = LANES // 2
    lower = lax.broadcasted_iota(jnp.int32, (1, LANES), 1) < half
    sent_ref[...] = jnp.zeros_like(sent_ref)
    for pair in range(owner_ref.shape[0] // 2):
        lanes = slice(pair * LANES, (pair + 1) * LANES)
        grid = grid_ref[:, lanes].astype(jnp.float32)
        values = [grid[0:1], grid[1:2], grid[2:3], cotan_ref[lanes].reshape(1, LANES)]
        turned = [pltpu.roll(value, half, 1) for value in values]
        sent_ref[owner_ref[2 * pair]] = jnp.concatenate(
            [
                jnp.where(lower, values[0], turned[1]),
                jnp.where(lower, values[2], turned[3]),
            ],
            axis=1,
        )
        sent_ref[owner_ref[2 * pair + 1]] = jnp.concatenate(
            [
                jnp.where(lower, turned[0], values[1]),
                jnp.where(lower, turned[2], values[3]),
            ],
            axis=1,
        )


def packed(hit_owner, query_grid, cotangent, slots, group_size):
    vmem = pl.BlockSpec(memory_space=pltpu.VMEM)
    return pl.pallas_call(
        pack_kernel,
        in_specs=[pl.BlockSpec(memory_space=pltpu.SMEM), vmem, vmem],
        out_specs=vmem,
        out_shape=jax.ShapeDtypeStruct((slots, 1, 4 * group_size), jnp.float32),
        name="pack",
    )(hit_owner, query_grid, cotangent)


def fetched(sources, targets, sems):
    copies = [
        pltpu.make_async_copy(source, target, sems.at[index])
        for index, (source, target) in enumerate(zip(sources, targets))
    ]
    for copy in copies:
        copy.start()
    return copies


def weights_kernel(cuts, tile_shape, *refs):
    sources, (weight0, weight1, column_tiles), (*targets, sems) = refs[:5], refs[5:8], refs[8:]
    map_ref, bias_ref, input_ref, hidden_ref, output_ref = targets
    for copy in fetched(sources, targets, sems):
        copy.wait()
    channels = map_ref.shape[0]
    hidden = hidden_ref.shape[0]
    f32, bf16 = jnp.float32, jnp.bfloat16
    lat_cell, lat_sub, lon_cell, lon_sub, level_cut, level_offset = cuts
    lat_offset, lon_offset = tile_offsets(tile_shape, cuts)
    weight0[:, :channels] = map_ref[:, :hidden].T
    bias = bias_ref[...].reshape(1, 2 * hidden)
    lat_weight = OMEGA * input_ref[0:1, :]
    lon_weight = OMEGA * input_ref[1:2, :]
    level_weight = OMEGA * input_ref[2:3, :]
    constant = (
        lat_offset * lat_weight
        + lon_offset * lon_weight
        + level_offset * level_weight
        + bias[:, :hidden]
    )
    zero = jnp.zeros_like(constant)
    coef = jnp.concatenate(
        [
            lat_cell * lat_weight,
            lat_sub * lat_weight,
            lon_cell * lon_weight,
            lon_sub * lon_weight,
            level_cut * level_weight,
            constant,
            zero,
            zero,
        ],
        axis=0,
    )
    high = coef.astype(bf16).astype(f32)
    mid = (coef - high).astype(bf16).astype(f32)
    low = coef - high - mid
    parts = jnp.concatenate([high, mid, low, jnp.zeros((LANES - 24, hidden), f32)], axis=0)
    weight0[:, channels:] = parts.T.astype(bf16)
    weight1[:, :hidden] = hidden_ref[...].T
    weight1[:, hidden:] = map_ref[:, hidden:].T
    column_tiles[:, :LANES] = jnp.broadcast_to(bias[:, hidden:], (LANES, hidden)).T
    column_tiles[:, LANES:] = jnp.broadcast_to(
        output_ref[...].reshape(1, hidden), (LANES, hidden)
    ).T


def tile_offsets(tile_shape, cuts):
    lat_step, lon_step = cuts[1], cuts[3]
    lat_base = 2 * SUB * tile_shape[0] * lax.axis_index("lat") + 1
    lon_base = 2 * SUB * tile_shape[1] * lax.axis_index("lon") + 1
    return (
        lat_base.astype(jnp.float32) * (0.5 * lat_step) - 1.0,
        lon_base.astype(jnp.float32) * (0.5 * lon_step) - 1.0,
    )


def prepared_weights(
    tile_shape, map_weight, map_bias, input_weight, hidden_weight, output_weight, cuts
):
    channels = map_weight.shape[0]
    hidden = hidden_weight.shape[0]
    sources = (map_weight, map_bias, input_weight, hidden_weight, output_weight)
    vmem = pl.BlockSpec(memory_space=pltpu.VMEM)
    return pl.pallas_call(
        functools.partial(weights_kernel, cuts, tile_shape),
        in_specs=[pl.BlockSpec(memory_space=pltpu.HBM)] * 5,
        out_specs=[vmem] * 3,
        out_shape=[
            jax.ShapeDtypeStruct((hidden, channels + LANES), jnp.bfloat16),
            jax.ShapeDtypeStruct((hidden, hidden + channels), jnp.bfloat16),
            jax.ShapeDtypeStruct((hidden, 2 * LANES), jnp.float32),
        ],
        scratch_shapes=[pltpu.VMEM(value.shape, value.dtype) for value in sources]
        + [pltpu.SemaphoreType.DMA((5,))],

        name="weights",
    )(*sources)


def query_kernel(
    cuts,
    scale,
    taps,
    serve_hbm,
    got_ref,
    tile_hbm,
    top_ref,
    bottom_ref,
    left_ref,
    right_ref,
    conv_hbm,
    map_hbm,
    hidden_hbm,
    weight0_hbm,
    weight1_hbm,
    columns_hbm,
    kept_ref,
    away_ref,
    conv_kept_ref,
    conv_away_ref,
    feature_grad_ref,
    serve_ref,
    tile_ref,
    conv_ref,
    map_ref,
    hidden_ref,
    weight0,
    weight1,
    column_tiles,
    sems,
    windows,
    shifted,
    fields,
    feat_t,
    stack0,
    stack1,
    picks,
    pre,
    cos0,
    rounded0,
    rounded1,
    sums,
    hidden_sums,
    out_sums,
):
    step = pl.program_id(0)
    lat_tile, lon_tile, channels = tile_ref.shape
    cells = lat_tile * lon_tile
    hidden = hidden_ref.shape[0]
    block = rounded0.shape[1]
    f32, bf16 = jnp.float32, jnp.bfloat16
    lat_cell, lat_sub, lon_cell, lon_sub, level_cut, level_offset = cuts
    lat_pos = lax.axis_index("lat")
    bit = lax.axis_index("lon") & 1
    lat_offset, lon_offset = tile_offsets((lat_tile, lon_tile), cuts)

    @pl.when(step == 0)
    def _():
        copies = fetched(
            (
                tile_hbm,
                serve_hbm,
                conv_hbm,
                weight0_hbm,
                weight1_hbm,
                columns_hbm,
                hidden_hbm,
                map_hbm,
            ),
            (
                tile_ref,
                serve_ref,
                conv_ref,
                weight0,
                weight1,
                column_tiles,
                hidden_ref,
                map_ref,
            ),
            sems,
        )
        copies[0].wait()
        copies[1].wait()
        flat = jnp.concatenate(
            [top_ref[0], tile_ref[...].reshape(cells, channels), bottom_ref[0]], axis=0
        )
        first = jnp.where(lat_pos == 0, 0.0, 1.0)
        last = jnp.where(lat_pos == lax.axis_size("lat") - 1, 0.0, 1.0)
        ends = cells + lon_tile

        def keep(slot, values):
            windows[slot, :lon_tile, :] = (values[:lon_tile] * first).astype(bf16)
            windows[slot, lon_tile:ends, :] = values[lon_tile:ends].astype(bf16)
            windows[slot, ends:, :] = (values[ends:] * last).astype(bf16)

        flat = flat.astype(f32)
        total_rows = flat.shape[0]
        keep(1, flat)
        left = left_ref[...].astype(f32)
        right = right_ref[...].astype(f32)
        shifted[...] = pltpu.roll(flat, 1, 0)
        for row in range(lat_tile + 2):
            shifted[row * lon_tile : row * lon_tile + 1, :] = left[row : row + 1]
        keep(0, shifted[...])
        shifted[...] = pltpu.roll(flat, total_rows - 1, 0)
        for row in range(1, lat_tile + 3):
            shifted[row * lon_tile - 1 : row * lon_tile, :] = right[row - 1 : row]
        keep(2, shifted[...])
        copies[2].wait()
        features = jnp.zeros((cells, channels), f32)
        for tap in range(taps):
            top = tap // 3 * lon_tile
            features = features + jnp.dot(
                windows[tap % 3, top : top + cells, :], conv_ref[tap], preferred_element_type=f32
            )
        feat_t[...] = features.T.astype(bf16)

        half = LANES // 2
        lower = lax.broadcasted_iota(jnp.int32, (1, LANES), 1) < half
        for pair in range(got_ref.shape[0] // 2):
            even, odd = got_ref[2 * pair], got_ref[2 * pair + 1]
            row = slice(pair, pair + 1)
            for place in range(2):
                lanes = slice(place * LANES, (place + 1) * LANES)
                near, far = even[:, lanes], odd[:, lanes]
                fields[2 * place, row, :] = jnp.where(lower, near, pltpu.roll(far, half, 1))
                fields[2 * place + 1, row, :] = jnp.where(lower, pltpu.roll(near, half, 1), far)
            serve = jnp.where(lower, serve_ref[0, 2 * pair], serve_ref[0, 2 * pair + 1])
            fields[4, row, :] = serve.astype(f32)
        serve = fields[4]
        tile_cell = jnp.where(serve < 0.0, -1.0, serve * float(BLOCK) + fields[0])
        cell_row = jnp.floor((tile_cell + 0.5) * (1.0 / lon_tile))
        sub = fields[1]
        sub_row = jnp.floor((sub + 0.5) * (1.0 / SUB))
        fields[0] = tile_cell
        fields[1] = cell_row
        fields[4] = sub_row
        fields[5] = tile_cell - cell_row * float(lon_tile)
        fields[6] = sub - sub_row * float(SUB)

        for copy in copies[3:]:
            copy.wait()
        stack0[...] = jnp.zeros_like(stack0)
        sums[...] = jnp.zeros_like(sums)
        hidden_sums[...] = jnp.zeros_like(hidden_sums)
        out_sums[...] = jnp.zeros_like(out_sums)

    ids = lax.broadcasted_iota(jnp.int32, (cells, LANES), 0)
    strips = block // LANES
    for strip in range(strips):
        row = pl.ds(step * strips + strip, 1)
        lanes = slice(strip * LANES, (strip + 1) * LANES)
        cell = fields[0, row, :].astype(jnp.int32)
        picks[:cells, lanes] = jnp.where(ids == cell, 1.0, 0.0).astype(bf16)
        one = jnp.ones((1, LANES), f32)
        group = jnp.concatenate(
            [
                fields[1, row, :],
                fields[4, row, :],
                fields[5, row, :],
                fields[6, row, :],
                fields[2, row, :],
                one,
                jnp.zeros((2, LANES), f32),
            ],
            axis=0,
        )
        coords = jnp.concatenate([group, group, group, jnp.zeros_like(group)], axis=0).astype(
            bf16
        )
        stack0[channels : channels + COORD_ROWS, lanes] = coords
        picks[cells:, lanes] = coords[:EXTRA]
    queried = jnp.dot(feat_t[...], picks[:cells, :], preferred_element_type=f32).astype(bf16)
    stack0[:channels, :] = queried
    stack1[hidden:, :] = queried
    pre[...] = jnp.dot(weight0[...], stack0[...], preferred_element_type=f32)
    for top in range(0, hidden, CHUNK):
        for left in range(0, block, LANES):
            at = (slice(top, top + CHUNK), slice(left, left + LANES))
            sine, cosine = sin_cos(pre[at])
            stack1[at] = sine.astype(bf16)
            cos0[at] = cosine
    pre[...] = jnp.dot(weight1[...], stack1[...], preferred_element_type=f32)
    for top in range(0, hidden, CHUNK):
        rows = slice(top, top + CHUNK)
        bias = column_tiles[rows, :LANES]
        out_weight = column_tiles[rows, LANES:]
        total = out_sums[rows, :]
        for strip in range(strips):
            at = (rows, slice(strip * LANES, (strip + 1) * LANES))
            cotan = fields[3, pl.ds(step * strips + strip, 1), :]
            sine, cosine = sin_cos(pre[at] + bias)
            total = total + sine * cotan
            rounded1[at] = (out_weight * cotan * cosine).astype(bf16)
        out_sums[rows, :] = total
    act_grad = jnp.dot(hidden_ref[...], rounded1[...], preferred_element_type=f32)
    rounded0[...] = (act_grad * cos0[...]).astype(bf16)
    across = (((1,), (1,)), ((), ()))
    sums[:, hidden:] += lax.dot_general(
        picks[...], rounded1[...], across, preferred_element_type=f32
    )
    hidden_sums[...] += lax.dot_general(
        stack1[:hidden, :], rounded1[...], across, preferred_element_type=f32
    )
    sums[:, :hidden] += lax.dot_general(
        picks[...], rounded0[...], across, preferred_element_type=f32
    )

    @pl.when(step == pl.num_programs(0) - 1)
    def _():
        cell_sums = sums[:cells, :]
        upper = cell_sums.astype(bf16)
        lower = (cell_sums - upper.astype(f32)).astype(bf16)
        map_grad = (
            jnp.dot(feat_t[...], upper, preferred_element_type=f32)
            + jnp.dot(feat_t[...], lower, preferred_element_type=f32)
        ) * scale
        feature_grad = (
            lax.dot_general(upper, map_ref[...], across, preferred_element_type=f32)
            + lax.dot_general(lower, map_ref[...], across, preferred_element_type=f32)
        ).astype(bf16)
        feature_grad_ref[...] = feature_grad
        hidden_grad = hidden_sums[...] * scale
        extra = sums[cells : cells + 8, :]
        total = extra[5:6, :hidden]
        lat_grad = (
            lat_cell * extra[0:1, :hidden] + lat_sub * extra[1:2, :hidden] + lat_offset * total
        )
        lon_grad = (
            lon_cell * extra[2:3, :hidden] + lon_sub * extra[3:4, :hidden] + lon_offset * total
        )
        level_grad = level_cut * extra[4:5, :hidden] + level_offset * total
        out_grad = jnp.sum(out_sums[...].T, axis=0, keepdims=True)
        gain = OMEGA * scale
        small = jnp.concatenate(
            [
                extra[5:6, :] * scale,
                jnp.concatenate([lat_grad, lon_grad], axis=1) * gain,
                jnp.concatenate([level_grad * gain, out_grad * scale], axis=1),
                jnp.zeros((EXTRA - 3, 2 * hidden), f32),
            ],
            axis=0,
        )
        folds = hidden // LANES

        def share(part):
            lanes = slice(part * LANES, (part + 1) * LANES)
            top = part // folds * channels
            left = part % folds * LANES
            return (
                map_grad[:, lanes],
                hidden_grad[top : top + channels, left : left + LANES],
                small[:, lanes],
            )

        half = PARTS // 2
        places = (
            slice(0, channels),
            slice(channels, 2 * channels),
            slice(2 * channels, 2 * channels + EXTRA),
        )
        for part in range(half):
            for place, low, high in zip(places, share(part), share(part + half)):
                kept_ref[part, place, :] = jnp.where(bit == 0, low, high).astype(bf16)
                away_ref[part, place, :] = jnp.where(bit == 0, high, low).astype(bf16)

        rows = taps * channels // PARTS
        pieces = {}
        for tap in range(taps):
            top = tap // 3 * lon_tile
            grad = lax.dot_general(
                windows[tap % 3, top : top + cells, :],
                feature_grad,
                (((0,), (0,)), ((), ())),
                preferred_element_type=f32,
            )
            grad = (grad * scale).astype(bf16)
            start = tap * channels
            while start < (tap + 1) * channels:
                end = min((start // rows + 1) * rows, (tap + 1) * channels)
                inside = slice(start % rows, start % rows + end - start)
                value = grad[start - tap * channels : end - tap * channels]
                part = start // rows

                @pl.when(bit == part // half)
                def _():
                    conv_kept_ref[part % half, inside, :] = value

                @pl.when(bit != part // half)
                def _():
                    conv_away_ref[part % half, inside, :] = value

                start = end


def query_pass(
    serve_block,
    got,
    latents,
    rims,
    conv_weight,
    map_weight,
    hidden_weight,
    weights,
    cuts,
    scale,
):
    lat_tile, lon_tile, channels = latents.shape
    cells = lat_tile * lon_tile
    taps = conv_weight.shape[0]
    slots = got.shape[0]
    queries = slots * got.shape[2] // 4
    hidden = hidden_weight.shape[0]
    width = map_weight.shape[1]
    block = min(TILE, queries)
    f32, bf16 = jnp.float32, jnp.bfloat16
    hbm = pl.BlockSpec(memory_space=pltpu.HBM)
    vmem = pl.BlockSpec(memory_space=pltpu.VMEM)
    share = (PARTS // 2, 2 * channels + EXTRA, LANES)
    conv_share = (PARTS // 2, taps * channels // PARTS, channels)

    return pl.pallas_call(
        functools.partial(query_kernel, cuts, scale, taps),
        grid=(queries // block,),
        in_specs=[hbm, vmem, hbm] + [vmem] * 4 + [hbm] * 6,
        out_specs=[vmem] * 5,
        out_shape=[
            jax.ShapeDtypeStruct(share, bf16),
            jax.ShapeDtypeStruct(share, bf16),
            jax.ShapeDtypeStruct(conv_share, bf16),
            jax.ShapeDtypeStruct(conv_share, bf16),
            jax.ShapeDtypeStruct((cells, channels), bf16),
        ],
        scratch_shapes=[
            pltpu.SMEM(serve_block.shape, jnp.int32),
            pltpu.VMEM(latents.shape, bf16),
            pltpu.VMEM(conv_weight.shape, bf16),
            pltpu.VMEM(map_weight.shape, bf16),
            pltpu.VMEM(hidden_weight.shape, bf16),
            *[pltpu.VMEM(value.shape, value.dtype) for value in weights],
            pltpu.SemaphoreType.DMA((8,)),
            pltpu.VMEM((3, cells + 2 * lon_tile, channels), bf16),
            pltpu.VMEM((cells + 2 * lon_tile, channels), f32),
            pltpu.VMEM((7, slots // 2, LANES), f32),
            pltpu.VMEM((channels, cells), bf16),
            pltpu.VMEM((channels + LANES, block), bf16),
            pltpu.VMEM((hidden + channels, block), bf16),
            pltpu.VMEM((cells + EXTRA, block), bf16),
            pltpu.VMEM((hidden, block), f32),
            pltpu.VMEM((hidden, block), f32),
            pltpu.VMEM((hidden, block), bf16),
            pltpu.VMEM((hidden, block), bf16),
            pltpu.VMEM((cells + EXTRA, width), f32),
            pltpu.VMEM((hidden, hidden), f32),
            pltpu.VMEM((hidden, LANES), f32),
        ],
        compiler_params=pltpu.CompilerParams(vmem_limit_bytes=56 * 1000 * 1000),
        name="queries",
    )(
        serve_block,
        got,
        latents,
        *rims,
        conv_weight,
        map_weight,
        hidden_weight,
        *weights,
    )


def bits_of(axis):
    return lax.axis_size(axis).bit_length() - 1


def flip(values, step):
    axis, bit = step
    count = lax.axis_size(axis)
    return lax.ppermute(values, axis, [(i, i ^ (1 << bit)) for i in range(count)])


def own_bit(step):
    axis, bit = step
    return (lax.axis_index(axis) >> bit) & 1


def added(left, right):
    return (left.astype(jnp.float32) + right.astype(jnp.float32)).astype(left.dtype)


def half_sum(kept, got, step, other):
    def pick(values):
        halves = values.reshape((2, values.shape[0] // 2) + values.shape[1:])
        mine = own_bit(step)
        place = 1 - mine if other else mine
        return lax.dynamic_index_in_dim(halves, place, 0, keepdims=False)

    return added(pick(kept), pick(got))


def ring(axis, turn):
    count = lax.axis_size(axis)
    return [(i, (i + turn) % count) for i in range(count)]


def lat_rims(tile):
    top = lax.ppermute(tile[-1:], "lat", ring("lat", 1))
    bottom = lax.ppermute(tile[:1], "lat", ring("lat", -1))
    return top, bottom


def lon_rims(tile, top, bottom):
    last = jnp.concatenate([top[:, -1], tile[:, -1], bottom[:, -1]], axis=0)
    first = jnp.concatenate([top[:, 0], tile[:, 0], bottom[:, 0]], axis=0)
    left = lax.ppermute(last, "lon", ring("lon", 1))
    right = lax.ppermute(first, "lon", ring("lon", -1))
    return left, right


def unpack_kernel(
    mine_a,
    theirs_a,
    mine_b,
    theirs_b,
    conv_ref,
    map_ref,
    bias_ref,
    input_ref,
    hidden_ref,
    out_ref,
):
    f32 = jnp.float32
    channels = map_ref.shape[0]
    folds = hidden_ref.shape[1] // LANES
    half = PARTS // 2
    lon_pos = lax.axis_index("lon")
    bit, bit_first, bit_second = lon_pos & 1, (lon_pos >> 1) & 1, (lon_pos >> 2) & 1

    def place(part, upper_bit, lower_bit):
        upper = 1 - upper_bit if part // 2 % 2 else upper_bit
        lower = 1 - lower_bit if part % 2 else lower_bit
        return upper * 2 + lower

    def fill(low_a, high_a, low_b, high_b):
        for part in range(PARTS):
            source = (low_a if part < half else high_a).at[place(part, bit_first, bit_second)]
            lanes = slice(part * LANES, (part + 1) * LANES)
            top = part // folds * channels
            left = part % folds * LANES
            map_ref[:, lanes] = source[:channels, :].astype(f32)
            hidden_ref[top : top + channels, left : left + LANES] = source[
                channels : 2 * channels, :
            ].astype(f32)
            small = source[2 * channels :, :].astype(f32)
            bias_ref[lanes] = small[0, :]
            side = slice(left, left + LANES)
            input_ref[part // folds, side] = small[1, :]
            if part < folds:
                input_ref[2, side] = small[2, :]
            else:
                out_ref[side] = small[2, :]
            source = (low_b if part < half else high_b).at[place(part, bit_second, bit_first)]
            rows = source.shape[0]
            conv_ref[part * rows : (part + 1) * rows, :] = source[...].astype(f32)

    @pl.when(bit == 0)
    def _():
        fill(mine_a, theirs_a, mine_b, theirs_b)

    @pl.when(bit == 1)
    def _():
        fill(theirs_a, mine_a, theirs_b, mine_b)


def unpacked(pair_a, pair_b, channels, hidden, width, conv_rows):
    f32 = jnp.float32
    vmem = pl.BlockSpec(memory_space=pltpu.VMEM)
    return pl.pallas_call(
        unpack_kernel,
        in_specs=[vmem] * 4,
        out_specs=[vmem] * 6,
        out_shape=[
            jax.ShapeDtypeStruct((conv_rows, channels), f32),
            jax.ShapeDtypeStruct((channels, width), f32),
            jax.ShapeDtypeStruct((width,), f32),
            jax.ShapeDtypeStruct((3, hidden), f32),
            jax.ShapeDtypeStruct((hidden, hidden), f32),
            jax.ShapeDtypeStruct((hidden,), f32),
        ],
        compiler_params=pltpu.CompilerParams(vmem_limit_bytes=20 * 1024 * 1024),
        name="unpack",
    )(*pair_a, *pair_b)


def on_device(
    latents,
    conv_weight,
    map_weight,
    map_bias,
    input_weight,
    hidden_weight,
    output_weight,
    hit_owner,
    serve_block,
    query_grid,
    cotangent,
):
    lat_tile, lon_tile, channels = latents.shape
    lat_parts = lax.axis_size("lat")
    lon_parts = lax.axis_size("lon")
    dev_count = lat_parts * lon_parts
    lat_cells = lat_tile * lat_parts
    lon_cells = lon_tile * lon_parts
    lat_pos = lax.axis_index("lat")
    hit_count = hit_owner.shape[0]
    group_size = cotangent.shape[0] // hit_count
    width = input_weight.shape[1]
    steps = [(axis, bit) for axis in ("lon", "lat") for bit in range(bits_of(axis))]
    core, first, second = steps[:3]
    rest = steps[3:]
    cuts = (
        2.0 / lat_cells,
        2.0 / (lat_cells * SUB),
        2.0 / lon_cells,
        2.0 / (lon_cells * SUB),
        2.0 / LEVELS,
        1.0 / LEVELS - 1.0,
    )
    grad_scale = float(hit_count * group_size * dev_count) ** (-0.5)
    sent = packed(hit_owner, query_grid, cotangent, dev_count, group_size)
    sent, rim_tile, late_map = lax.optimization_barrier((sent, latents, map_weight))
    got = lax.all_to_all(sent, ("lat", "lon"), split_axis=0, concat_axis=0, tiled=True)
    top, bottom = lat_rims(rim_tile)
    rims = (top, bottom, *lon_rims(rim_tile, top, bottom))
    weights = prepared_weights(
        (lat_tile, lon_tile),
        late_map,
        map_bias,
        input_weight,
        hidden_weight[0],
        output_weight,
        cuts,
    )
    kept_a, away_a, kept_b, away_b, feature_grad = query_pass(
        serve_block,
        got,
        latents,
        rims,
        conv_weight,
        map_weight,
        hidden_weight[0],
        weights,
        cuts,
        grad_scale,
    )
    taps = conv_weight.shape[0]
    feature_grad = feature_grad.reshape(lat_tile, lon_tile, channels)
    hold = lax.optimization_barrier
    got_a, got_b = flip(away_a, core), flip(away_b, core)

    away_a, away_b = half_sum(kept_a, got_a, first, 1), half_sum(kept_b, got_b, second, 1)
    away_a, away_b, feature_grad = hold((away_a, away_b, feature_grad))
    kept_a, kept_b = half_sum(kept_a, got_a, first, 0), half_sum(kept_b, got_b, second, 0)
    got_a, got_b = flip(away_a, first), flip(away_b, second)
    top, bottom = lat_rims(feature_grad)

    away_a, away_b = half_sum(kept_a, got_a, second, 1), half_sum(kept_b, got_b, first, 1)
    away_a, away_b, top, bottom = hold((away_a, away_b, top, bottom))
    kept_a, kept_b = half_sum(kept_a, got_a, second, 0), half_sum(kept_b, got_b, first, 0)
    got_a, got_b = flip(away_a, second), flip(away_b, first)

    sum_a, sum_b = added(kept_a, got_a), added(kept_b, got_b)
    for step_a, step_b in zip(rest, rest[::-1]):
        sum_a, sum_b = hold((sum_a, sum_b))
        got_a, got_b = flip(sum_a, step_a), flip(sum_b, step_b)
        if step_a == rest[0]:
            left, right = lon_rims(feature_grad, top, bottom)
        sum_a, sum_b = added(sum_a, got_a), added(sum_b, got_b)

    for step_a, step_b in ((second, first), (first, second)):
        sum_a, sum_b = hold((sum_a, sum_b))
        got_a, got_b = flip(sum_a, step_a), flip(sum_b, step_b)
        sum_a = jnp.concatenate([sum_a, got_a], axis=0)
        sum_b = jnp.concatenate([sum_b, got_b], axis=0)
    sum_a, sum_b = hold((sum_a, sum_b))
    got_a, got_b = flip(sum_a, core), flip(sum_b, core)

    padded_grad = close_poles(
        jnp.concatenate(
            [
                left[:, None],
                jnp.concatenate([top, feature_grad, bottom], axis=0),
                right[:, None],
            ],
            axis=1,
        ),
        lat_pos,
        lat_parts,
    )
    latent_grad = conv_apply(padded_grad, conv_weight, lat_tile, lon_tile, True).reshape(
        lat_tile, lon_tile, channels
    )
    totals = unpacked(
        (sum_a, got_a),
        (sum_b, got_b),
        channels,
        width,
        2 * width,
        taps * channels,
    )
    return (
        latent_grad,
        totals[0].reshape(taps, channels, channels),
        *totals[1:4],
        totals[4][None],
        totals[5],
    )


def solution(mesh):
    placed = (
        P("lat", "lon", None),
        P(),
        P(),
        P(),
        P(),
        P(),
        P(),
        P(("lat", "lon")),
        P(("lat", "lon"), None),
        P(None, ("lat", "lon")),
        P(("lat", "lon")),
    )
    return jax.shard_map(
        on_device,
        mesh=mesh,
        in_specs=placed,
        out_specs=(P("lat", "lon", None), P(), P(), P(), P(), P(), P()),
        check_vma=False,
    )
```

```python
import functools

import jax
import jax.numpy as jnp
from jax import lax
from jax.experimental import pallas as pl
from jax.experimental.pallas import tpu as pltpu
from jax.sharding import PartitionSpec as P

BLOCK = 128
LEVELS = 37
SUB = 6


OMEGA = 30.0
TILE = 2048
SPAN = 256
PARTS = 8


def conv_apply(padded, kernel, row_count, col_count, flipped):
    channels = padded.shape[-1]
    result = jnp.zeros((row_count * col_count, kernel.shape[-1]), jnp.float32)
    for shift_a in (-1, 0, 1):
        for shift_b in (-1, 0, 1):
            tap_index = (shift_a + 1) * 3 + shift_b + 1
            if flipped:
                window = padded[
                    1 - shift_a : 1 - shift_a + row_count, 1 - shift_b : 1 - shift_b + col_count
                ]
                matrix = kernel[tap_index].T
            else:
                window = padded[
                    1 + shift_a : 1 + shift_a + row_count, 1 + shift_b : 1 + shift_b + col_count
                ]
                matrix = kernel[tap_index]
            result = result + jnp.dot(
                window.reshape(row_count * col_count, channels),
                matrix,
                preferred_element_type=jnp.float32,
            )
    return result


def close_poles(padded, lat_pos, lat_parts):
    top_rim = jnp.where(lat_pos == 0, jnp.zeros_like(padded[:1]), padded[:1])
    bottom_rim = jnp.where(lat_pos == lat_parts - 1, jnp.zeros_like(padded[-1:]), padded[-1:])
    return jnp.concatenate([top_rim, padded[1:-1], bottom_rim], axis=0)


SIN_TERMS = (
    0.7071067781421408,
    -0.029462767114633488,
    0.0003682722504284759,
    -2.1886040931894034e-06,
    7.195418014521965e-09,
)
COS_TERMS = (
    1.4142134959273227,
    -0.17677635831469551,
    0.0036825740917005817,
    -3.061241565438332e-05,
    1.2789559619534725e-07,
)
TURN = 6.283185307179586
TURN_HIGH = 6.28125
TURN_LOW = TURN - TURN_HIGH
EXTRA = 16
COORD_ROWS = 32
CHUNK = 64
LANES = 128


def sin_cos(angle):
    turns = jnp.round(angle * (1.0 / TURN))
    rest = (angle - turns * TURN_HIGH) - turns * TURN_LOW
    square = rest * rest

    def series(terms):
        value = jnp.full_like(square, terms[-1])
        for term in terms[-2::-1]:
            value = value * square + term
        return value

    half_sin = rest * series(SIN_TERMS)
    half_cos = series(COS_TERMS)
    return half_sin * half_cos, 1.0 - half_sin * half_sin


def pack_kernel(owner_ref, grid_ref, cotan_ref, sent_ref):
    half = LANES // 2
    lower = lax.broadcasted_iota(jnp.int32, (1, LANES), 1) < half
    sent_ref[...] = jnp.zeros_like(sent_ref)
    for pair in range(owner_ref.shape[0] // 2):
        lanes = slice(pair * LANES, (pair + 1) * LANES)
        grid = grid_ref[:, lanes].astype(jnp.float32)
        values = [grid[0:1], grid[1:2], grid[2:3], cotan_ref[lanes].reshape(1, LANES)]
        turned = [pltpu.roll(value, half, 1) for value in values]
        sent_ref[owner_ref[2 * pair]] = jnp.concatenate(
            [
                jnp.where(lower, values[0], turned[1]),
                jnp.where(lower, values[2], turned[3]),
            ],
            axis=1,
        )
        sent_ref[owner_ref[2 * pair + 1]] = jnp.concatenate(
            [
                jnp.where(lower, turned[0], values[1]),
                jnp.where(lower, turned[2], values[3]),
            ],
            axis=1,
        )


def packed(hit_owner, query_grid, cotangent, slots, group_size):
    vmem = pl.BlockSpec(memory_space=pltpu.VMEM)
    return pl.pallas_call(
        pack_kernel,
        in_specs=[pl.BlockSpec(memory_space=pltpu.SMEM), vmem, vmem],
        out_specs=vmem,
        out_shape=jax.ShapeDtypeStruct((slots, 1, 4 * group_size), jnp.float32),
        name="pack",
    )(hit_owner, query_grid, cotangent)


def fetched(sources, targets, sems):
    copies = [
        pltpu.make_async_copy(source, target, sems.at[index])
        for index, (source, target) in enumerate(zip(sources, targets))
    ]
    for copy in copies:
        copy.start()
    return copies


def weights_kernel(cuts, tile_shape, *refs):
    sources, (weight0, weight1, column_tiles), (*targets, sems) = refs[:5], refs[5:8], refs[8:]
    map_ref, bias_ref, input_ref, hidden_ref, output_ref = targets
    for copy in fetched(sources, targets, sems):
        copy.wait()
    channels = map_ref.shape[0]
    hidden = hidden_ref.shape[0]
    f32, bf16 = jnp.float32, jnp.bfloat16
    lat_cell, lat_sub, lon_cell, lon_sub, level_cut, level_offset = cuts
    lat_offset, lon_offset = tile_offsets(tile_shape, cuts)
    weight0[:, :channels] = map_ref[:, :hidden].T
    bias = bias_ref[...].reshape(1, 2 * hidden)
    lat_weight = OMEGA * input_ref[0:1, :]
    lon_weight = OMEGA * input_ref[1:2, :]
    level_weight = OMEGA * input_ref[2:3, :]
    constant = (
        lat_offset * lat_weight
        + lon_offset * lon_weight
        + level_offset * level_weight
        + bias[:, :hidden]
    )
    zero = jnp.zeros_like(constant)
    coef = jnp.concatenate(
        [
            lat_cell * lat_weight,
            lat_sub * lat_weight,
            lon_cell * lon_weight,
            lon_sub * lon_weight,
            level_cut * level_weight,
            constant,
            zero,
            zero,
        ],
        axis=0,
    )
    high = coef.astype(bf16).astype(f32)
    mid = (coef - high).astype(bf16).astype(f32)
    low = coef - high - mid
    parts = jnp.concatenate([high, mid, low, jnp.zeros((LANES - 24, hidden), f32)], axis=0)
    weight0[:, channels:] = parts.T.astype(bf16)
    weight1[:, :hidden] = hidden_ref[...].T
    weight1[:, hidden:] = map_ref[:, hidden:].T
    column_tiles[:, :LANES] = jnp.broadcast_to(bias[:, hidden:], (LANES, hidden)).T
    column_tiles[:, LANES:] = jnp.broadcast_to(
        output_ref[...].reshape(1, hidden), (LANES, hidden)
    ).T


def tile_offsets(tile_shape, cuts):
    lat_step, lon_step = cuts[1], cuts[3]
    lat_base = 2 * SUB * tile_shape[0] * lax.axis_index("lat") + 1
    lon_base = 2 * SUB * tile_shape[1] * lax.axis_index("lon") + 1
    return (
        lat_base.astype(jnp.float32) * (0.5 * lat_step) - 1.0,
        lon_base.astype(jnp.float32) * (0.5 * lon_step) - 1.0,
    )


def prepared_weights(
    tile_shape, map_weight, map_bias, input_weight, hidden_weight, output_weight, cuts
):
    channels = map_weight.shape[0]
    hidden = hidden_weight.shape[0]
    sources = (map_weight, map_bias, input_weight, hidden_weight, output_weight)
    vmem = pl.BlockSpec(memory_space=pltpu.VMEM)
    return pl.pallas_call(
        functools.partial(weights_kernel, cuts, tile_shape),
        in_specs=[pl.BlockSpec(memory_space=pltpu.HBM)] * 5,
        out_specs=[vmem] * 3,
        out_shape=[
            jax.ShapeDtypeStruct((hidden, channels + LANES), jnp.bfloat16),
            jax.ShapeDtypeStruct((hidden, hidden + channels), jnp.bfloat16),
            jax.ShapeDtypeStruct((hidden, 2 * LANES), jnp.float32),
        ],
        scratch_shapes=[pltpu.VMEM(value.shape, value.dtype) for value in sources]
        + [pltpu.SemaphoreType.DMA((5,))],

        name="weights",
    )(*sources)


def query_kernel(
    cuts,
    scale,
    taps,
    single,
    serve_hbm,
    got_ref,
    tile_hbm,
    top_ref,
    bottom_ref,
    left_ref,
    right_ref,
    conv_hbm,
    map_hbm,
    hidden_hbm,
    weight0_hbm,
    weight1_hbm,
    columns_hbm,
    kept_ref,
    away_ref,
    conv_kept_ref,
    conv_away_ref,
    feature_grad_ref,
    serve_ref,
    tile_ref,
    conv_ref,
    map_ref,
    hidden_ref,
    weight0,
    weight1,
    column_tiles,
    sems,
    windows,
    turned,
    shifted,
    fields,
    feat_t,
    stack0,
    lefts,
    pre0,
    pre1,
    cos0,
    rounded0,
    rounded1,
    sums,
    later_sums,
    out_sums,
):
    step = pl.program_id(0)
    lat_tile, lon_tile, channels = tile_ref.shape
    cells = lat_tile * lon_tile
    hidden = hidden_ref.shape[0]
    block = rounded0.shape[1]
    left_rows = cells + EXTRA
    f32, bf16 = jnp.float32, jnp.bfloat16
    lat_cell, lat_sub, lon_cell, lon_sub, level_cut, level_offset = cuts
    lat_pos = lax.axis_index("lat")
    bit = lax.axis_index("lon") & 1
    lat_offset, lon_offset = tile_offsets((lat_tile, lon_tile), cuts)

    @pl.when(step == 0)
    def _():
        copies = fetched(
            (
                tile_hbm,
                serve_hbm,
                conv_hbm,
                weight0_hbm,
                weight1_hbm,
                columns_hbm,
                hidden_hbm,
                map_hbm,
            ),
            (
                tile_ref,
                serve_ref,
                conv_ref,
                weight0,
                weight1,
                column_tiles,
                hidden_ref,
                map_ref,
            ),
            sems,
        )
        copies[1].wait()
        half = LANES // 2
        lower = lax.broadcasted_iota(jnp.int32, (1, LANES), 1) < half
        for pair in range(got_ref.shape[0] // 2):
            even, odd = got_ref[2 * pair], got_ref[2 * pair + 1]
            row = slice(pair, pair + 1)
            for place in range(2):
                lanes = slice(place * LANES, (place + 1) * LANES)
                near, far = even[:, lanes], odd[:, lanes]
                fields[2 * place, row, :] = jnp.where(lower, near, pltpu.roll(far, half, 1))
                fields[2 * place + 1, row, :] = jnp.where(lower, pltpu.roll(near, half, 1), far)
            serve = jnp.where(lower, serve_ref[0, 2 * pair], serve_ref[0, 2 * pair + 1])
            fields[4, row, :] = serve.astype(f32)
        serve = fields[4]
        tile_cell = jnp.where(serve < 0.0, -1.0, serve * float(BLOCK) + fields[0])
        cell_row = jnp.floor((tile_cell + 0.5) * (1.0 / lon_tile))
        sub = fields[1]
        sub_row = jnp.floor((sub + 0.5) * (1.0 / SUB))
        fields[0] = tile_cell
        fields[1] = cell_row
        fields[4] = sub_row
        fields[5] = tile_cell - cell_row * float(lon_tile)
        fields[6] = sub - sub_row * float(SUB)

        copies[0].wait()
        flat = jnp.concatenate(
            [top_ref[0], tile_ref[...].reshape(cells, channels), bottom_ref[0]], axis=0
        )
        first = jnp.where(lat_pos == 0, 0.0, 1.0)
        last = jnp.where(lat_pos == lax.axis_size("lat") - 1, 0.0, 1.0)
        ends = cells + lon_tile

        def keep(slot, values):
            windows[slot, :lon_tile, :] = (values[:lon_tile] * first).astype(bf16)
            windows[slot, lon_tile:ends, :] = values[lon_tile:ends].astype(bf16)
            windows[slot, ends:, :] = (values[ends:] * last).astype(bf16)

        flat = flat.astype(f32)
        total_rows = flat.shape[0]
        keep(1, flat)
        left = left_ref[...].astype(f32)
        right = right_ref[...].astype(f32)
        shifted[...] = pltpu.roll(flat, 1, 0)
        for row in range(lat_tile + 2):
            shifted[row * lon_tile : row * lon_tile + 1, :] = left[row : row + 1]
        keep(0, shifted[...])
        shifted[...] = pltpu.roll(flat, total_rows - 1, 0)
        for row in range(1, lat_tile + 3):
            shifted[row * lon_tile - 1 : row * lon_tile, :] = right[row - 1 : row]
        keep(2, shifted[...])
        for tap in range(taps):
            top = tap // 3 * lon_tile
            turned[tap] = windows[tap % 3, top : top + cells, :].T
        copies[2].wait()
        features = jnp.zeros((cells, channels), f32)
        for tap in range(taps):
            top = tap // 3 * lon_tile
            features = features + jnp.dot(
                windows[tap % 3, top : top + cells, :], conv_ref[tap], preferred_element_type=f32
            )
        feat_t[...] = features.T.astype(bf16)

        for copy in copies[3:]:
            copy.wait()
        stack0[...] = jnp.zeros_like(stack0)
        if not single:
            sums[...] = jnp.zeros_like(sums)
            later_sums[...] = jnp.zeros_like(later_sums)
        out_sums[...] = jnp.zeros_like(out_sums)

    ids = lax.broadcasted_iota(jnp.int32, (cells, LANES), 0)
    strips = block // LANES
    for strip in range(strips):
        row = pl.ds(step * strips + strip, 1)
        lanes = slice(strip * LANES, (strip + 1) * LANES)
        cell = fields[0, row, :].astype(jnp.int32)
        lefts[:cells, lanes] = jnp.where(ids == cell, 1.0, 0.0).astype(bf16)
        one = jnp.ones((1, LANES), f32)
        group = jnp.concatenate(
            [
                fields[1, row, :],
                fields[4, row, :],
                fields[5, row, :],
                fields[6, row, :],
                fields[2, row, :],
                one,
                jnp.zeros((2, LANES), f32),
            ],
            axis=0,
        )
        coords = jnp.concatenate([group, group, group, jnp.zeros_like(group)], axis=0).astype(
            bf16
        )
        stack0[channels : channels + COORD_ROWS, lanes] = coords
        lefts[cells:left_rows, lanes] = coords[:EXTRA]
    across = (((1,), (1,)), ((), ()))
    spans = block // SPAN
    acts = left_rows + hidden

    def span(index):
        return slice(index * SPAN, (index + 1) * SPAN)

    def first_dots(index):
        lanes = span(index)
        queried = jnp.dot(feat_t[...], lefts[:cells, lanes], preferred_element_type=f32)
        queried = queried.astype(bf16)
        stack0[:channels, lanes] = queried
        lefts[acts:, lanes] = queried
        pre0[:, lanes] = jnp.dot(weight0[...], stack0[:, lanes], preferred_element_type=f32)

    def first_sines(index):
        for top in range(0, hidden, CHUNK):
            for left in range(index * SPAN, (index + 1) * SPAN, LANES):
                at = (slice(top, top + CHUNK), slice(left, left + LANES))
                sine, cosine = sin_cos(pre0[at])
                lefts[left_rows + top : left_rows + top + CHUNK, at[1]] = sine.astype(bf16)
                cos0[at] = cosine

    def second_dots(index):
        lanes = span(index)
        pre1[:, lanes] = jnp.dot(
            weight1[...], lefts[left_rows:, lanes], preferred_element_type=f32
        )

    def second_sines(index):
        for top in range(0, hidden, CHUNK):
            rows = slice(top, top + CHUNK)
            bias = column_tiles[rows, :LANES]
            out_weight = column_tiles[rows, LANES:]
            total = out_sums[rows, :]
            for left in range(index * SPAN, (index + 1) * SPAN, LANES):
                at = (rows, slice(left, left + LANES))
                cotan = fields[3, pl.ds(step * strips + left // LANES, 1), :]
                sine, cosine = sin_cos(pre1[at] + bias)
                total = total + sine * cotan
                rounded1[at] = (out_weight * cotan * cosine).astype(bf16)
            out_sums[rows, :] = total

    def third_dots(index):
        lanes = span(index)
        act_grad = jnp.dot(hidden_ref[...], rounded1[:, lanes], preferred_element_type=f32)
        rounded0[:, lanes] = (act_grad * cos0[:, lanes]).astype(bf16)

    def joins(lanes):
        later = lax.dot_general(
            lefts[:acts, lanes], rounded1[:, lanes], across, preferred_element_type=f32
        )
        early = lax.dot_general(
            lefts[:left_rows, lanes], rounded0[:, lanes], across, preferred_element_type=f32
        )
        if single:
            later_sums[...] = later
            sums[...] = early
        else:
            later_sums[...] += later
            sums[...] += early

    first_dots(0)
    for turn in range(spans + 2):
        if turn + 1 < spans:
            first_dots(turn + 1)
        if turn < spans:
            first_sines(turn)
            second_dots(turn)
        if 0 <= turn - 1 < spans:
            second_sines(turn - 1)
            third_dots(turn - 1)
    joins(slice(0, block))

    @pl.when(step == pl.num_programs(0) - 1)
    def _():
        cell_sums = jnp.concatenate([sums[:cells, :], later_sums[:cells, :]], axis=1)
        upper = cell_sums.astype(bf16)
        lower = (cell_sums - upper.astype(f32)).astype(bf16)
        map_grad = (
            jnp.dot(feat_t[...], upper, preferred_element_type=f32)
            + jnp.dot(feat_t[...], lower, preferred_element_type=f32)
        ) * scale
        feature_grad = (
            lax.dot_general(upper, map_ref[...], across, preferred_element_type=f32)
            + lax.dot_general(lower, map_ref[...], across, preferred_element_type=f32)
        ).astype(bf16)
        feature_grad_ref[...] = feature_grad
        hidden_grad = later_sums[left_rows:, :] * scale
        extra = sums[cells : cells + 8, :]
        later_bias = later_sums[cells + 5 : cells + 6, :]
        total = extra[5:6, :]
        lat_grad = (
            lat_cell * extra[0:1, :] + lat_sub * extra[1:2, :] + lat_offset * total
        )
        lon_grad = (
            lon_cell * extra[2:3, :] + lon_sub * extra[3:4, :] + lon_offset * total
        )
        level_grad = level_cut * extra[4:5, :] + level_offset * total
        out_grad = jnp.sum(out_sums[...].T, axis=0, keepdims=True)
        gain = OMEGA * scale
        small = jnp.concatenate(
            [
                jnp.concatenate([total, later_bias], axis=1) * scale,
                jnp.concatenate([lat_grad, lon_grad], axis=1) * gain,
                jnp.concatenate([level_grad * gain, out_grad * scale], axis=1),
                jnp.zeros((EXTRA - 3, 2 * hidden), f32),
            ],
            axis=0,
        )
        folds = hidden // LANES

        def share(part):
            lanes = slice(part * LANES, (part + 1) * LANES)
            top = part // folds * channels
            left = part % folds * LANES
            return (
                map_grad[:, lanes],
                hidden_grad[top : top + channels, left : left + LANES],
                small[:, lanes],
            )

        half = PARTS // 2
        places = (
            slice(0, channels),
            slice(channels, 2 * channels),
            slice(2 * channels, 2 * channels + EXTRA),
        )
        for part in range(half):
            for place, low, high in zip(places, share(part), share(part + half)):
                kept_ref[part, place, :] = jnp.where(bit == 0, low, high).astype(bf16)
                away_ref[part, place, :] = jnp.where(bit == 0, high, low).astype(bf16)

        rows = taps * channels // PARTS
        for tap in range(taps):
            grad = jnp.dot(turned[tap], feature_grad, preferred_element_type=f32)
            grad = (grad * scale).astype(bf16)
            start = tap * channels
            while start < (tap + 1) * channels:
                end = min((start // rows + 1) * rows, (tap + 1) * channels)
                inside = slice(start % rows, start % rows + end - start)
                value = grad[start - tap * channels : end - tap * channels]
                part = start // rows

                @pl.when(bit == part // half)
                def _():
                    conv_kept_ref[part % half, inside, :] = value

                @pl.when(bit != part // half)
                def _():
                    conv_away_ref[part % half, inside, :] = value

                start = end


def query_pass(
    serve_block,
    got,
    latents,
    rims,
    conv_weight,
    map_weight,
    hidden_weight,
    weights,
    cuts,
    scale,
):
    lat_tile, lon_tile, channels = latents.shape
    cells = lat_tile * lon_tile
    taps = conv_weight.shape[0]
    slots = got.shape[0]
    queries = slots * got.shape[2] // 4
    hidden = hidden_weight.shape[0]
    width = map_weight.shape[1]
    block = min(TILE, queries)
    f32, bf16 = jnp.float32, jnp.bfloat16
    hbm = pl.BlockSpec(memory_space=pltpu.HBM)
    vmem = pl.BlockSpec(memory_space=pltpu.VMEM)
    share = (PARTS // 2, 2 * channels + EXTRA, LANES)
    conv_share = (PARTS // 2, taps * channels // PARTS, channels)

    return pl.pallas_call(
        functools.partial(query_kernel, cuts, scale, taps, queries == block),
        grid=(queries // block,),
        in_specs=[hbm, vmem, hbm] + [vmem] * 4 + [hbm] * 6,
        out_specs=[vmem] * 5,
        out_shape=[
            jax.ShapeDtypeStruct(share, bf16),
            jax.ShapeDtypeStruct(share, bf16),
            jax.ShapeDtypeStruct(conv_share, bf16),
            jax.ShapeDtypeStruct(conv_share, bf16),
            jax.ShapeDtypeStruct((cells, channels), bf16),
        ],
        scratch_shapes=[
            pltpu.SMEM(serve_block.shape, jnp.int32),
            pltpu.VMEM(latents.shape, bf16),
            pltpu.VMEM(conv_weight.shape, bf16),
            pltpu.VMEM(map_weight.shape, bf16),
            pltpu.VMEM(hidden_weight.shape, bf16),
            *[pltpu.VMEM(value.shape, value.dtype) for value in weights],
            pltpu.SemaphoreType.DMA((8,)),
            pltpu.VMEM((3, cells + 2 * lon_tile, channels), bf16),
            pltpu.VMEM((taps, channels, cells), bf16),
            pltpu.VMEM((cells + 2 * lon_tile, channels), f32),
            pltpu.VMEM((7, slots // 2, LANES), f32),
            pltpu.VMEM((channels, cells), bf16),
            pltpu.VMEM((channels + LANES, block), bf16),
            pltpu.VMEM((cells + EXTRA + hidden + channels, block), bf16),
            pltpu.VMEM((hidden, block), f32),
            pltpu.VMEM((hidden, block), f32),
            pltpu.VMEM((hidden, block), f32),
            pltpu.VMEM((hidden, block), bf16),
            pltpu.VMEM((hidden, block), bf16),
            pltpu.VMEM((cells + EXTRA, hidden), f32),
            pltpu.VMEM((cells + EXTRA + hidden, hidden), f32),
            pltpu.VMEM((hidden, LANES), f32),
        ],
        compiler_params=pltpu.CompilerParams(vmem_limit_bytes=56 * 1000 * 1000),
        name="queries",
    )(
        serve_block,
        got,
        latents,
        *rims,
        conv_weight,
        map_weight,
        hidden_weight,
        *weights,
    )


def bits_of(axis):
    return lax.axis_size(axis).bit_length() - 1


def flip(values, step):
    axis, bit = step
    count = lax.axis_size(axis)
    return lax.ppermute(values, axis, [(i, i ^ (1 << bit)) for i in range(count)])


def own_bit(step):
    axis, bit = step
    return (lax.axis_index(axis) >> bit) & 1


def added(left, right):
    return (left.astype(jnp.float32) + right.astype(jnp.float32)).astype(left.dtype)


def half_sum(kept, got, step, other):
    def pick(values):
        halves = values.reshape((2, values.shape[0] // 2) + values.shape[1:])
        mine = own_bit(step)
        place = 1 - mine if other else mine
        return lax.dynamic_index_in_dim(halves, place, 0, keepdims=False)

    return added(pick(kept), pick(got))


def ring(axis, turn):
    count = lax.axis_size(axis)
    return [(i, (i + turn) % count) for i in range(count)]


def lat_rims(tile):
    top = lax.ppermute(tile[-1:], "lat", ring("lat", 1))
    bottom = lax.ppermute(tile[:1], "lat", ring("lat", -1))
    return top, bottom


def lon_rims(tile, top, bottom):
    last = jnp.concatenate([top[:, -1], tile[:, -1], bottom[:, -1]], axis=0)
    first = jnp.concatenate([top[:, 0], tile[:, 0], bottom[:, 0]], axis=0)
    left = lax.ppermute(last, "lon", ring("lon", 1))
    right = lax.ppermute(first, "lon", ring("lon", -1))
    return left, right


def unpack_kernel(
    mine_a,
    theirs_a,
    mine_b,
    theirs_b,
    conv_ref,
    map_ref,
    bias_ref,
    input_ref,
    hidden_ref,
    out_ref,
):
    f32 = jnp.float32
    channels = map_ref.shape[0]
    folds = hidden_ref.shape[1] // LANES
    half = PARTS // 2
    lon_pos = lax.axis_index("lon")
    bit, bit_first, bit_second = lon_pos & 1, (lon_pos >> 1) & 1, (lon_pos >> 2) & 1

    def place(part, upper_bit, lower_bit):
        upper = 1 - upper_bit if part // 2 % 2 else upper_bit
        lower = 1 - lower_bit if part % 2 else lower_bit
        return upper * 2 + lower

    def fill(low_a, high_a, low_b, high_b):
        for part in range(PARTS):
            source = (low_a if part < half else high_a).at[place(part, bit_first, bit_second)]
            lanes = slice(part * LANES, (part + 1) * LANES)
            top = part // folds * channels
            left = part % folds * LANES
            map_ref[:, lanes] = source[:channels, :].astype(f32)
            hidden_ref[top : top + channels, left : left + LANES] = source[
                channels : 2 * channels, :
            ].astype(f32)
            small = source[2 * channels :, :].astype(f32)
            bias_ref[lanes] = small[0, :]
            side = slice(left, left + LANES)
            input_ref[part // folds, side] = small[1, :]
            if part < folds:
                input_ref[2, side] = small[2, :]
            else:
                out_ref[side] = small[2, :]
            source = (low_b if part < half else high_b).at[place(part, bit_second, bit_first)]
            rows = source.shape[0]
            conv_ref[part * rows : (part + 1) * rows, :] = source[...].astype(f32)

    @pl.when(bit == 0)
    def _():
        fill(mine_a, theirs_a, mine_b, theirs_b)

    @pl.when(bit == 1)
    def _():
        fill(theirs_a, mine_a, theirs_b, mine_b)


def unpacked(pair_a, pair_b, channels, hidden, width, conv_rows):
    f32 = jnp.float32
    vmem = pl.BlockSpec(memory_space=pltpu.VMEM)
    return pl.pallas_call(
        unpack_kernel,
        in_specs=[vmem] * 4,
        out_specs=[vmem] * 6,
        out_shape=[
            jax.ShapeDtypeStruct((conv_rows, channels), f32),
            jax.ShapeDtypeStruct((channels, width), f32),
            jax.ShapeDtypeStruct((width,), f32),
            jax.ShapeDtypeStruct((3, hidden), f32),
            jax.ShapeDtypeStruct((hidden, hidden), f32),
            jax.ShapeDtypeStruct((hidden,), f32),
        ],
        compiler_params=pltpu.CompilerParams(vmem_limit_bytes=20 * 1024 * 1024),
        name="unpack",
    )(*pair_a, *pair_b)


def on_device(
    latents,
    conv_weight,
    map_weight,
    map_bias,
    input_weight,
    hidden_weight,
    output_weight,
    hit_owner,
    serve_block,
    query_grid,
    cotangent,
):
    lat_tile, lon_tile, channels = latents.shape
    lat_parts = lax.axis_size("lat")
    lon_parts = lax.axis_size("lon")
    dev_count = lat_parts * lon_parts
    lat_cells = lat_tile * lat_parts
    lon_cells = lon_tile * lon_parts
    lat_pos = lax.axis_index("lat")
    hit_count = hit_owner.shape[0]
    group_size = cotangent.shape[0] // hit_count
    width = input_weight.shape[1]
    steps = [(axis, bit) for axis in ("lon", "lat") for bit in range(bits_of(axis))]
    core, first, second = steps[:3]
    rest = steps[3:]
    cuts = (
        2.0 / lat_cells,
        2.0 / (lat_cells * SUB),
        2.0 / lon_cells,
        2.0 / (lon_cells * SUB),
        2.0 / LEVELS,
        1.0 / LEVELS - 1.0,
    )
    grad_scale = float(hit_count * group_size * dev_count) ** (-0.5)
    sent = packed(hit_owner, query_grid, cotangent, dev_count, group_size)
    sent, rim_tile, late_map = lax.optimization_barrier((sent, latents, map_weight))
    got = lax.all_to_all(sent, ("lat", "lon"), split_axis=0, concat_axis=0, tiled=True)
    top, bottom = lat_rims(rim_tile)
    rims = (top, bottom, *lon_rims(rim_tile, top, bottom))
    weights = prepared_weights(
        (lat_tile, lon_tile),
        late_map,
        map_bias,
        input_weight,
        hidden_weight[0],
        output_weight,
        cuts,
    )
    kept_a, away_a, kept_b, away_b, feature_grad = query_pass(
        serve_block,
        got,
        latents,
        rims,
        conv_weight,
        map_weight,
        hidden_weight[0],
        weights,
        cuts,
        grad_scale,
    )
    taps = conv_weight.shape[0]
    feature_grad = feature_grad.reshape(lat_tile, lon_tile, channels)
    hold = lax.optimization_barrier
    got_a, got_b = flip(away_a, core), flip(away_b, core)

    away_a, away_b = half_sum(kept_a, got_a, first, 1), half_sum(kept_b, got_b, second, 1)
    away_a, away_b, feature_grad = hold((away_a, away_b, feature_grad))
    kept_a, kept_b = half_sum(kept_a, got_a, first, 0), half_sum(kept_b, got_b, second, 0)
    got_a, got_b = flip(away_a, first), flip(away_b, second)
    top, bottom = lat_rims(feature_grad)

    away_a, away_b = half_sum(kept_a, got_a, second, 1), half_sum(kept_b, got_b, first, 1)
    away_a, away_b = hold((away_a, away_b))
    kept_a, kept_b = half_sum(kept_a, got_a, second, 0), half_sum(kept_b, got_b, first, 0)
    got_a, got_b = flip(away_a, second), flip(away_b, first)

    sum_a, sum_b = added(kept_a, got_a), added(kept_b, got_b)
    for step_a, step_b in zip(rest, rest[::-1]):
        sum_a, sum_b, top, bottom = hold((sum_a, sum_b, top, bottom))
        got_a, got_b = flip(sum_a, step_a), flip(sum_b, step_b)
        if step_a == rest[0]:
            left, right = lon_rims(feature_grad, top, bottom)
        sum_a, sum_b = added(sum_a, got_a), added(sum_b, got_b)

    for step_a, step_b in ((second, first), (first, second)):
        sum_a, sum_b = hold((sum_a, sum_b))
        got_a, got_b = flip(sum_a, step_a), flip(sum_b, step_b)
        sum_a = jnp.concatenate([sum_a, got_a], axis=0)
        sum_b = jnp.concatenate([sum_b, got_b], axis=0)
    sum_a, sum_b = hold((sum_a, sum_b))
    got_a, got_b = flip(sum_a, core), flip(sum_b, core)

    padded_grad = close_poles(
        jnp.concatenate(
            [
                left[:, None],
                jnp.concatenate([top, feature_grad, bottom], axis=0),
                right[:, None],
            ],
            axis=1,
        ),
        lat_pos,
        lat_parts,
    )
    latent_grad = conv_apply(padded_grad, conv_weight, lat_tile, lon_tile, True).reshape(
        lat_tile, lon_tile, channels
    )
    totals = unpacked(
        (sum_a, got_a),
        (sum_b, got_b),
        channels,
        width,
        2 * width,
        taps * channels,
    )
    return (
        latent_grad,
        totals[0].reshape(taps, channels, channels),
        *totals[1:4],
        totals[4][None],
        totals[5],
    )


def solution(mesh):
    placed = (
        P("lat", "lon", None),
        P(),
        P(),
        P(),
        P(),
        P(),
        P(),
        P(("lat", "lon")),
        P(("lat", "lon"), None),
        P(None, ("lat", "lon")),
        P(("lat", "lon")),
    )
    return jax.shard_map(
        on_device,
        mesh=mesh,
        in_specs=placed,
        out_specs=(P("lat", "lon", None), P(), P(), P(), P(), P(), P()),
        check_vma=False,
    )
```

```python
import functools

import jax
import jax.numpy as jnp
from jax import lax
from jax.experimental import pallas as pl
from jax.experimental.pallas import tpu as pltpu
from jax.sharding import PartitionSpec as P

BLOCK = 128
LEVELS = 37
SUB = 6


OMEGA = 30.0
TILE = 2048
SPAN = 256
PARTS = 8


def conv_apply(padded, kernel, row_count, col_count, flipped):
    channels = padded.shape[-1]
    result = jnp.zeros((row_count * col_count, kernel.shape[-1]), jnp.float32)
    for shift_a in (-1, 0, 1):
        for shift_b in (-1, 0, 1):
            tap_index = (shift_a + 1) * 3 + shift_b + 1
            if flipped:
                window = padded[
                    1 - shift_a : 1 - shift_a + row_count, 1 - shift_b : 1 - shift_b + col_count
                ]
                matrix = kernel[tap_index].T
            else:
                window = padded[
                    1 + shift_a : 1 + shift_a + row_count, 1 + shift_b : 1 + shift_b + col_count
                ]
                matrix = kernel[tap_index]
            result = result + jnp.dot(
                window.reshape(row_count * col_count, channels),
                matrix,
                preferred_element_type=jnp.float32,
            )
    return result


def close_poles(padded, lat_pos, lat_parts):
    top_rim = jnp.where(lat_pos == 0, jnp.zeros_like(padded[:1]), padded[:1])
    bottom_rim = jnp.where(lat_pos == lat_parts - 1, jnp.zeros_like(padded[-1:]), padded[-1:])
    return jnp.concatenate([top_rim, padded[1:-1], bottom_rim], axis=0)


SIN_TERMS = (
    0.7071067781421408,
    -0.029462767114633488,
    0.0003682722504284759,
    -2.1886040931894034e-06,
    7.195418014521965e-09,
)
COS_TERMS = (
    1.4142134959273227,
    -0.17677635831469551,
    0.0036825740917005817,
    -3.061241565438332e-05,
    1.2789559619534725e-07,
)
TURN = 6.283185307179586
TURN_HIGH = 6.28125
TURN_LOW = TURN - TURN_HIGH
EXTRA = 16
COORD_ROWS = 32
CHUNK = 64
LANES = 128


def sin_cos(angle):
    turns = jnp.round(angle * (1.0 / TURN))
    rest = (angle - turns * TURN_HIGH) - turns * TURN_LOW
    square = rest * rest

    def series(terms):
        value = jnp.full_like(square, terms[-1])
        for term in terms[-2::-1]:
            value = value * square + term
        return value

    half_sin = rest * series(SIN_TERMS)
    half_cos = series(COS_TERMS)
    return half_sin * half_cos, 1.0 - half_sin * half_sin


def pack_kernel(
    owner_ref, grid_ref, cotan_ref, tile_ref, sent_ref, first_row, last_row, first_col, last_col
):
    lat_tile, lon_tile, channels = tile_ref.shape
    first_row[...] = tile_ref[:1]
    last_row[...] = tile_ref[lat_tile - 1 :]
    cells = tile_ref[...].reshape(lat_tile * lon_tile, channels).astype(jnp.float32)
    for column, out_ref in ((0, first_col), (lon_tile - 1, last_col)):
        picked = [
            cells[row * lon_tile + column : row * lon_tile + column + 1]
            for row in range(lat_tile)
        ]
        out_ref[...] = jnp.concatenate(picked, axis=0).astype(out_ref.dtype)
    half = LANES // 2
    lower = lax.broadcasted_iota(jnp.int32, (1, LANES), 1) < half
    sent_ref[...] = jnp.zeros_like(sent_ref)
    for pair in range(owner_ref.shape[0] // 2):
        lanes = slice(pair * LANES, (pair + 1) * LANES)
        grid = grid_ref[:, lanes].astype(jnp.float32)
        values = [grid[0:1], grid[1:2], grid[2:3], cotan_ref[lanes].reshape(1, LANES)]
        turned = [pltpu.roll(value, half, 1) for value in values]
        sent_ref[owner_ref[2 * pair]] = jnp.concatenate(
            [
                jnp.where(lower, values[0], turned[1]),
                jnp.where(lower, values[2], turned[3]),
            ],
            axis=1,
        )
        sent_ref[owner_ref[2 * pair + 1]] = jnp.concatenate(
            [
                jnp.where(lower, turned[0], values[1]),
                jnp.where(lower, turned[2], values[3]),
            ],
            axis=1,
        )


def packed(hit_owner, query_grid, cotangent, latents, slots, group_size):
    lat_tile, lon_tile, channels = latents.shape
    row = jax.ShapeDtypeStruct((1, lon_tile, channels), latents.dtype)
    column = jax.ShapeDtypeStruct((lat_tile, channels), latents.dtype)
    vmem = pl.BlockSpec(memory_space=pltpu.VMEM)
    return pl.pallas_call(
        pack_kernel,
        in_specs=[pl.BlockSpec(memory_space=pltpu.SMEM), vmem, vmem, vmem],
        out_specs=[vmem] * 5,
        out_shape=[
            jax.ShapeDtypeStruct((slots, 1, 4 * group_size), jnp.float32),
            row,
            row,
            column,
            column,
        ],
        name="pack",
    )(hit_owner, query_grid, cotangent, latents)


def fetched(sources, targets, sems):
    copies = [
        pltpu.make_async_copy(source, target, sems.at[index])
        for index, (source, target) in enumerate(zip(sources, targets))
    ]
    for copy in copies:
        copy.start()
    return copies


def weights_kernel(cuts, tile_shape, *refs):
    sources, (weight0, weight1, column_tiles), (*targets, sems) = refs[:5], refs[5:8], refs[8:]
    map_ref, bias_ref, input_ref, hidden_ref, output_ref = targets
    for copy in fetched(sources, targets, sems):
        copy.wait()
    channels = map_ref.shape[0]
    hidden = hidden_ref.shape[0]
    f32, bf16 = jnp.float32, jnp.bfloat16
    lat_cell, lat_sub, lon_cell, lon_sub, level_cut, level_offset = cuts
    lat_offset, lon_offset = tile_offsets(tile_shape, cuts)
    weight0[:, :channels] = map_ref[:, :hidden].T
    bias = bias_ref[...].reshape(1, 2 * hidden)
    lat_weight = OMEGA * input_ref[0:1, :]
    lon_weight = OMEGA * input_ref[1:2, :]
    level_weight = OMEGA * input_ref[2:3, :]
    constant = (
        lat_offset * lat_weight
        + lon_offset * lon_weight
        + level_offset * level_weight
        + bias[:, :hidden]
    )
    zero = jnp.zeros_like(constant)
    coef = jnp.concatenate(
        [
            lat_cell * lat_weight,
            lat_sub * lat_weight,
            lon_cell * lon_weight,
            lon_sub * lon_weight,
            level_cut * level_weight,
            constant,
            zero,
            zero,
        ],
        axis=0,
    )
    high = coef.astype(bf16).astype(f32)
    mid = (coef - high).astype(bf16).astype(f32)
    low = coef - high - mid
    parts = jnp.concatenate([high, mid, low, jnp.zeros((LANES - 24, hidden), f32)], axis=0)
    weight0[:, channels:] = parts.T.astype(bf16)
    weight1[:, :hidden] = hidden_ref[...].T
    weight1[:, hidden:] = map_ref[:, hidden:].T
    column_tiles[:, :LANES] = jnp.broadcast_to(bias[:, hidden:], (LANES, hidden)).T
    column_tiles[:, LANES:] = jnp.broadcast_to(
        output_ref[...].reshape(1, hidden), (LANES, hidden)
    ).T


def tile_offsets(tile_shape, cuts):
    lat_step, lon_step = cuts[1], cuts[3]
    lat_base = 2 * SUB * tile_shape[0] * lax.axis_index("lat") + 1
    lon_base = 2 * SUB * tile_shape[1] * lax.axis_index("lon") + 1
    return (
        lat_base.astype(jnp.float32) * (0.5 * lat_step) - 1.0,
        lon_base.astype(jnp.float32) * (0.5 * lon_step) - 1.0,
    )


def prepared_weights(
    tile_shape, map_weight, map_bias, input_weight, hidden_weight, output_weight, cuts
):
    channels = map_weight.shape[0]
    hidden = hidden_weight.shape[0]
    sources = (map_weight, map_bias, input_weight, hidden_weight, output_weight)
    vmem = pl.BlockSpec(memory_space=pltpu.VMEM)
    return pl.pallas_call(
        functools.partial(weights_kernel, cuts, tile_shape),
        in_specs=[pl.BlockSpec(memory_space=pltpu.HBM)] * 5,
        out_specs=[vmem] * 3,
        out_shape=[
            jax.ShapeDtypeStruct((hidden, channels + LANES), jnp.bfloat16),
            jax.ShapeDtypeStruct((hidden, hidden + channels), jnp.bfloat16),
            jax.ShapeDtypeStruct((hidden, 2 * LANES), jnp.float32),
        ],
        scratch_shapes=[pltpu.VMEM(value.shape, value.dtype) for value in sources]
        + [pltpu.SemaphoreType.DMA((5,))],
        name="weights",
    )(*sources)


def query_kernel(
    cuts,
    scale,
    taps,
    single,
    serve_hbm,
    got_ref,
    tile_hbm,
    top_ref,
    bottom_ref,
    left_ref,
    right_ref,
    conv_hbm,
    map_hbm,
    hidden_hbm,
    weight0_hbm,
    weight1_hbm,
    columns_hbm,
    kept_ref,
    away_ref,
    conv_kept_ref,
    conv_away_ref,
    feature_grad_ref,
    serve_ref,
    tile_ref,
    conv_ref,
    map_ref,
    hidden_ref,
    weight0,
    weight1,
    column_tiles,
    sems,
    windows,
    turned,
    shifted,
    fields,
    feat_t,
    stack0,
    lefts,
    pre0,
    pre1,
    cos0,
    rounded0,
    rounded1,
    sums,
    later_sums,
    out_sums,
):
    step = pl.program_id(0)
    lat_tile, lon_tile, channels = tile_ref.shape
    cells = lat_tile * lon_tile
    hidden = hidden_ref.shape[0]
    block = rounded0.shape[1]
    left_rows = cells + EXTRA
    f32, bf16 = jnp.float32, jnp.bfloat16
    lat_cell, lat_sub, lon_cell, lon_sub, level_cut, level_offset = cuts
    lat_pos = lax.axis_index("lat")
    bit = lax.axis_index("lon") & 1
    lat_offset, lon_offset = tile_offsets((lat_tile, lon_tile), cuts)

    @pl.when(step == 0)
    def _():
        copies = fetched(
            (
                tile_hbm,
                serve_hbm,
                conv_hbm,
                weight0_hbm,
                weight1_hbm,
                columns_hbm,
                hidden_hbm,
                map_hbm,
            ),
            (
                tile_ref,
                serve_ref,
                conv_ref,
                weight0,
                weight1,
                column_tiles,
                hidden_ref,
                map_ref,
            ),
            sems,
        )
        copies[1].wait()
        half = LANES // 2
        lower = lax.broadcasted_iota(jnp.int32, (1, LANES), 1) < half
        for pair in range(got_ref.shape[0] // 2):
            even, odd = got_ref[2 * pair], got_ref[2 * pair + 1]
            row = slice(pair, pair + 1)
            for place in range(2):
                lanes = slice(place * LANES, (place + 1) * LANES)
                near, far = even[:, lanes], odd[:, lanes]
                fields[2 * place, row, :] = jnp.where(lower, near, pltpu.roll(far, half, 1))
                fields[2 * place + 1, row, :] = jnp.where(lower, pltpu.roll(near, half, 1), far)
            serve = jnp.where(lower, serve_ref[0, 2 * pair], serve_ref[0, 2 * pair + 1])
            fields[4, row, :] = serve.astype(f32)
        serve = fields[4]
        tile_cell = jnp.where(serve < 0.0, -1.0, serve * float(BLOCK) + fields[0])
        cell_row = jnp.floor((tile_cell + 0.5) * (1.0 / lon_tile))
        sub = fields[1]
        sub_row = jnp.floor((sub + 0.5) * (1.0 / SUB))
        fields[0] = tile_cell
        fields[1] = cell_row
        fields[4] = sub_row
        fields[5] = tile_cell - cell_row * float(lon_tile)
        fields[6] = sub - sub_row * float(SUB)

        copies[0].wait()
        flat = jnp.concatenate(
            [top_ref[0], tile_ref[...].reshape(cells, channels), bottom_ref[0]], axis=0
        )
        first = jnp.where(lat_pos == 0, 0.0, 1.0)
        last = jnp.where(lat_pos == lax.axis_size("lat") - 1, 0.0, 1.0)
        ends = cells + lon_tile

        def keep(slot, values):
            windows[slot, :lon_tile, :] = (values[:lon_tile] * first).astype(bf16)
            windows[slot, lon_tile:ends, :] = values[lon_tile:ends].astype(bf16)
            windows[slot, ends:, :] = (values[ends:] * last).astype(bf16)

        flat = flat.astype(f32)
        total_rows = flat.shape[0]
        keep(1, flat)
        left = left_ref[...].astype(f32)
        right = right_ref[...].astype(f32)
        shifted[...] = pltpu.roll(flat, 1, 0)
        for row in range(lat_tile + 2):
            shifted[row * lon_tile : row * lon_tile + 1, :] = left[row : row + 1]
        keep(0, shifted[...])
        shifted[...] = pltpu.roll(flat, total_rows - 1, 0)
        for row in range(1, lat_tile + 3):
            shifted[row * lon_tile - 1 : row * lon_tile, :] = right[row - 1 : row]
        keep(2, shifted[...])
        for tap in range(taps):
            top = tap // 3 * lon_tile
            turned[tap] = windows[tap % 3, top : top + cells, :].T
        copies[2].wait()
        features = jnp.zeros((cells, channels), f32)
        for tap in range(taps):
            top = tap // 3 * lon_tile
            features = features + jnp.dot(
                windows[tap % 3, top : top + cells, :], conv_ref[tap], preferred_element_type=f32
            )
        feat_t[...] = features.T.astype(bf16)

        for copy in copies[3:]:
            copy.wait()
        stack0[...] = jnp.zeros_like(stack0)
        if not single:
            sums[...] = jnp.zeros_like(sums)
            later_sums[...] = jnp.zeros_like(later_sums)
        out_sums[...] = jnp.zeros_like(out_sums)

    ids = lax.broadcasted_iota(jnp.int32, (cells, LANES), 0)
    strips = block // LANES
    for strip in range(strips):
        row = pl.ds(step * strips + strip, 1)
        lanes = slice(strip * LANES, (strip + 1) * LANES)
        cell = fields[0, row, :].astype(jnp.int32)
        lefts[:cells, lanes] = jnp.where(ids == cell, 1.0, 0.0).astype(bf16)
        one = jnp.ones((1, LANES), f32)
        group = jnp.concatenate(
            [
                fields[1, row, :],
                fields[4, row, :],
                fields[5, row, :],
                fields[6, row, :],
                fields[2, row, :],
                one,
                jnp.zeros((2, LANES), f32),
            ],
            axis=0,
        )
        coords = jnp.concatenate([group, group, group, jnp.zeros_like(group)], axis=0).astype(
            bf16
        )
        stack0[channels : channels + COORD_ROWS, lanes] = coords
        lefts[cells:left_rows, lanes] = coords[:EXTRA]
    across = (((1,), (1,)), ((), ()))
    spans = block // SPAN
    acts = left_rows + hidden

    def span(index):
        return slice(index * SPAN, (index + 1) * SPAN)

    def first_dots(index):
        lanes = span(index)
        queried = jnp.dot(feat_t[...], lefts[:cells, lanes], preferred_element_type=f32)
        queried = queried.astype(bf16)
        stack0[:channels, lanes] = queried
        lefts[acts:, lanes] = queried
        pre0[:, lanes] = jnp.dot(weight0[...], stack0[:, lanes], preferred_element_type=f32)

    def first_sines(index):
        for top in range(0, hidden, CHUNK):
            for left in range(index * SPAN, (index + 1) * SPAN, LANES):
                at = (slice(top, top + CHUNK), slice(left, left + LANES))
                sine, cosine = sin_cos(pre0[at])
                lefts[left_rows + top : left_rows + top + CHUNK, at[1]] = sine.astype(bf16)
                cos0[at] = cosine

    def second_dots(index):
        lanes = span(index)
        pre1[:, lanes] = jnp.dot(
            weight1[...], lefts[left_rows:, lanes], preferred_element_type=f32
        )

    def second_sines(index):
        for top in range(0, hidden, CHUNK):
            rows = slice(top, top + CHUNK)
            bias = column_tiles[rows, :LANES]
            out_weight = column_tiles[rows, LANES:]
            total = out_sums[rows, :]
            for left in range(index * SPAN, (index + 1) * SPAN, LANES):
                at = (rows, slice(left, left + LANES))
                cotan = fields[3, pl.ds(step * strips + left // LANES, 1), :]
                sine, cosine = sin_cos(pre1[at] + bias)
                total = total + sine * cotan
                rounded1[at] = (out_weight * cotan * cosine).astype(bf16)
            out_sums[rows, :] = total

    def third_dots(index):
        lanes = span(index)
        act_grad = jnp.dot(hidden_ref[...], rounded1[:, lanes], preferred_element_type=f32)
        rounded0[:, lanes] = (act_grad * cos0[:, lanes]).astype(bf16)

    def joins(lanes):
        later = lax.dot_general(
            lefts[:acts, lanes], rounded1[:, lanes], across, preferred_element_type=f32
        )
        early = lax.dot_general(
            lefts[:left_rows, lanes], rounded0[:, lanes], across, preferred_element_type=f32
        )
        if single:
            later_sums[...] = later
            sums[...] = early
        else:
            later_sums[...] += later
            sums[...] += early

    first_dots(0)
    for turn in range(spans + 2):
        if turn + 1 < spans:
            first_dots(turn + 1)
        if turn < spans:
            first_sines(turn)
            second_dots(turn)
        if 0 <= turn - 1 < spans:
            second_sines(turn - 1)
            third_dots(turn - 1)
    joins(slice(0, block))

    @pl.when(step == pl.num_programs(0) - 1)
    def _():
        cell_sums = jnp.concatenate([sums[:cells, :], later_sums[:cells, :]], axis=1)
        upper = cell_sums.astype(bf16)
        lower = (cell_sums - upper.astype(f32)).astype(bf16)
        map_grad = (
            jnp.dot(feat_t[...], upper, preferred_element_type=f32)
            + jnp.dot(feat_t[...], lower, preferred_element_type=f32)
        ) * scale
        feature_grad = (
            lax.dot_general(upper, map_ref[...], across, preferred_element_type=f32)
            + lax.dot_general(lower, map_ref[...], across, preferred_element_type=f32)
        ).astype(bf16)
        feature_grad_ref[...] = feature_grad
        hidden_grad = later_sums[left_rows:, :] * scale
        extra = sums[cells : cells + 8, :]
        later_bias = later_sums[cells + 5 : cells + 6, :]
        total = extra[5:6, :]
        lat_grad = (
            lat_cell * extra[0:1, :] + lat_sub * extra[1:2, :] + lat_offset * total
        )
        lon_grad = (
            lon_cell * extra[2:3, :] + lon_sub * extra[3:4, :] + lon_offset * total
        )
        level_grad = level_cut * extra[4:5, :] + level_offset * total
        out_grad = jnp.sum(out_sums[...].T, axis=0, keepdims=True)
        gain = OMEGA * scale
        small = jnp.concatenate(
            [
                jnp.concatenate([total, later_bias], axis=1) * scale,
                jnp.concatenate([lat_grad, lon_grad], axis=1) * gain,
                jnp.concatenate([level_grad * gain, out_grad * scale], axis=1),
                jnp.zeros((EXTRA - 3, 2 * hidden), f32),
            ],
            axis=0,
        )
        folds = hidden // LANES

        def share(part):
            lanes = slice(part * LANES, (part + 1) * LANES)
            top = part // folds * channels
            left = part % folds * LANES
            return (
                map_grad[:, lanes],
                hidden_grad[top : top + channels, left : left + LANES],
                small[:, lanes],
            )

        half = PARTS // 2
        places = (
            slice(0, channels),
            slice(channels, 2 * channels),
            slice(2 * channels, 2 * channels + EXTRA),
        )
        for part in range(half):
            for place, low, high in zip(places, share(part), share(part + half)):
                kept_ref[part, place, :] = jnp.where(bit == 0, low, high).astype(bf16)
                away_ref[part, place, :] = jnp.where(bit == 0, high, low).astype(bf16)

        rows = taps * channels // PARTS
        for tap in range(taps):
            grad = jnp.dot(turned[tap], feature_grad, preferred_element_type=f32)
            grad = (grad * scale).astype(bf16)
            start = tap * channels
            while start < (tap + 1) * channels:
                end = min((start // rows + 1) * rows, (tap + 1) * channels)
                inside = slice(start % rows, start % rows + end - start)
                value = grad[start - tap * channels : end - tap * channels]
                part = start // rows

                @pl.when(bit == part // half)
                def _():
                    conv_kept_ref[part % half, inside, :] = value

                @pl.when(bit != part // half)
                def _():
                    conv_away_ref[part % half, inside, :] = value

                start = end


def query_pass(
    serve_block,
    got,
    latents,
    rims,
    conv_weight,
    map_weight,
    hidden_weight,
    weights,
    cuts,
    scale,
):
    lat_tile, lon_tile, channels = latents.shape
    cells = lat_tile * lon_tile
    taps = conv_weight.shape[0]
    slots = got.shape[0]
    queries = slots * got.shape[2] // 4
    hidden = hidden_weight.shape[0]
    block = min(TILE, queries)
    f32, bf16 = jnp.float32, jnp.bfloat16
    hbm = pl.BlockSpec(memory_space=pltpu.HBM)
    vmem = pl.BlockSpec(memory_space=pltpu.VMEM)
    share = (PARTS // 2, 2 * channels + EXTRA, LANES)
    conv_share = (PARTS // 2, taps * channels // PARTS, channels)

    return pl.pallas_call(
        functools.partial(query_kernel, cuts, scale, taps, queries == block),
        grid=(queries // block,),
        in_specs=[hbm, vmem, hbm] + [vmem] * 4 + [hbm] * 6,
        out_specs=[vmem] * 5,
        out_shape=[
            jax.ShapeDtypeStruct(share, bf16),
            jax.ShapeDtypeStruct(share, bf16),
            jax.ShapeDtypeStruct(conv_share, bf16),
            jax.ShapeDtypeStruct(conv_share, bf16),
            jax.ShapeDtypeStruct((cells, channels), bf16),
        ],
        scratch_shapes=[
            pltpu.SMEM(serve_block.shape, jnp.int32),
            pltpu.VMEM(latents.shape, bf16),
            pltpu.VMEM(conv_weight.shape, bf16),
            pltpu.VMEM(map_weight.shape, bf16),
            pltpu.VMEM(hidden_weight.shape, bf16),
            *[pltpu.VMEM(value.shape, value.dtype) for value in weights],
            pltpu.SemaphoreType.DMA((8,)),
            pltpu.VMEM((3, cells + 2 * lon_tile, channels), bf16),
            pltpu.VMEM((taps, channels, cells), bf16),
            pltpu.VMEM((cells + 2 * lon_tile, channels), f32),
            pltpu.VMEM((7, slots // 2, LANES), f32),
            pltpu.VMEM((channels, cells), bf16),
            pltpu.VMEM((channels + LANES, block), bf16),
            pltpu.VMEM((cells + EXTRA + hidden + channels, block), bf16),
            pltpu.VMEM((hidden, block), f32),
            pltpu.VMEM((hidden, block), f32),
            pltpu.VMEM((hidden, block), f32),
            pltpu.VMEM((hidden, block), bf16),
            pltpu.VMEM((hidden, block), bf16),
            pltpu.VMEM((cells + EXTRA, hidden), f32),
            pltpu.VMEM((cells + EXTRA + hidden, hidden), f32),
            pltpu.VMEM((hidden, LANES), f32),
        ],
        compiler_params=pltpu.CompilerParams(vmem_limit_bytes=56 * 1000 * 1000),
        name="queries",
    )(
        serve_block,
        got,
        latents,
        *rims,
        conv_weight,
        map_weight,
        hidden_weight,
        *weights,
    )


def bits_of(axis):
    return lax.axis_size(axis).bit_length() - 1


def flip(values, step):
    axis, bit = step
    count = lax.axis_size(axis)
    return lax.ppermute(values, axis, [(i, i ^ (1 << bit)) for i in range(count)])


def own_bit(step):
    axis, bit = step
    return (lax.axis_index(axis) >> bit) & 1


def added(left, right):
    return (left.astype(jnp.float32) + right.astype(jnp.float32)).astype(left.dtype)


def half_sum(kept, got, step, other):
    def pick(values):
        halves = values.reshape((2, values.shape[0] // 2) + values.shape[1:])
        mine = own_bit(step)
        place = 1 - mine if other else mine
        return lax.dynamic_index_in_dim(halves, place, 0, keepdims=False)

    return added(pick(kept), pick(got))


def ring(axis, turn):
    count = lax.axis_size(axis)
    return [(i, (i + turn) % count) for i in range(count)]


def lat_rims(first_row, last_row):
    top = lax.ppermute(last_row, "lat", ring("lat", 1))
    bottom = lax.ppermute(first_row, "lat", ring("lat", -1))
    return top, bottom


def lon_rims(first_col, last_col, top, bottom):
    last = jnp.concatenate([top[:, -1], last_col, bottom[:, -1]], axis=0)
    first = jnp.concatenate([top[:, 0], first_col, bottom[:, 0]], axis=0)
    left = lax.ppermute(last, "lon", ring("lon", 1))
    right = lax.ppermute(first, "lon", ring("lon", -1))
    return left, right


def unpack_kernel(
    mine_a,
    theirs_a,
    mine_b,
    theirs_b,
    conv_ref,
    map_ref,
    bias_ref,
    input_ref,
    hidden_ref,
    out_ref,
):
    f32 = jnp.float32
    channels = map_ref.shape[0]
    folds = hidden_ref.shape[1] // LANES
    half = PARTS // 2
    lon_pos = lax.axis_index("lon")
    bit, bit_first, bit_second = lon_pos & 1, (lon_pos >> 1) & 1, (lon_pos >> 2) & 1

    def place(part, upper_bit, lower_bit):
        upper = 1 - upper_bit if part // 2 % 2 else upper_bit
        lower = 1 - lower_bit if part % 2 else lower_bit
        return upper * 2 + lower

    def fill(low_a, high_a, low_b, high_b):
        for part in range(PARTS):
            source = (low_a if part < half else high_a).at[place(part, bit_first, bit_second)]
            lanes = slice(part * LANES, (part + 1) * LANES)
            top = part // folds * channels
            left = part % folds * LANES
            map_ref[:, lanes] = source[:channels, :].astype(f32)
            hidden_ref[top : top + channels, left : left + LANES] = source[
                channels : 2 * channels, :
            ].astype(f32)
            small = source[2 * channels :, :].astype(f32)
            bias_ref[lanes] = small[0, :]
            side = slice(left, left + LANES)
            input_ref[part // folds, side] = small[1, :]
            if part < folds:
                input_ref[2, side] = small[2, :]
            else:
                out_ref[side] = small[2, :]
            source = (low_b if part < half else high_b).at[place(part, bit_second, bit_first)]
            rows = source.shape[0]
            conv_ref[part * rows : (part + 1) * rows, :] = source[...].astype(f32)

    @pl.when(bit == 0)
    def _():
        fill(mine_a, theirs_a, mine_b, theirs_b)

    @pl.when(bit == 1)
    def _():
        fill(theirs_a, mine_a, theirs_b, mine_b)


def unpacked(pair_a, pair_b, channels, hidden, width, conv_rows):
    f32 = jnp.float32
    vmem = pl.BlockSpec(memory_space=pltpu.VMEM)
    return pl.pallas_call(
        unpack_kernel,
        in_specs=[vmem] * 4,
        out_specs=[vmem] * 6,
        out_shape=[
            jax.ShapeDtypeStruct((conv_rows, channels), f32),
            jax.ShapeDtypeStruct((channels, width), f32),
            jax.ShapeDtypeStruct((width,), f32),
            jax.ShapeDtypeStruct((3, hidden), f32),
            jax.ShapeDtypeStruct((hidden, hidden), f32),
            jax.ShapeDtypeStruct((hidden,), f32),
        ],
        compiler_params=pltpu.CompilerParams(vmem_limit_bytes=20 * 1024 * 1024),
        name="unpack",
    )(*pair_a, *pair_b)


def on_device(
    latents,
    conv_weight,
    map_weight,
    map_bias,
    input_weight,
    hidden_weight,
    output_weight,
    hit_owner,
    serve_block,
    query_grid,
    cotangent,
):
    lat_tile, lon_tile, channels = latents.shape
    lat_parts = lax.axis_size("lat")
    lon_parts = lax.axis_size("lon")
    dev_count = lat_parts * lon_parts
    lat_cells = lat_tile * lat_parts
    lon_cells = lon_tile * lon_parts
    lat_pos = lax.axis_index("lat")
    hit_count = hit_owner.shape[0]
    group_size = cotangent.shape[0] // hit_count
    width = input_weight.shape[1]
    steps = [(axis, bit) for axis in ("lon", "lat") for bit in range(bits_of(axis))]
    core, first, second = steps[:3]
    rest = steps[3:]
    cuts = (
        2.0 / lat_cells,
        2.0 / (lat_cells * SUB),
        2.0 / lon_cells,
        2.0 / (lon_cells * SUB),
        2.0 / LEVELS,
        1.0 / LEVELS - 1.0,
    )
    grad_scale = float(hit_count * group_size * dev_count) ** (-0.5)
    sent, first_row, last_row, first_col, last_col = packed(
        hit_owner, query_grid, cotangent, latents, dev_count, group_size
    )
    sent, late_map = lax.optimization_barrier((sent, map_weight))
    got = lax.all_to_all(sent, ("lat", "lon"), split_axis=0, concat_axis=0, tiled=True)
    top, bottom = lat_rims(first_row, last_row)
    rims = (top, bottom, *lon_rims(first_col, last_col, top, bottom))
    weights = prepared_weights(
        (lat_tile, lon_tile),
        late_map,
        map_bias,
        input_weight,
        hidden_weight[0],
        output_weight,
        cuts,
    )
    kept_a, away_a, kept_b, away_b, feature_grad = query_pass(
        serve_block,
        got,
        latents,
        rims,
        conv_weight,
        map_weight,
        hidden_weight[0],
        weights,
        cuts,
        grad_scale,
    )
    taps = conv_weight.shape[0]
    feature_grad = feature_grad.reshape(lat_tile, lon_tile, channels)
    hold = lax.optimization_barrier
    got_a, got_b = flip(away_a, core), flip(away_b, core)

    away_a, away_b = half_sum(kept_a, got_a, first, 1), half_sum(kept_b, got_b, second, 1)
    away_a, away_b, feature_grad = hold((away_a, away_b, feature_grad))
    kept_a, kept_b = half_sum(kept_a, got_a, first, 0), half_sum(kept_b, got_b, second, 0)
    got_a, got_b = flip(away_a, first), flip(away_b, second)
    top, bottom = lat_rims(feature_grad[:1], feature_grad[-1:])

    away_a, away_b = half_sum(kept_a, got_a, second, 1), half_sum(kept_b, got_b, first, 1)
    away_a, away_b = hold((away_a, away_b))
    kept_a, kept_b = half_sum(kept_a, got_a, second, 0), half_sum(kept_b, got_b, first, 0)
    got_a, got_b = flip(away_a, second), flip(away_b, first)

    sum_a, sum_b = added(kept_a, got_a), added(kept_b, got_b)
    for step_a, step_b in zip(rest, rest[::-1]):
        sum_a, sum_b, top, bottom = hold((sum_a, sum_b, top, bottom))
        got_a = flip(sum_a, step_a)
        got_b = flip(sum_b, step_b)
        if step_a == rest[0]:
            left, right = lon_rims(feature_grad[:, 0], feature_grad[:, -1], top, bottom)
        sum_a, sum_b = added(sum_a, got_a), added(sum_b, got_b)

    for step_a, step_b in ((second, first), (first, second)):
        sum_a, sum_b = hold((sum_a, sum_b))
        got_a = flip(sum_a, step_a)
        got_b = flip(sum_b, step_b)
        sum_a = jnp.concatenate([sum_a, got_a], axis=0)
        sum_b = jnp.concatenate([sum_b, got_b], axis=0)
    sum_a, sum_b = hold((sum_a, sum_b))
    got_a, got_b = flip(sum_a, core), flip(sum_b, core)

    padded_grad = close_poles(
        jnp.concatenate(
            [
                left[:, None],
                jnp.concatenate([top, feature_grad, bottom], axis=0),
                right[:, None],
            ],
            axis=1,
        ),
        lat_pos,
        lat_parts,
    )
    latent_grad = conv_apply(padded_grad, conv_weight, lat_tile, lon_tile, True).reshape(
        lat_tile, lon_tile, channels
    )
    totals = unpacked(
        (sum_a, got_a),
        (sum_b, got_b),
        channels,
        width,
        2 * width,
        taps * channels,
    )
    return (
        latent_grad,
        totals[0].reshape(taps, channels, channels),
        *totals[1:4],
        totals[4][None],
        totals[5],
    )


def solution(mesh):
    placed = (
        P("lat", "lon", None),
        P(),
        P(),
        P(),
        P(),
        P(),
        P(),
        P(("lat", "lon")),
        P(("lat", "lon"), None),
        P(None, ("lat", "lon")),
        P(("lat", "lon")),
    )
    return jax.shard_map(
        on_device,
        mesh=mesh,
        in_specs=placed,
        out_specs=(P("lat", "lon", None), P(), P(), P(), P(), P(), P()),
        check_vma=False,
    )
```

```python
import functools

import jax
import jax.numpy as jnp
from jax import lax
from jax.experimental import pallas as pl
from jax.experimental.pallas import tpu as pltpu
from jax.sharding import PartitionSpec as P

BLOCK = 128
LEVELS = 37
SUB = 6


OMEGA = 30.0
TILE = 2048
SPAN = 256
PARTS = 8


def conv_apply(padded, kernel, row_count, col_count, flipped):
    channels = padded.shape[-1]
    result = jnp.zeros((row_count * col_count, kernel.shape[-1]), jnp.float32)
    for shift_a in (-1, 0, 1):
        for shift_b in (-1, 0, 1):
            tap_index = (shift_a + 1) * 3 + shift_b + 1
            if flipped:
                window = padded[
                    1 - shift_a : 1 - shift_a + row_count, 1 - shift_b : 1 - shift_b + col_count
                ]
                matrix = kernel[tap_index].T
            else:
                window = padded[
                    1 + shift_a : 1 + shift_a + row_count, 1 + shift_b : 1 + shift_b + col_count
                ]
                matrix = kernel[tap_index]
            result = result + jnp.dot(
                window.reshape(row_count * col_count, channels),
                matrix,
                preferred_element_type=jnp.float32,
            )
    return result


def close_poles(padded, lat_pos, lat_parts):
    top_rim = jnp.where(lat_pos == 0, jnp.zeros_like(padded[:1]), padded[:1])
    bottom_rim = jnp.where(lat_pos == lat_parts - 1, jnp.zeros_like(padded[-1:]), padded[-1:])
    return jnp.concatenate([top_rim, padded[1:-1], bottom_rim], axis=0)


SIN_TERMS = (
    0.7071067781421408,
    -0.029462767114633488,
    0.0003682722504284759,
    -2.1886040931894034e-06,
    7.195418014521965e-09,
)
COS_TERMS = (
    1.4142134959273227,
    -0.17677635831469551,
    0.0036825740917005817,
    -3.061241565438332e-05,
    1.2789559619534725e-07,
)
TURN = 6.283185307179586
TURN_HIGH = 6.28125
TURN_LOW = TURN - TURN_HIGH
EXTRA = 16
COORD_ROWS = 32
CHUNK = 64
LANES = 128


def sin_cos(angle):
    turns = jnp.round(angle * (1.0 / TURN))
    rest = (angle - turns * TURN_HIGH) - turns * TURN_LOW
    square = rest * rest

    def series(terms):
        value = jnp.full_like(square, terms[-1])
        for term in terms[-2::-1]:
            value = value * square + term
        return value

    half_sin = rest * series(SIN_TERMS)
    half_cos = series(COS_TERMS)
    return half_sin * half_cos, 1.0 - half_sin * half_sin


def pack_kernel(
    cuts,
    owner_ref,
    grid_ref,
    cotan_ref,
    tile_ref,
    bias_ref,
    input_ref,
    output_ref,
    sent_ref,
    first_row,
    last_row,
    first_col,
    last_col,
    coef_out,
):
    lat_tile, lon_tile, channels = tile_ref.shape
    coef_kernel(cuts, (lat_tile, lon_tile), bias_ref, input_ref, output_ref, coef_out)
    first_row[...] = tile_ref[:1]
    last_row[...] = tile_ref[lat_tile - 1 :]
    cells = tile_ref[...].reshape(lat_tile * lon_tile, channels).astype(jnp.float32)
    for column, out_ref in ((0, first_col), (lon_tile - 1, last_col)):
        picked = [
            cells[row * lon_tile + column : row * lon_tile + column + 1]
            for row in range(lat_tile)
        ]
        out_ref[...] = jnp.concatenate(picked, axis=0).astype(out_ref.dtype)
    half = LANES // 2
    lower = lax.broadcasted_iota(jnp.int32, (1, LANES), 1) < half
    sent_ref[...] = jnp.zeros_like(sent_ref)
    for pair in range(owner_ref.shape[0] // 2):
        lanes = slice(pair * LANES, (pair + 1) * LANES)
        grid = grid_ref[:, lanes].astype(jnp.float32)
        values = [grid[0:1], grid[1:2], grid[2:3], cotan_ref[lanes].reshape(1, LANES)]
        turned = [pltpu.roll(value, half, 1) for value in values]
        sent_ref[owner_ref[2 * pair]] = jnp.concatenate(
            [
                jnp.where(lower, values[0], turned[1]),
                jnp.where(lower, values[2], turned[3]),
            ],
            axis=1,
        )
        sent_ref[owner_ref[2 * pair + 1]] = jnp.concatenate(
            [
                jnp.where(lower, turned[0], values[1]),
                jnp.where(lower, turned[2], values[3]),
            ],
            axis=1,
        )


def packed(hit_owner, query_grid, cotangent, latents, params, cuts, slots, group_size):
    lat_tile, lon_tile, channels = latents.shape
    row = jax.ShapeDtypeStruct((1, lon_tile, channels), latents.dtype)
    column = jax.ShapeDtypeStruct((lat_tile, channels), latents.dtype)
    vmem = pl.BlockSpec(memory_space=pltpu.VMEM)
    return pl.pallas_call(
        functools.partial(pack_kernel, cuts),
        in_specs=[pl.BlockSpec(memory_space=pltpu.SMEM)] + [vmem] * 6,
        out_specs=[vmem] * 6,
        out_shape=[
            jax.ShapeDtypeStruct((slots, 1, 4 * group_size), jnp.float32),
            row,
            row,
            column,
            column,
            jax.ShapeDtypeStruct((16, params[1].shape[1]), jnp.float32),
        ],
        name="pack",
    )(hit_owner, query_grid, cotangent, latents, *params)


def fetched(sources, targets, sems):
    copies = [
        pltpu.make_async_copy(source, target, sems.at[index])
        for index, (source, target) in enumerate(zip(sources, targets))
    ]
    for copy in copies:
        copy.start()
    return copies


def coef_kernel(cuts, tile_shape, bias_ref, input_ref, output_ref, coef_out):
    hidden = input_ref.shape[1]
    lat_cell, lat_sub, lon_cell, lon_sub, level_cut, level_offset = cuts
    lat_offset, lon_offset = tile_offsets(tile_shape, cuts)
    bias = bias_ref[...].reshape(1, 2 * hidden)
    lat_weight = OMEGA * input_ref[0:1, :]
    lon_weight = OMEGA * input_ref[1:2, :]
    level_weight = OMEGA * input_ref[2:3, :]
    constant = (
        lat_offset * lat_weight
        + lon_offset * lon_weight
        + level_offset * level_weight
        + bias[:, :hidden]
    )
    zero = jnp.zeros_like(constant)
    coef = jnp.concatenate(
        [
            lat_cell * lat_weight,
            lat_sub * lat_weight,
            lon_cell * lon_weight,
            lon_sub * lon_weight,
            level_cut * level_weight,
            constant,
            zero,
            zero,
        ],
        axis=0,
    )
    coef_out[...] = jnp.concatenate(
        [coef, bias[:, hidden:], output_ref[...].reshape(1, hidden)] + [zero] * 6, axis=0
    )


def prepare_weights(map_ref, hidden_ref, coef_ref, weight0, weight1, column_tiles):
    channels = map_ref.shape[0]
    hidden = hidden_ref.shape[0]
    f32, bf16 = jnp.float32, jnp.bfloat16
    weight0[:, :channels] = map_ref[:, :hidden].T
    coef = coef_ref[:8]
    high = coef.astype(bf16).astype(f32)
    mid = (coef - high).astype(bf16).astype(f32)
    low = coef - high - mid
    parts = jnp.concatenate([high, mid, low, jnp.zeros((LANES - 24, hidden), f32)], axis=0)
    weight0[:, channels:] = parts.T.astype(bf16)
    weight1[:, :hidden] = hidden_ref[...].T
    weight1[:, hidden:] = map_ref[:, hidden:].T
    column_tiles[:, :LANES] = jnp.broadcast_to(coef_ref[8:9], (LANES, hidden)).T
    column_tiles[:, LANES:] = jnp.broadcast_to(coef_ref[9:10], (LANES, hidden)).T


def tile_offsets(tile_shape, cuts):
    lat_step, lon_step = cuts[1], cuts[3]
    lat_base = 2 * SUB * tile_shape[0] * lax.axis_index("lat") + 1
    lon_base = 2 * SUB * tile_shape[1] * lax.axis_index("lon") + 1
    return (
        lat_base.astype(jnp.float32) * (0.5 * lat_step) - 1.0,
        lon_base.astype(jnp.float32) * (0.5 * lon_step) - 1.0,
    )


def query_kernel(
    cuts,
    scale,
    taps,
    single,
    serve_hbm,
    got_ref,
    tile_hbm,
    top_ref,
    bottom_ref,
    left_ref,
    right_ref,
    conv_hbm,
    map_hbm,
    hidden_hbm,
    coef_hbm,
    kept_ref,
    away_ref,
    conv_kept_ref,
    conv_away_ref,
    feature_grad_ref,
    serve_ref,
    tile_ref,
    conv_ref,
    map_ref,
    hidden_ref,
    coef_ref,
    weight0,
    weight1,
    column_tiles,
    sems,
    windows,
    turned,
    shifted,
    fields,
    feat_t,
    stack0,
    lefts,
    pre0,
    pre1,
    cos0,
    rounded0,
    rounded1,
    sums,
    later_sums,
    out_sums,
):
    step = pl.program_id(0)
    lat_tile, lon_tile, channels = tile_ref.shape
    cells = lat_tile * lon_tile
    hidden = hidden_ref.shape[0]
    block = rounded0.shape[1]
    left_rows = cells + EXTRA
    f32, bf16 = jnp.float32, jnp.bfloat16
    lat_cell, lat_sub, lon_cell, lon_sub, level_cut, level_offset = cuts
    lat_pos = lax.axis_index("lat")
    bit = lax.axis_index("lon") & 1
    lat_offset, lon_offset = tile_offsets((lat_tile, lon_tile), cuts)

    @pl.when(step == 0)
    def _():
        copies = fetched(
            (
                tile_hbm,
                serve_hbm,
                map_hbm,
                hidden_hbm,
                coef_hbm,
                conv_hbm,
            ),
            (
                tile_ref,
                serve_ref,
                map_ref,
                hidden_ref,
                coef_ref,
                conv_ref,
            ),
            sems,
        )
        copies[1].wait()
        half = LANES // 2
        lower = lax.broadcasted_iota(jnp.int32, (1, LANES), 1) < half
        for pair in range(got_ref.shape[0] // 2):
            even, odd = got_ref[2 * pair], got_ref[2 * pair + 1]
            row = slice(pair, pair + 1)
            for place in range(2):
                lanes = slice(place * LANES, (place + 1) * LANES)
                near, far = even[:, lanes], odd[:, lanes]
                fields[2 * place, row, :] = jnp.where(lower, near, pltpu.roll(far, half, 1))
                fields[2 * place + 1, row, :] = jnp.where(lower, pltpu.roll(near, half, 1), far)
            serve = jnp.where(lower, serve_ref[0, 2 * pair], serve_ref[0, 2 * pair + 1])
            fields[4, row, :] = serve.astype(f32)
        serve = fields[4]
        tile_cell = jnp.where(serve < 0.0, -1.0, serve * float(BLOCK) + fields[0])
        cell_row = jnp.floor((tile_cell + 0.5) * (1.0 / lon_tile))
        sub = fields[1]
        sub_row = jnp.floor((sub + 0.5) * (1.0 / SUB))
        fields[0] = tile_cell
        fields[1] = cell_row
        fields[4] = sub_row
        fields[5] = tile_cell - cell_row * float(lon_tile)
        fields[6] = sub - sub_row * float(SUB)

        copies[0].wait()
        flat = jnp.concatenate(
            [top_ref[0], tile_ref[...].reshape(cells, channels), bottom_ref[0]], axis=0
        )
        first = jnp.where(lat_pos == 0, 0.0, 1.0)
        last = jnp.where(lat_pos == lax.axis_size("lat") - 1, 0.0, 1.0)
        ends = cells + lon_tile

        def keep(slot, values):
            windows[slot, :lon_tile, :] = (values[:lon_tile] * first).astype(bf16)
            windows[slot, lon_tile:ends, :] = values[lon_tile:ends].astype(bf16)
            windows[slot, ends:, :] = (values[ends:] * last).astype(bf16)

        flat = flat.astype(f32)
        total_rows = flat.shape[0]
        keep(1, flat)
        left = left_ref[...].astype(f32)
        right = right_ref[...].astype(f32)
        shifted[...] = pltpu.roll(flat, 1, 0)
        for row in range(lat_tile + 2):
            shifted[row * lon_tile : row * lon_tile + 1, :] = left[row : row + 1]
        keep(0, shifted[...])
        shifted[...] = pltpu.roll(flat, total_rows - 1, 0)
        for row in range(1, lat_tile + 3):
            shifted[row * lon_tile - 1 : row * lon_tile, :] = right[row - 1 : row]
        keep(2, shifted[...])
        for tap in range(taps):
            top = tap // 3 * lon_tile
            turned[tap] = windows[tap % 3, top : top + cells, :].T
        for copy in copies[2:-1]:
            copy.wait()
        prepare_weights(
            map_ref,
            hidden_ref,
            coef_ref,
            weight0,
            weight1,
            column_tiles,
        )
        copies[-1].wait()
        features = jnp.zeros((cells, channels), f32)
        for tap in range(taps):
            top = tap // 3 * lon_tile
            features = features + jnp.dot(
                windows[tap % 3, top : top + cells, :], conv_ref[tap], preferred_element_type=f32
            )
        feat_t[...] = features.T.astype(bf16)

        stack0[...] = jnp.zeros_like(stack0)
        if not single:
            sums[...] = jnp.zeros_like(sums)
            later_sums[...] = jnp.zeros_like(later_sums)
        out_sums[...] = jnp.zeros_like(out_sums)

    ids = lax.broadcasted_iota(jnp.int32, (cells, LANES), 0)
    strips = block // LANES
    for strip in range(strips):
        row = pl.ds(step * strips + strip, 1)
        lanes = slice(strip * LANES, (strip + 1) * LANES)
        cell = fields[0, row, :].astype(jnp.int32)
        lefts[:cells, lanes] = jnp.where(ids == cell, 1.0, 0.0).astype(bf16)
        one = jnp.ones((1, LANES), f32)
        group = jnp.concatenate(
            [
                fields[1, row, :],
                fields[4, row, :],
                fields[5, row, :],
                fields[6, row, :],
                fields[2, row, :],
                one,
                jnp.zeros((2, LANES), f32),
            ],
            axis=0,
        )
        coords = jnp.concatenate([group, group, group, jnp.zeros_like(group)], axis=0).astype(
            bf16
        )
        stack0[channels : channels + COORD_ROWS, lanes] = coords
        lefts[cells:left_rows, lanes] = coords[:EXTRA]
    across = (((1,), (1,)), ((), ()))
    spans = block // SPAN
    acts = left_rows + hidden

    def span(index):
        return slice(index * SPAN, (index + 1) * SPAN)

    def first_dots(index):
        lanes = span(index)
        queried = jnp.dot(feat_t[...], lefts[:cells, lanes], preferred_element_type=f32)
        queried = queried.astype(bf16)
        stack0[:channels, lanes] = queried
        lefts[acts:, lanes] = queried
        pre0[:, lanes] = jnp.dot(weight0[...], stack0[:, lanes], preferred_element_type=f32)

    def first_sines(index):
        for top in range(0, hidden, CHUNK):
            for left in range(index * SPAN, (index + 1) * SPAN, LANES):
                at = (slice(top, top + CHUNK), slice(left, left + LANES))
                sine, cosine = sin_cos(pre0[at])
                lefts[left_rows + top : left_rows + top + CHUNK, at[1]] = sine.astype(bf16)
                cos0[at] = cosine

    def second_dots(index):
        lanes = span(index)
        pre1[:, lanes] = jnp.dot(
            weight1[...], lefts[left_rows:, lanes], preferred_element_type=f32
        )

    def second_sines(index):
        for top in range(0, hidden, CHUNK):
            rows = slice(top, top + CHUNK)
            bias = column_tiles[rows, :LANES]
            out_weight = column_tiles[rows, LANES:]
            total = out_sums[rows, :]
            for left in range(index * SPAN, (index + 1) * SPAN, LANES):
                at = (rows, slice(left, left + LANES))
                cotan = fields[3, pl.ds(step * strips + left // LANES, 1), :]
                sine, cosine = sin_cos(pre1[at] + bias)
                total = total + sine * cotan
                rounded1[at] = (out_weight * cotan * cosine).astype(bf16)
            out_sums[rows, :] = total

    def third_dots(index):
        lanes = span(index)
        act_grad = jnp.dot(hidden_ref[...], rounded1[:, lanes], preferred_element_type=f32)
        rounded0[:, lanes] = (act_grad * cos0[:, lanes]).astype(bf16)

    def joins(lanes):
        later = lax.dot_general(
            lefts[:acts, lanes], rounded1[:, lanes], across, preferred_element_type=f32
        )
        early = lax.dot_general(
            lefts[:left_rows, lanes], rounded0[:, lanes], across, preferred_element_type=f32
        )
        if single:
            later_sums[...] = later
            sums[...] = early
        else:
            later_sums[...] += later
            sums[...] += early

    first_dots(0)
    for turn in range(spans + 2):
        if turn + 1 < spans:
            first_dots(turn + 1)
        if turn < spans:
            first_sines(turn)
            second_dots(turn)
        if 0 <= turn - 1 < spans:
            second_sines(turn - 1)
            third_dots(turn - 1)
    joins(slice(0, block))

    @pl.when(step == pl.num_programs(0) - 1)
    def _():
        cell_sums = jnp.concatenate([sums[:cells, :], later_sums[:cells, :]], axis=1)
        upper = cell_sums.astype(bf16)
        lower = (cell_sums - upper.astype(f32)).astype(bf16)
        map_grad = (
            jnp.dot(feat_t[...], upper, preferred_element_type=f32)
            + jnp.dot(feat_t[...], lower, preferred_element_type=f32)
        ) * scale
        feature_grad = (
            lax.dot_general(upper, map_ref[...], across, preferred_element_type=f32)
            + lax.dot_general(lower, map_ref[...], across, preferred_element_type=f32)
        ).astype(bf16)
        feature_grad_ref[...] = feature_grad
        hidden_grad = later_sums[left_rows:, :] * scale
        extra = sums[cells : cells + 8, :]
        later_bias = later_sums[cells + 5 : cells + 6, :]
        total = extra[5:6, :]
        lat_grad = (
            lat_cell * extra[0:1, :] + lat_sub * extra[1:2, :] + lat_offset * total
        )
        lon_grad = (
            lon_cell * extra[2:3, :] + lon_sub * extra[3:4, :] + lon_offset * total
        )
        level_grad = level_cut * extra[4:5, :] + level_offset * total
        out_grad = jnp.sum(out_sums[...].T, axis=0, keepdims=True)
        gain = OMEGA * scale
        small = jnp.concatenate(
            [
                jnp.concatenate([total, later_bias], axis=1) * scale,
                jnp.concatenate([lat_grad, lon_grad], axis=1) * gain,
                jnp.concatenate([level_grad * gain, out_grad * scale], axis=1),
                jnp.zeros((EXTRA - 3, 2 * hidden), f32),
            ],
            axis=0,
        )
        folds = hidden // LANES

        def share(part):
            lanes = slice(part * LANES, (part + 1) * LANES)
            top = part // folds * channels
            left = part % folds * LANES
            return (
                map_grad[:, lanes],
                hidden_grad[top : top + channels, left : left + LANES],
                small[:, lanes],
            )

        half = PARTS // 2
        places = (
            slice(0, channels),
            slice(channels, 2 * channels),
            slice(2 * channels, 2 * channels + EXTRA),
        )
        for part in range(half):
            for place, low, high in zip(places, share(part), share(part + half)):
                kept_ref[part, place, :] = jnp.where(bit == 0, low, high).astype(bf16)
                away_ref[part, place, :] = jnp.where(bit == 0, high, low).astype(bf16)

        rows = taps * channels // PARTS
        for tap in range(taps):
            grad = jnp.dot(turned[tap], feature_grad, preferred_element_type=f32)
            grad = (grad * scale).astype(bf16)
            start = tap * channels
            while start < (tap + 1) * channels:
                end = min((start // rows + 1) * rows, (tap + 1) * channels)
                inside = slice(start % rows, start % rows + end - start)
                value = grad[start - tap * channels : end - tap * channels]
                part = start // rows

                @pl.when(bit == part // half)
                def _():
                    conv_kept_ref[part % half, inside, :] = value

                @pl.when(bit != part // half)
                def _():
                    conv_away_ref[part % half, inside, :] = value

                start = end


def query_pass(
    serve_block,
    got,
    latents,
    rims,
    conv_weight,
    map_weight,
    hidden_weight,
    weights,
    cuts,
    scale,
):
    lat_tile, lon_tile, channels = latents.shape
    cells = lat_tile * lon_tile
    taps = conv_weight.shape[0]
    slots = got.shape[0]
    queries = slots * got.shape[2] // 4
    hidden = hidden_weight.shape[0]
    block = min(TILE, queries)
    f32, bf16 = jnp.float32, jnp.bfloat16
    hbm = pl.BlockSpec(memory_space=pltpu.HBM)
    vmem = pl.BlockSpec(memory_space=pltpu.VMEM)
    share = (PARTS // 2, 2 * channels + EXTRA, LANES)
    conv_share = (PARTS // 2, taps * channels // PARTS, channels)

    return pl.pallas_call(
        functools.partial(query_kernel, cuts, scale, taps, queries == block),
        grid=(queries // block,),
        in_specs=[hbm, vmem, hbm] + [vmem] * 4 + [hbm] * 4,
        out_specs=[vmem] * 5,
        out_shape=[
            jax.ShapeDtypeStruct(share, bf16),
            jax.ShapeDtypeStruct(share, bf16),
            jax.ShapeDtypeStruct(conv_share, bf16),
            jax.ShapeDtypeStruct(conv_share, bf16),
            jax.ShapeDtypeStruct((cells, channels), bf16),
        ],
        scratch_shapes=[
            pltpu.SMEM(serve_block.shape, jnp.int32),
            pltpu.VMEM(latents.shape, bf16),
            pltpu.VMEM(conv_weight.shape, bf16),
            pltpu.VMEM(map_weight.shape, bf16),
            pltpu.VMEM(hidden_weight.shape, bf16),
            *[pltpu.VMEM(value.shape, value.dtype) for value in weights],
            pltpu.VMEM((hidden, channels + LANES), bf16),
            pltpu.VMEM((hidden, hidden + channels), bf16),
            pltpu.VMEM((hidden, 2 * LANES), f32),
            pltpu.SemaphoreType.DMA((8,)),
            pltpu.VMEM((3, cells + 2 * lon_tile, channels), bf16),
            pltpu.VMEM((taps, channels, cells), bf16),
            pltpu.VMEM((cells + 2 * lon_tile, channels), f32),
            pltpu.VMEM((7, slots // 2, LANES), f32),
            pltpu.VMEM((channels, cells), bf16),
            pltpu.VMEM((channels + LANES, block), bf16),
            pltpu.VMEM((cells + EXTRA + hidden + channels, block), bf16),
            pltpu.VMEM((hidden, block), f32),
            pltpu.VMEM((hidden, block), f32),
            pltpu.VMEM((hidden, block), f32),
            pltpu.VMEM((hidden, block), bf16),
            pltpu.VMEM((hidden, block), bf16),
            pltpu.VMEM((cells + EXTRA, hidden), f32),
            pltpu.VMEM((cells + EXTRA + hidden, hidden), f32),
            pltpu.VMEM((hidden, LANES), f32),
        ],
        compiler_params=pltpu.CompilerParams(vmem_limit_bytes=56 * 1000 * 1000),
        name="queries",
    )(
        serve_block,
        got,
        latents,
        *rims,
        conv_weight,
        map_weight,
        hidden_weight,
        *weights,
    )


def bits_of(axis):
    return lax.axis_size(axis).bit_length() - 1


def flip(values, step):
    axis, bit = step
    count = lax.axis_size(axis)
    return lax.ppermute(values, axis, [(i, i ^ (1 << bit)) for i in range(count)])


def own_bit(step):
    axis, bit = step
    return (lax.axis_index(axis) >> bit) & 1


def added(left, right):
    return (left.astype(jnp.float32) + right.astype(jnp.float32)).astype(left.dtype)


def half_sum(kept, got, step, other):
    def pick(values):
        halves = values.reshape((2, values.shape[0] // 2) + values.shape[1:])
        mine = own_bit(step)
        place = 1 - mine if other else mine
        return lax.dynamic_index_in_dim(halves, place, 0, keepdims=False)

    return added(pick(kept), pick(got))


def ring(axis, turn):
    count = lax.axis_size(axis)
    return [(i, (i + turn) % count) for i in range(count)]


def lat_rims(first_row, last_row):
    top = lax.ppermute(last_row, "lat", ring("lat", 1))
    bottom = lax.ppermute(first_row, "lat", ring("lat", -1))
    return top, bottom


def lon_rims(first_col, last_col, top, bottom):
    last = jnp.concatenate([top[:, -1], last_col, bottom[:, -1]], axis=0)
    first = jnp.concatenate([top[:, 0], first_col, bottom[:, 0]], axis=0)
    left = lax.ppermute(last, "lon", ring("lon", 1))
    right = lax.ppermute(first, "lon", ring("lon", -1))
    return left, right


def unpack_kernel(
    mine_a,
    theirs_a,
    mine_b,
    theirs_b,
    conv_ref,
    map_ref,
    bias_ref,
    input_ref,
    hidden_ref,
    out_ref,
):
    f32 = jnp.float32
    channels = map_ref.shape[0]
    folds = hidden_ref.shape[1] // LANES
    half = PARTS // 2
    lon_pos = lax.axis_index("lon")
    bit, bit_first, bit_second = lon_pos & 1, (lon_pos >> 1) & 1, (lon_pos >> 2) & 1

    def place(part, upper_bit, lower_bit):
        upper = 1 - upper_bit if part // 2 % 2 else upper_bit
        lower = 1 - lower_bit if part % 2 else lower_bit
        return upper * 2 + lower

    def fill(low_a, high_a, low_b, high_b):
        for part in range(PARTS):
            source = (low_a if part < half else high_a).at[place(part, bit_first, bit_second)]
            lanes = slice(part * LANES, (part + 1) * LANES)
            top = part // folds * channels
            left = part % folds * LANES
            map_ref[:, lanes] = source[:channels, :].astype(f32)
            hidden_ref[top : top + channels, left : left + LANES] = source[
                channels : 2 * channels, :
            ].astype(f32)
            small = source[2 * channels :, :].astype(f32)
            bias_ref[lanes] = small[0, :]
            side = slice(left, left + LANES)
            input_ref[part // folds, side] = small[1, :]
            if part < folds:
                input_ref[2, side] = small[2, :]
            else:
                out_ref[side] = small[2, :]
            source = (low_b if part < half else high_b).at[place(part, bit_second, bit_first)]
            rows = source.shape[0]
            conv_ref[part * rows : (part + 1) * rows, :] = source[...].astype(f32)

    @pl.when(bit == 0)
    def _():
        fill(mine_a, theirs_a, mine_b, theirs_b)

    @pl.when(bit == 1)
    def _():
        fill(theirs_a, mine_a, theirs_b, mine_b)


def unpacked(pair_a, pair_b, channels, hidden, width, conv_rows):
    f32 = jnp.float32
    vmem = pl.BlockSpec(memory_space=pltpu.VMEM)
    return pl.pallas_call(
        unpack_kernel,
        in_specs=[vmem] * 4,
        out_specs=[vmem] * 6,
        out_shape=[
            jax.ShapeDtypeStruct((conv_rows, channels), f32),
            jax.ShapeDtypeStruct((channels, width), f32),
            jax.ShapeDtypeStruct((width,), f32),
            jax.ShapeDtypeStruct((3, hidden), f32),
            jax.ShapeDtypeStruct((hidden, hidden), f32),
            jax.ShapeDtypeStruct((hidden,), f32),
        ],
        compiler_params=pltpu.CompilerParams(vmem_limit_bytes=20 * 1024 * 1024),
        name="unpack",
    )(*pair_a, *pair_b)


def on_device(
    latents,
    conv_weight,
    map_weight,
    map_bias,
    input_weight,
    hidden_weight,
    output_weight,
    hit_owner,
    serve_block,
    query_grid,
    cotangent,
):
    lat_tile, lon_tile, channels = latents.shape
    lat_parts = lax.axis_size("lat")
    lon_parts = lax.axis_size("lon")
    dev_count = lat_parts * lon_parts
    lat_cells = lat_tile * lat_parts
    lon_cells = lon_tile * lon_parts
    lat_pos = lax.axis_index("lat")
    hit_count = hit_owner.shape[0]
    group_size = cotangent.shape[0] // hit_count
    width = input_weight.shape[1]
    steps = [(axis, bit) for axis in ("lon", "lat") for bit in range(bits_of(axis))]
    core, first, second = steps[:3]
    rest = steps[3:]
    cuts = (
        2.0 / lat_cells,
        2.0 / (lat_cells * SUB),
        2.0 / lon_cells,
        2.0 / (lon_cells * SUB),
        2.0 / LEVELS,
        1.0 / LEVELS - 1.0,
    )
    grad_scale = float(hit_count * group_size * dev_count) ** (-0.5)
    sent, first_row, last_row, first_col, last_col, coefs = packed(
        hit_owner,
        query_grid,
        cotangent,
        latents,
        (map_bias, input_weight, output_weight),
        cuts,
        dev_count,
        group_size,
    )
    got = lax.all_to_all(sent, ("lat", "lon"), split_axis=0, concat_axis=0, tiled=True)
    top, bottom = lat_rims(first_row, last_row)
    rims = (top, bottom, *lon_rims(first_col, last_col, top, bottom))
    kept_a, away_a, kept_b, away_b, feature_grad = query_pass(
        serve_block,
        got,
        latents,
        rims,
        conv_weight,
        map_weight,
        hidden_weight[0],
        (coefs,),
        cuts,
        grad_scale,
    )
    taps = conv_weight.shape[0]
    feature_grad = feature_grad.reshape(lat_tile, lon_tile, channels)
    hold = lax.optimization_barrier
    got_a, got_b = flip(away_a, core), flip(away_b, core)

    away_a, away_b = half_sum(kept_a, got_a, first, 1), half_sum(kept_b, got_b, second, 1)
    away_a, away_b, feature_grad = hold((away_a, away_b, feature_grad))
    kept_a, kept_b = half_sum(kept_a, got_a, first, 0), half_sum(kept_b, got_b, second, 0)
    got_a, got_b = flip(away_a, first), flip(away_b, second)
    top, bottom = lat_rims(feature_grad[:1], feature_grad[-1:])

    away_a, away_b = half_sum(kept_a, got_a, second, 1), half_sum(kept_b, got_b, first, 1)
    away_a, away_b = hold((away_a, away_b))
    kept_a, kept_b = half_sum(kept_a, got_a, second, 0), half_sum(kept_b, got_b, first, 0)
    got_a, got_b = flip(away_a, second), flip(away_b, first)

    sum_a, sum_b = added(kept_a, got_a), added(kept_b, got_b)
    for step_a, step_b in zip(rest, rest[::-1]):
        sum_a, sum_b, top, bottom = hold((sum_a, sum_b, top, bottom))
        got_a = flip(sum_a, step_a)
        got_b = flip(sum_b, step_b)
        if step_a == rest[0]:
            left, right = lon_rims(feature_grad[:, 0], feature_grad[:, -1], top, bottom)
        sum_a, sum_b = added(sum_a, got_a), added(sum_b, got_b)

    for step_a, step_b in ((second, first), (first, second)):
        sum_a, sum_b = hold((sum_a, sum_b))
        got_a = flip(sum_a, step_a)
        got_b = flip(sum_b, step_b)
        sum_a = jnp.concatenate([sum_a, got_a], axis=0)
        sum_b = jnp.concatenate([sum_b, got_b], axis=0)
    sum_a, sum_b = hold((sum_a, sum_b))
    got_a, got_b = flip(sum_a, core), flip(sum_b, core)

    padded_grad = close_poles(
        jnp.concatenate(
            [
                left[:, None],
                jnp.concatenate([top, feature_grad, bottom], axis=0),
                right[:, None],
            ],
            axis=1,
        ),
        lat_pos,
        lat_parts,
    )
    latent_grad = conv_apply(padded_grad, conv_weight, lat_tile, lon_tile, True).reshape(
        lat_tile, lon_tile, channels
    )
    totals = unpacked(
        (sum_a, got_a),
        (sum_b, got_b),
        channels,
        width,
        2 * width,
        taps * channels,
    )
    return (
        latent_grad,
        totals[0].reshape(taps, channels, channels),
        *totals[1:4],
        totals[4][None],
        totals[5],
    )


def solution(mesh):
    placed = (
        P("lat", "lon", None),
        P(),
        P(),
        P(),
        P(),
        P(),
        P(),
        P(("lat", "lon")),
        P(("lat", "lon"), None),
        P(None, ("lat", "lon")),
        P(("lat", "lon")),
    )
    return jax.shard_map(
        on_device,
        mesh=mesh,
        in_specs=placed,
        out_specs=(P("lat", "lon", None), P(), P(), P(), P(), P(), P()),
        check_vma=False,
    )
```
